32 devices in a mesh: dp: 8 (over y, x, core), tensor: 4 (over z).
Axes of the slice: x: 2, y: 2, z: 4, core: 2. Of those that a mesh axis runs over, the one named last changes fastest.
Arguments:
- inputs: bfloat16 [32768, 512], P(('dp', 'tensor')), may hold values from -6 to 6
- norm_gain: float32 [512], replicated, may hold values from 0.5 to 1.5
- in_weight: bfloat16 [512, 2, 1024], P(None, None, 'tensor'), may hold values from -0.25 to 0.25
- conv_kernel: float32 [4, 1024], P(None, 'tensor'), may hold values from -3 to 3
- gate_bias: float32 [1024], P('tensor'), may hold values from -9 to -2
- out_weight: bfloat16 [1024, 512], P('tensor'), may hold values from -0.25 to 0.25
- mlp_gain: float32 [512], replicated, may hold values from 0.5 to 1.5
- up_weight: bfloat16 [512, 2048], P(None, 'tensor'), may hold values from -0.25 to 0.25
- down_weight: bfloat16 [2048, 512], P('tensor'), may hold values from -0.1875 to 0.1875
- short_lengths: int32 [16], P('dp'), may hold values from 256 to 1024, as said below
- long_lengths: int32 [8], P('dp'), may hold values from 512 to 2048, as said below
- cotangent: bfloat16 [32768, 512], P(('dp', 'tensor')), may hold values from -6 to 6
Outputs:
- result: bfloat16 [32768, 512], P(('dp', 'tensor'))
- grad_inputs: float32 [32768, 512], P(('dp', 'tensor'))
- grad_norm_gain: float32 [512], replicated
- grad_in_weight: float32 [512, 2, 1024], P(None, None, 'tensor')
- grad_conv_kernel: float32 [4, 1024], P(None, 'tensor')
- grad_gate_bias: float32 [1024], P('tensor')
- grad_out_weight: float32 [1024, 512], P('tensor')
- grad_mlp_gain: float32 [512], replicated
- grad_up_weight: float32 [512, 2048], P(None, 'tensor')
- grad_down_weight: float32 [2048, 512], P('tensor')
The draws below stay inside these ranges and needn't reach their ends.
Inputs may be any that keep to these rules, and one draw needn't show every extreme that they name: `short_lengths`: the first short sequence of group 0 is full. `long_lengths`: the first long sequence of group 0 is full.
All inputs are finite; a program needn't handle non-finite values.
Results may differ from the reference program's by a relative error of at most 0.0075.
Values may be sent and summed in bfloat16 or wider, within the bound.
A program may use at most 192 MiB of HBM per device.

```python
import jax
import jax.numpy as jnp
from jax import lax

D = 512
H = 1024
FF = 2048
KW = 4
LSHORT = 1024
LLONG = 2048
BLOCK = 256
SHORTS = 2
LONGS = 1
GROUP = 4096
TOKENS = 32768
SHORT_ALL = 16
LONG_ALL = 8
N_DP = 8


def draw_short_lengths(key, part):
    drawn = jax.random.randint(key, (SHORT_ALL,), LSHORT // 4, LSHORT + 1, dtype=jnp.int32)
    return drawn.at[0].set(LSHORT)


def draw_long_lengths(key, part):
    drawn = jax.random.randint(jax.random.fold_in(key, 7), (LONG_ALL,), LLONG // 4, LLONG + 1, dtype=jnp.int32)
    return drawn.at[0].set(LLONG)


def draw_gate_bias(key, part):
    slow_key = jax.random.fold_in(key, 11)
    fast_key = jax.random.fold_in(key, 12)
    pick_key = jax.random.fold_in(key, 13)
    pick = jax.random.uniform(pick_key, (H,), jnp.float32)
    slow = jax.random.uniform(slow_key, (H,), jnp.float32, -9.0, -6.5)
    fast = jax.random.uniform(fast_key, (H,), jnp.float32, -5.0, -2.0)
    return jnp.where(pick < 0.55, slow, fast)


def level_of(stream_key, extent, cuts, least, high):
    def one(position, shards_of):
        draws = jax.random.uniform(jax.random.fold_in(jax.random.fold_in(stream_key, 6), position), (shards_of,), jnp.float32, least / len(cuts), high / len(cuts))
        return jnp.repeat(jnp.exp(draws), extent[position] // shards_of).reshape((-1,) + (1,) * (len(extent) - position - 1))

    loudness = one(*cuts[0])
    for cut in cuts[1:]:
        loudness = loudness * one(*cut)
    return loudness


def normal_values(rng, extent, scale, reach, cuts=(), held_as=jnp.bfloat16):
    result = scale * jax.random.normal(rng, extent, jnp.float32)
    if cuts:
        result = result * level_of(rng, extent, cuts, -0.22, 0.18)
    return jnp.clip(result, -reach, reach).astype(held_as)


def setup_inputs(seed: int = 0) -> dict:
    splits = jax.random.split(jax.random.key(seed), 13)
    inputs = normal_values(splits[0], (TOKENS, D), 1.0, 6.0, ((0, 32),))
    norm_gain = jnp.clip(1.0 + 0.1 * jax.random.normal(splits[1], (D,), jnp.float32), 0.5, 1.5)
    in_weight = normal_values(splits[2], (D, 2, H), D ** -0.5, 0.25, ((2, 4),))
    conv_kernel = normal_values(splits[3], (KW, H), 0.5, 3.0, ((1, 4),), jnp.float32)
    gate_bias = draw_gate_bias(jax.random.fold_in(splits[12], 71), 0)
    out_weight = normal_values(splits[5], (H, D), (H // 2) ** -0.5, 0.25, ((0, 4),))
    mlp_gain = jnp.clip(1.0 + 0.1 * jax.random.normal(splits[6], (D,), jnp.float32), 0.5, 1.5)
    up_weight = normal_values(splits[7], (D, FF), D ** -0.5, 0.25, ((1, 4),))
    down_weight = normal_values(splits[8], (FF, D), (FF // 2) ** -0.5, 0.1875, ((0, 4),))
    short_lengths = draw_short_lengths(jax.random.fold_in(splits[12], 71), 0)
    long_lengths = draw_long_lengths(jax.random.fold_in(splits[12], 71), 0)
    cotangent = normal_values(splits[11], (TOKENS, D), 1.0, 6.0, ((0, 32),))
    return {"inputs": inputs, "norm_gain": norm_gain, "in_weight": in_weight, "conv_kernel": conv_kernel, "gate_bias": gate_bias, "out_weight": out_weight, "mlp_gain": mlp_gain, "up_weight": up_weight, "down_weight": down_weight, "short_lengths": short_lengths, "long_lengths": long_lengths, "cotangent": cotangent}


epsilon = 1e-05

@jax.custom_vjp
def low(v):
    return lax.optimization_barrier(v.astype(jnp.bfloat16)).astype(jnp.float32)

@jax.custom_vjp
def low_back(v):
    return v

def low_keep(v):
    return (low(v), None)

def low_pass(kept, grad):
    return (grad,)

def back_keep(v):
    return (v, None)

def back_low(kept, grad):
    return (low(grad),)
low.defvjp(low_keep, low_pass)
low_back.defvjp(back_keep, back_low)

def normalize(values, gain):
    scale = lax.rsqrt(lax.optimization_barrier(jnp.mean(values * values, axis=-1, keepdims=True)) + epsilon)
    return values * scale * gain

def gelu_exact(values):
    return jax.nn.gelu(values, approximate=False)

def causal_filter(values, kernel):
    width = kernel.shape[0]
    length = values.shape[1]
    padded = jnp.pad(values, ((0, 0), (width - 1, 0), (0, 0)))
    total = values * kernel[0]
    for lag in range(1, width):
        total = total + padded[:, width - 1 - lag:width - 1 - lag + length] * kernel[lag]
    return total

def combine(early, late):
    return (early[0] * late[0], late[0] * early[1] + late[1])

def block_step(carry, pieces):
    decay, drive = pieces
    product, summed = lax.associative_scan(combine, (decay, drive), axis=1)
    states = product * carry[:, None, :] + summed
    return (states[:, -1, :], states)

def recurrence(gate, candidate, kernel):
    filtered = causal_filter(candidate, kernel)
    update = jax.nn.sigmoid(gate)
    decay = 1.0 - update
    drive = update * filtered
    sequences, length, channels = decay.shape
    count = length // BLOCK

    def blocks(values):
        return values.reshape(sequences, count, BLOCK, channels).transpose(1, 0, 2, 3)
    begin = jnp.zeros((sequences, channels), jnp.float32)
    final, states = lax.scan(jax.checkpoint(block_step), begin, (blocks(decay), blocks(drive)))
    return states.transpose(1, 0, 2, 3).reshape(sequences, length, channels)

def mixer(projected, kernel, bias):
    split = SHORTS * LSHORT
    channels = projected.shape[-1]
    shorter = projected[:split].reshape(SHORTS, LSHORT, 2, channels)
    longer = projected[split:].reshape(LONGS, LLONG, 2, channels)
    first_part = recurrence(shorter[:, :, 0] + bias, shorter[:, :, 1], kernel)
    second_part = recurrence(longer[:, :, 0] + bias, longer[:, :, 1], kernel)
    return jnp.concatenate([first_part.reshape(split, channels), second_part.reshape(LONGS * LLONG, channels)], axis=0)

def row_keep(short_lengths, long_lengths):
    short_place = jnp.arange(LSHORT, dtype=jnp.int32)
    long_place = jnp.arange(LLONG, dtype=jnp.int32)
    short_keep = (short_place[None, :] < short_lengths[:, None]).reshape(-1)
    long_keep = (long_place[None, :] < long_lengths[:, None]).reshape(-1)
    return jnp.concatenate([short_keep, long_keep]).astype(jnp.float32)

def forward(rows, norm_gain, in_weight, conv_kernel, gate_bias, out_weight, mlp_gain, up_weight, down_weight):
    precise = lax.Precision.HIGHEST
    first = low(normalize(rows, norm_gain))
    projected = low_back(jnp.einsum('rd,dch->rch', first, in_weight, precision=precise))
    hidden = low(mixer(projected, conv_kernel, gate_bias))
    mixed = low_back(jnp.dot(hidden, out_weight, precision=precise))
    middle = rows + mixed
    second = low(normalize(middle, mlp_gain))
    inner = low_back(jnp.dot(second, up_weight, precision=precise))
    activ = low(gelu_exact(inner))
    branch = low_back(jnp.dot(activ, down_weight, precision=precise))
    return middle + branch

def reference(inputs, norm_gain, in_weight, conv_kernel, gate_bias, out_weight, mlp_gain, up_weight, down_weight, short_lengths, long_lengths, cotangent):
    weights = (norm_gain, in_weight.astype(jnp.float32), conv_kernel, gate_bias, out_weight.astype(jnp.float32), mlp_gain, up_weight.astype(jnp.float32), down_weight.astype(jnp.float32))
    groups = N_DP
    row_groups = inputs.reshape(groups, GROUP, D)
    cot_groups = cotangent.reshape(groups, GROUP, D)
    short_groups = short_lengths.reshape(groups, SHORTS)
    long_groups = long_lengths.reshape(groups, LONGS)

    def step(totals, items):
        rows, cot_rows, short_part, long_part = items
        keep = row_keep(short_part, long_part)
        output, pull = jax.vjp(forward, rows.astype(jnp.float32), *weights)
        grads = pull(cot_rows.astype(jnp.float32) * keep[:, None])
        updated = tuple((total + grad for total, grad in zip(totals, grads[1:])))
        return (updated, (output.astype(jnp.bfloat16), grads[0]))
    zeros_start = tuple((jnp.zeros_like(weight) for weight in weights))
    totals, (outputs, grad_rows) = lax.scan(step, zeros_start, (row_groups, cot_groups, short_groups, long_groups))
    return (outputs.reshape(TOKENS, D), grad_rows.reshape(TOKENS, D), totals[0], totals[1], totals[2], totals[3], totals[4], totals[5], totals[6], totals[7])
```

```python
import functools

import jax
import jax.numpy as jnp
import numpy as np
from jax import lax
from jax.experimental import pallas as pl
from jax.experimental.pallas import tpu as pltpu
from jax.sharding import PartitionSpec as P

LSHORT = 1024
LLONG = 2048
SEGS = 8
EPS = 1e-05
CHUNK = 256
F32 = jnp.float32
BF16 = jnp.bfloat16
MESH = pl.DeviceIdType.MESH


def dot(a, b):
    return jnp.dot(a, b, preferred_element_type=F32)


def dot_t(a, b):
    return lax.dot_general(a, b, (((1,), (1,)), ((), ())), preferred_element_type=F32)


def scale_of(v):
    return lax.rsqrt(jnp.mean(v * v, axis=-1, keepdims=True) + EPS)


def sigmoid(v):
    return 1.0 / (1.0 + jnp.exp(-v))


def block_kernel(
    dims,
    lim_ref,
    x_ref,
    halo_ref,
    cot_ref,
    g1_ref,
    g2_ref,
    w_ref,
    conv_ref,
    bias_ref,
    res_ref,
    gx_ref,
    grad_ref,
    gains_ref,
    chan_ref,
    cand,
    upd,
    filt,
    st,
    dst,
    lhs,
    first_t,
    second_t,
    dout,
    dout_t,
    dmix_t,
    bufa,
    mid,
    bufc,
    act,
    din,
    ends,
    bends,
    fsend,
    frecv,
    bsend,
    brecv,
    sems,
):
    rows, d, blocks, ch, ff = dims
    steps = rows // SEGS
    t = lax.axis_index("tensor")
    even = lax.rem(t, 2) == 0
    partner = t + 1 - 2 * lax.rem(t, 2)
    nchunk = rows // CHUNK
    o_in, o_out, o_up, o_down = 0, d, d + ch, d + ch + ff

    barrier = pltpu.get_barrier_semaphore()
    pl.semaphore_signal(barrier, inc=1, device_id={"tensor": partner}, device_id_type=MESH)
    pl.semaphore_wait(barrier, 1)

    def norm_rows(r, _):
        at = pl.multiple_of(r * CHUNK, CHUNK)
        xv = x_ref[pl.ds(at, CHUNK), :].astype(F32)
        fv = xv * scale_of(xv) * g1_ref[...]
        lhs[pl.ds(at, CHUNK), :] = fv.astype(BF16)
        first_t[:, pl.ds(at, CHUNK)] = fv.T.astype(BF16)
        place = at + lax.broadcasted_iota(jnp.int32, (CHUNK, d), 0)
        pos = lax.rem(place, SEGS) * steps + place // SEGS
        dv = jnp.where(pos < lim_ref[0], cot_ref[pl.ds(at, CHUNK), :].astype(F32), 0.0)
        dout[pl.ds(at, CHUNK), :] = dv.astype(BF16)
        dout_t[:, pl.ds(at, CHUNK)] = dv.T.astype(BF16)
        return 0

    lax.fori_loop(0, nchunk, norm_rows, 0)
    hv = halo_ref[...].astype(F32)
    lhs[pl.ds(rows, 16), :] = (hv * scale_of(hv) * g1_ref[...]).astype(BF16)

    seg_id = lax.broadcasted_iota(jnp.int32, (SEGS, ch), 0)
    has_prev = jnp.where(t == 3, 1.0, 0.0).astype(F32)
    has_next = jnp.where(t == 2, 1.0, 0.0).astype(F32)

    def forward_block(b, _):
        def project(r, _):
            at = pl.multiple_of(r * CHUNK, CHUNK)
            p = dot(lhs[pl.ds(at, CHUNK), :], w_ref[b, pl.ds(o_in, d), :])
            bufa[pl.ds(at, CHUNK), :ch] = p[:, :ch]
            cand[b, pl.ds(at + 3 * SEGS, CHUNK), :] = p[:, ch:]
            return 0

        lax.fori_loop(0, nchunk, project, 0)
        ph = dot(lhs[pl.ds(rows, 16), :], w_ref[b, pl.ds(o_in, d), ch:])
        for back in range(3):
            last = cand[b, pl.ds((steps + back) * SEGS, SEGS), :]
            rolled = pltpu.roll(last, 1, 0)
            edge = ph[13 + back : 14 + back, :] * has_prev
            cand[b, pl.ds(back * SEGS, SEGS), :] = jnp.where(seg_id == 0, edge, rolled)
        k = [jnp.broadcast_to(conv_ref[b, pl.ds(i, 1), :], (SEGS, ch)) for i in range(4)]
        bias = jnp.broadcast_to(bias_ref[b], (SEGS, ch))

        def step4(j, carry):
            s, p = carry
            for q in range(4):
                at = pl.multiple_of((j * 4 + q) * SEGS, SEGS)
                u = sigmoid(bufa[pl.ds(at, SEGS), :ch] + bias)
                f = k[0] * cand[b, pl.ds(at + 3 * SEGS, SEGS), :]
                for lag in range(1, 4):
                    f = f + k[lag] * cand[b, pl.ds(at + (3 - lag) * SEGS, SEGS), :]
                upd[b, pl.ds(at, SEGS), :] = u
                filt[b, pl.ds(at, SEGS), :] = f
                a = 1.0 - u
                s = a * s + u * f
                p = a * p
            return s, p

        s, p = lax.fori_loop(
            0, steps // 4, step4, (jnp.zeros((SEGS, ch), F32), jnp.ones((SEGS, ch), F32))
        )
        ends[0, b] = s
        ends[1, b] = p
        return 0

    lax.fori_loop(0, blocks, forward_block, 0)

    def forward_chain(start):
        run = start
        for seg in range(SEGS):
            st[:, pl.ds(seg, 1), :] = run
            run = ends[0, :, pl.ds(seg, 1), :] + ends[1, :, pl.ds(seg, 1), :] * run
        return run

    final = forward_chain(jnp.zeros((blocks, 1, ch), F32))
    fsend[...] = jnp.broadcast_to(final, (blocks, 8, ch))
    fcopy = pltpu.make_async_remote_copy(
        src_ref=fsend,
        dst_ref=frecv,
        send_sem=sems.at[0],
        recv_sem=sems.at[1],
        device_id={"tensor": partner},
        device_id_type=MESH,
    )

    fcopy.start()
    fcopy.wait()
    forward_chain(frecv[:, pl.ds(0, 1), :] * has_prev)

    def forward_fix(b, _):
        def step8(j, s):
            for q in range(8):
                at = pl.multiple_of((j * 8 + q) * SEGS, SEGS)
                u = upd[b, pl.ds(at, SEGS), :]
                s = (1.0 - u) * s + u * filt[b, pl.ds(at, SEGS), :]
                st[b, pl.ds(at + SEGS, SEGS), :] = s
            return s

        lax.fori_loop(0, steps // 8, step8, st[b, pl.ds(0, SEGS), :])
        return 0

    lax.fori_loop(0, blocks, forward_fix, 0)

    def second_rows(r, _):
        at = pl.multiple_of(r * CHUNK, CHUNK)
        m = x_ref[pl.ds(at, CHUNK), :].astype(F32)
        for b in range(blocks):
            m = m + dot(st[b, pl.ds(at + SEGS, CHUNK), :].astype(BF16), w_ref[b, pl.ds(o_out, ch), :])
        mid[pl.ds(at, CHUNK), :] = m
        sv = m * scale_of(m) * g2_ref[...]
        lhs[pl.ds(at, CHUNK), :] = sv.astype(BF16)
        second_t[:, pl.ds(at, CHUNK)] = sv.T.astype(BF16)
        bufa[pl.ds(at, CHUNK), :] = m
        bufc[pl.ds(at, CHUNK), :] = jnp.zeros((CHUNK, d), F32)
        return 0

    lax.fori_loop(0, nchunk, second_rows, 0)

    def ff_block(b, _):
        def ff_rows(r, _):
            at = pl.multiple_of(r * CHUNK, CHUNK)
            wu = w_ref[b, pl.ds(o_up, ff), :]
            wd = w_ref[b, pl.ds(o_down, ff), :]
            inner = dot(lhs[pl.ds(at, CHUNK), :], wu)
            da = dot_t(dout[pl.ds(at, CHUNK), :], wd)
            cdf = 0.5 + 0.5 * lax.erf(inner * np.float32(np.sqrt(0.5)))
            pdf = jnp.exp(inner * inner * -0.5) * np.float32(1.0 / np.sqrt(2.0 * np.pi))
            av = (inner * cdf).astype(BF16)
            dv = (da * (cdf + inner * pdf)).astype(BF16)
            act[pl.ds(at, CHUNK), :] = av
            din[pl.ds(at, CHUNK), :] = dv
            bufa[pl.ds(at, CHUNK), :] += dot(av, wd)
            bufc[pl.ds(at, CHUNK), :] += dot_t(dv, wu)
            return 0

        lax.fori_loop(0, nchunk, ff_rows, 0)

        def ff_grads(r, _):
            at = pl.multiple_of(r * CHUNK, CHUNK)
            grad_ref[b, pl.ds(o_up + at, CHUNK), :] = dot(second_t[pl.ds(at, CHUNK), :], din[...]).astype(BF16)
            grad_ref[b, pl.ds(o_down + at, CHUNK), :] = dot(dout_t[pl.ds(at, CHUNK), :], act[...]).astype(BF16)
            return 0

        lax.fori_loop(0, d // CHUNK, ff_grads, 0)
        return 0

    lax.fori_loop(0, blocks, ff_block, 0)

    def second_back(r, gain):
        at = pl.multiple_of(r * CHUNK, CHUNK)
        res_ref[pl.ds(at, CHUNK), :] = bufa[pl.ds(at, CHUNK), :].astype(BF16)
        m = mid[pl.ds(at, CHUNK), :]
        s = scale_of(m)
        dn = bufc[pl.ds(at, CHUNK), :]
        gain = gain + jnp.sum(dn * m * s, axis=0, keepdims=True)
        gd = dn * g2_ref[...]
        dm = dout[pl.ds(at, CHUNK), :].astype(F32) + s * gd - m * (s * s * s * jnp.mean(gd * m, axis=-1, keepdims=True))
        gx_ref[pl.ds(at, CHUNK), :] = dm
        lhs[pl.ds(at, CHUNK), :] = dm.astype(BF16)
        dmix_t[:, pl.ds(at, CHUNK)] = dm.T.astype(BF16)
        bufc[pl.ds(at, CHUNK), :] = jnp.zeros((CHUNK, d), F32)
        return gain

    gains_ref[pl.ds(1, 1), :] = lax.fori_loop(0, nchunk, second_back, jnp.zeros((1, d), F32))

    def backward_block(b, _):
        def project(r, _):
            at = pl.multiple_of(r * CHUNK, CHUNK)
            dst[b, pl.ds(at, CHUNK), :] = dot_t(lhs[pl.ds(at, CHUNK), :], w_ref[b, pl.ds(o_out, ch), :])
            return 0

        lax.fori_loop(0, nchunk, project, 0)
        for half in range(2):
            rr = d // 2
            grad_ref[b, pl.ds(o_out, ch), half * ch : (half + 1) * ch] = dot(
                dmix_t[half * rr : (half + 1) * rr, :], st[b, pl.ds(SEGS, rows), :].astype(BF16)
            ).astype(BF16)

        def one(step, w, p):
            at = pl.multiple_of(step * SEGS, SEGS)
            a = 1.0 - upd[b, pl.ds(at, SEGS), :]
            c = dst[b, pl.ds(at, SEGS), :] + w
            return c, a * c, p * a

        w, p = jnp.zeros((SEGS, ch), F32), jnp.ones((SEGS, ch), F32)
        for step in range(steps - 1, steps - 6, -1):
            _, w, p = one(step, w, p)

        def step8(j, carry):
            w, p = carry
            for q in range(8):
                _, w, p = one(steps - 6 - (j * 8 + q), w, p)
            return w, p

        left = (steps - 8) // 8
        w, p = lax.fori_loop(0, left, step8, (w, p))
        for step in range(2, -1, -1):
            bends[2 * step, b] = p
            c, w, p = one(step, w, p)
            bends[2 * step + 1, b] = c
        bends[6, b] = w
        bends[7, b] = p
        return 0

    lax.fori_loop(0, blocks, backward_block, 0)

    def backward_chain(start):
        run = start
        for seg in range(SEGS - 1, -1, -1):
            ends[0, :, pl.ds(seg, 1), :] = run
            run = bends[6, :, pl.ds(seg, 1), :] + bends[7, :, pl.ds(seg, 1), :] * run
        return run

    bsend[:, pl.ds(0, 1), :] = backward_chain(jnp.zeros((blocks, 1, ch), F32))
    for step in range(3):
        bsend[:, pl.ds(step + 1, 1), :] = upd[:, pl.ds(step * SEGS, 1), :] * (
            bends[2 * step + 1, :, pl.ds(0, 1), :]
            + bends[2 * step, :, pl.ds(0, 1), :] * ends[0, :, pl.ds(0, 1), :]
        )
    bcopy = pltpu.make_async_remote_copy(
        src_ref=bsend,
        dst_ref=brecv,
        send_sem=sems.at[2],
        recv_sem=sems.at[3],
        device_id={"tensor": partner},
        device_id_type=MESH,
    )
    bcopy.start()
    bcopy.wait()
    backward_chain(brecv[:, pl.ds(0, 1), :] * has_next)

    def backward_fix(b, _):
        w = ends[0, b]
        after = []
        for step in range(3):
            df = upd[b, pl.ds(step * SEGS, SEGS), :] * (bends[2 * step + 1, b] + bends[2 * step, b] * w)
            edge = brecv[b, pl.ds(step + 1, 1), :] * has_next
            after.append(jnp.where(seg_id == SEGS - 1, edge, pltpu.roll(df, SEGS - 1, 0)))
        k = [jnp.broadcast_to(conv_ref[b, pl.ds(i, 1), :], (SEGS, ch)) for i in range(4)]
        zero = jnp.zeros((SEGS, ch), F32)

        def pair(j, carry):
            w, d1, d2, d3, c0, c1, c2, k0, k1, k2, k3, gb = carry
            top = steps - 2 - 2 * j
            made = []
            for q in range(2):
                step = top + 1 - q
                at = pl.multiple_of(step * SEGS, SEGS)
                u = upd[b, pl.ds(at, SEGS), :]
                c = dst[b, pl.ds(at, SEGS), :] + w
                d0 = c * u
                a = 1.0 - u
                w = a * c
                dg = d0 * a * (filt[b, pl.ds(at, SEGS), :] - st[b, pl.ds(at, SEGS), :])
                dc = k[0] * d0 + k[1] * d1 + k[2] * d2 + k[3] * d3
                c3 = cand[b, pl.ds(at, SEGS), :]
                k0, k1, k2, k3 = k0 + d0 * c0, k1 + d0 * c1, k2 + d0 * c2, k3 + d0 * c3
                gb = gb + dg
                c0, c1, c2 = c1, c2, c3
                d1, d2, d3 = d0, d1, d2
                made.append((dg, dc))
            at = pl.multiple_of(top * SEGS, 2 * SEGS)
            act[pl.ds(at, 2 * SEGS), :ch] = jnp.concatenate([made[1][0], made[0][0]], axis=0).astype(BF16)
            act[pl.ds(at, 2 * SEGS), ch:] = jnp.concatenate([made[1][1], made[0][1]], axis=0).astype(BF16)
            return w, d1, d2, d3, c0, c1, c2, k0, k1, k2, k3, gb

        window = [cand[b, pl.ds((steps + 2 - i) * SEGS, SEGS), :] for i in range(3)]
        out = lax.fori_loop(0, steps // 2, pair, (w, *after, *window, zero, zero, zero, zero, zero))
        for i in range(5):
            chan_ref[b, pl.ds(i, 1), :] = jnp.sum(out[7 + i], axis=0, keepdims=True)

        def first_grad(r, _):
            at = pl.multiple_of(r * CHUNK, CHUNK)
            grad_ref[b, pl.ds(o_in + at, CHUNK), :] = dot(first_t[pl.ds(at, CHUNK), :], act[...]).astype(BF16)
            return 0

        lax.fori_loop(0, d // CHUNK, first_grad, 0)

        def first_back(r, _):
            at = pl.multiple_of(r * CHUNK, CHUNK)
            bufc[pl.ds(at, CHUNK), :] += dot_t(act[pl.ds(at, CHUNK), :], w_ref[b, pl.ds(o_in, d), :])
            return 0

        lax.fori_loop(0, nchunk, first_back, 0)
        return 0

    chan_ref[...] = jnp.zeros_like(chan_ref)
    lax.fori_loop(0, blocks, backward_fix, 0)

    def first_norm_back(r, gain):
        at = pl.multiple_of(r * CHUNK, CHUNK)
        m = x_ref[pl.ds(at, CHUNK), :].astype(F32)
        s = scale_of(m)
        dn = bufc[pl.ds(at, CHUNK), :]
        gain = gain + jnp.sum(dn * m * s, axis=0, keepdims=True)
        gd = dn * g1_ref[...]
        gx_ref[pl.ds(at, CHUNK), :] += s * gd - m * (s * s * s * jnp.mean(gd * m, axis=-1, keepdims=True))
        return gain

    gains_ref[pl.ds(0, 1), :] = lax.fori_loop(0, nchunk, first_norm_back, jnp.zeros((1, d), F32))


def permute(v):
    rows, d = v.shape
    return v.reshape(SEGS, rows // SEGS, d).transpose(1, 0, 2).reshape(rows, d)


def unpermute(v):
    rows, d = v.shape
    return v.reshape(rows // SEGS, SEGS, d).transpose(1, 0, 2).reshape(rows, d)


def per_device(
    inputs,
    norm_gain,
    in_weight,
    conv_kernel,
    gate_bias,
    out_weight,
    mlp_gain,
    up_weight,
    down_weight,
    short_lengths,
    long_lengths,
    cotangent,
):
    rows, d = inputs.shape
    ch = in_weight.shape[2]
    ff = up_weight.shape[1]
    blocks = lax.axis_size("tensor")
    dp = lax.axis_size("dp")
    assert blocks == 4 and rows == LSHORT and 2 * rows == LLONG
    assert short_lengths.shape == (2,) and long_lengths.shape == (1,)
    t = lax.axis_index("tensor")
    shard = jnp.concatenate([in_weight.reshape(d, 2 * ch), out_weight, up_weight, down_weight], axis=0)
    total = shard.shape[0]
    mine = lax.dynamic_slice_in_dim(shard, lax.axis_index("dp") * (total // dp), total // dp, 0)
    w_all = lax.all_gather(mine, ("tensor", "dp"), axis=0, tiled=True).reshape(blocks, total, d)
    small = jnp.concatenate([conv_kernel, gate_bias[None]], axis=0)
    small_all = lax.all_gather(small, "tensor", axis=0)
    conv_all = small_all[:, :4]
    bias_all = small_all[:, 4:5]
    halo = lax.ppermute(inputs[-16:], "tensor", [(i, i + 1) for i in range(blocks - 1)])
    lengths = jnp.concatenate([short_lengths, long_lengths, long_lengths - rows])
    limit = lax.dynamic_slice_in_dim(lengths, t, 1, 0)
    vm = pl.BlockSpec(memory_space=pltpu.VMEM)
    dims = (rows, d, blocks, ch, ff)
    res, gx, grads, gains, chan = pl.pallas_call(
        functools.partial(block_kernel, dims),
        out_shape=(
            jax.ShapeDtypeStruct((rows, d), BF16),
            jax.ShapeDtypeStruct((rows, d), F32),
            jax.ShapeDtypeStruct((blocks, total, d), BF16),
            jax.ShapeDtypeStruct((2, d), F32),
            jax.ShapeDtypeStruct((blocks, 8, ch), F32),
        ),
        in_specs=[pl.BlockSpec(memory_space=pltpu.SMEM)] + [vm] * 8,
        out_specs=(vm,) * 5,
        scratch_shapes=[
            pltpu.VMEM((blocks, rows + 3 * SEGS, ch), F32),
            pltpu.VMEM((blocks, rows, ch), F32),
            pltpu.VMEM((blocks, rows, ch), F32),
            pltpu.VMEM((blocks, rows + SEGS, ch), F32),
            pltpu.VMEM((blocks, rows, ch), F32),
            pltpu.VMEM((rows + 16, d), BF16),
            pltpu.VMEM((d, rows), BF16),
            pltpu.VMEM((d, rows), BF16),
            pltpu.VMEM((rows, d), BF16),
            pltpu.VMEM((d, rows), BF16),
            pltpu.VMEM((d, rows), BF16),
            pltpu.VMEM((rows, d), F32),
            pltpu.VMEM((rows, d), F32),
            pltpu.VMEM((rows, d), F32),
            pltpu.VMEM((rows, ff), BF16),
            pltpu.VMEM((rows, ff), BF16),
            pltpu.VMEM((2, blocks, SEGS, ch), F32),
            pltpu.VMEM((8, blocks, SEGS, ch), F32),
            pltpu.VMEM((blocks, 8, ch), F32),
            pltpu.VMEM((blocks, 8, ch), F32),
            pltpu.VMEM((blocks, 8, ch), F32),
            pltpu.VMEM((blocks, 8, ch), F32),
            pltpu.SemaphoreType.DMA((4,)),
        ],
        compiler_params=pltpu.CompilerParams(
            collective_id=0, has_side_effects=True, vmem_limit_bytes=67043328
        ),
        name="block",
    )(limit, permute(inputs), halo, permute(cotangent), norm_gain[None], mlp_gain[None], w_all, conv_all, bias_all)
    result = unpermute(res)
    grad_inputs = unpermute(gx)
    part = lax.psum_scatter(grads, "dp", scatter_dimension=1, tiled=True)
    part = lax.psum_scatter(part, "tensor", scatter_dimension=0, tiled=True)
    own = lax.all_gather(part[0], "dp", axis=0, tiled=True).astype(F32)
    grad_in = own[:d].reshape(d, 2, ch)
    packed = own[d : d + ch]
    grad_out = jnp.concatenate([packed[:, :ch], packed[:, ch:]], axis=0).T
    grad_up = own[d + ch : d + ch + ff]
    grad_down = own[d + ch + ff :].T
    gains, chan = lax.psum((gains, chan), ("dp", "tensor"))
    chan = lax.dynamic_slice_in_dim(chan, t, 1, 0)[0]
    return (
        result,
        grad_inputs,
        gains[0],
        grad_in,
        chan[:4],
        chan[4],
        grad_out,
        gains[1],
        grad_up,
        grad_down,
    )


def solution(mesh):
    placed = (
        P(("dp", "tensor"), None),
        P(),
        P(None, None, "tensor"),
        P(None, "tensor"),
        P("tensor"),
        P("tensor", None),
        P(),
        P(None, "tensor"),
        P("tensor", None),
        P("dp"),
        P("dp"),
        P(("dp", "tensor"), None),
    )
    return jax.shard_map(
        per_device,
        mesh=mesh,
        in_specs=placed,
        out_specs=(
            P(("dp", "tensor"), None),
            P(("dp", "tensor"), None),
            P(),
            P(None, None, "tensor"),
            P(None, "tensor"),
            P("tensor"),
            P("tensor", None),
            P(),
            P(None, "tensor"),
            P("tensor", None),
        ),
        check_vma=False,
    )
```

```python
import functools

import jax
import jax.numpy as jnp
import numpy as np
from jax import lax
from jax.experimental import pallas as pl
from jax.experimental.pallas import tpu as pltpu
from jax.sharding import PartitionSpec as P

LSHORT = 1024
LLONG = 2048
SEGS = 8
EPS = 1e-05
CHUNK = 256
TILE = 16
LANES = 128
F32 = jnp.float32
BF16 = jnp.bfloat16
MESH = pl.DeviceIdType.MESH
IN, OUT, FF = 0, 1, 2


def dot(a, b):
    return jnp.dot(a, b, preferred_element_type=F32)


def dot_t(a, b):
    return lax.dot_general(a, b, (((1,), (1,)), ((), ())), preferred_element_type=F32)


def scale_of(v):
    return lax.rsqrt(jnp.mean(v * v, axis=-1, keepdims=True) + EPS)


def sigmoid(v):
    return 1.0 / (1.0 + jnp.exp(-v))


def bit_of(v, bit):
    return lax.rem(lax.div(v, 1 << bit), 2)


def flip(v, bit):
    return v + (1 << bit) * (1 - 2 * bit_of(v, bit))


def log2(n):
    return int(n).bit_length() - 1


def block_kernel(
    dims,
    short_ref,
    long_ref,
    x_hbm,
    cot_hbm,
    g1_ref,
    g2_ref,
    conv_ref,
    bias_ref,
    win_hbm,
    wout_hbm,
    wup_hbm,
    wdown_hbm,
    res_hbm,
    gx_hbm,
    gin_ref,
    gout_ref,
    gup_ref,
    gdown_ref,
    gains_ref,
    chan_ref,
    w_all,
    grad,
    fin,
    xp,
    cand,
    upd,
    st,
    dst,
    lhs,
    first_t,
    second_t,
    dout,
    dout_t,
    bufa,
    mid,
    bufc,
    dproj,
    perm,
    halo,
    cb,
    ends,
    bends,
    fsend,
    frecv,
    bsend,
    brecv,
    zbuf,
    gsum,
    grecv,
    csum,
    crecv,
    lsem,
    csem,
    zsem,
    w_s,
    w_r,
    r_s,
    r_r,
    a_s,
    a_r,
    s_s,
    s_r,
    *stage_bufs,
):
    rows, d, blocks, ch, ff, nb = dims
    steps = rows // SEGS
    t = lax.axis_index("tensor")
    p = lax.axis_index("dp")
    partner = flip(t, 0)
    nchunk = rows // CHUNK
    offs = (0, d, d + ch)
    sizes = (d, ch, 2 * ff)
    o_in, o_out, o_up, o_down = 0, d, d + ch, d + ch + ff
    halves = tuple(min(nb, log2(r // TILE)) for r in sizes)
    half_d = d // 2
    lanes = (pl.ds(0, half_d), pl.ds(half_d, half_d))
    orders = ((0,) + tuple(range(nb - 1, 0, -1)), tuple(range(nb)))
    nstage = len(stage_bufs)

    def zflip(j):
        b0, b1 = lax.rem(j, 2), lax.div(j, 2)
        return t + b0 * (1 - 2 * bit_of(t, 0)) + b1 * (2 - 4 * bit_of(t, 1))

    def low_of(kind, c, k):
        low = 0
        for i in range(min(k, halves[kind])):
            low = low + bit_of(p, orders[c][i]) * (sizes[kind] >> (i + 1))
        return low

    def span(kind, k):
        return sizes[kind] >> min(k, halves[kind])

    def at_rows(kind, start, n):
        return pl.ds(pl.multiple_of(offs[kind] + start, TILE), n)

    def stage_rows(kind, k):
        base = sum(span(i, k + 1) for i in range(kind))
        return pl.ds(base, span(kind, k + 1))

    def remote(src, dst_, ss, rs, **dev):
        return pltpu.make_async_remote_copy(
            src_ref=src, dst_ref=dst_, send_sem=ss, recv_sem=rs, device_id=dev, device_id_type=MESH
        )

    def w_z(kind, j, c, shard, target):
        at = at_rows(kind, low_of(kind, c, nb), span(kind, nb))
        ref = w_all.at[shard, at, lanes[c]]
        return remote(ref, ref, w_s.at[kind, j, nb, c], w_r.at[kind, j, nb, c], tensor=target)

    def w_step(kind, j, k):
        s = zflip(j)
        if k == 0:
            at = at_rows(kind, low_of(kind, 0, 1), span(kind, 1))
            ref = w_all.at[s, at, :]
            return [remote(ref, ref, w_s.at[kind, j, 0, 0], w_r.at[kind, j, 0, 0], dp=flip(p, 0))]
        made = []
        for c in range(2):
            at = at_rows(kind, low_of(kind, c, k + 1), span(kind, k + 1))
            ref = w_all.at[s, at, lanes[c]]
            made.append(remote(ref, ref, w_s.at[kind, j, k, c], w_r.at[kind, j, k, c], dp=flip(p, orders[c][k])))
        return made

    def w_sources(kind, j):
        return [w_z(kind, j, c, t, zflip(j)) for c in range(2)]

    def w_wait(kind, j, k):
        if k == halves[kind]:
            copies = [w_z(kind, j, c, zflip(j), zflip(j)) for c in range(2)]
        else:
            copies = w_step(kind, j, k)
        for copy in copies:
            copy.wait_recv()

    def w_forward(kind, j, k):
        w_wait(kind, j, k + 1)
        for copy in w_step(kind, j, k):
            copy.start()

    def w_all_j(kind, k):
        def go(j, _):
            w_forward(kind, j, k)
            return 0

        lax.fori_loop(1, blocks, go, 0)

    def r_step(kind, j, k):
        s = zflip(j)
        buf = stage_bufs[k]
        base = sum(span(i, k + 1) for i in range(kind))
        made = []
        for c in range(2):
            if k < halves[kind]:
                low = low_of(kind, c, k) + (1 - bit_of(p, orders[c][k])) * span(kind, k + 1)
            else:
                low = low_of(kind, c, k)
            which = slice(None) if k == 0 else lanes[c]
            made.append(
                remote(
                    grad.at[s, at_rows(kind, low, span(kind, k + 1)), which],
                    buf.at[j, pl.ds(base, span(kind, k + 1)), which],
                    r_s.at[kind, j, k, c],
                    r_r.at[kind, j, k, c],
                    dp=flip(p, orders[c][k]),
                )
            )
            if k == 0:
                break
        return made

    def r_start(kind, j, k):
        for copy in r_step(kind, j, k):
            copy.start()

    def r_finish(kind, j, k):
        s = zflip(j)
        buf = stage_bufs[k]
        base = sum(span(i, k + 1) for i in range(kind))
        n = span(kind, k + 1)
        for copy in r_step(kind, j, k):
            if k >= halves[kind]:
                copy.wait_send()
            copy.wait_recv()
        piece = min(n, 128)
        for c in range(2):
            low = low_of(kind, c, k + 1)

            def add(i, _):
                at = at_rows(kind, low + i * piece, piece)
                here = pl.ds(pl.multiple_of(base + i * piece, TILE), piece)
                grad[s, at, lanes[c]] = (
                    grad[s, at, lanes[c]].astype(F32) + buf[j, here, lanes[c]].astype(F32)
                ).astype(BF16)
                return 0

            lax.fori_loop(0, n // piece, add, 0)

    def r_z(kind, j):
        s = zflip(j)
        base = sum(span(i, nb) for i in range(kind))
        made = []
        for c in range(2):
            at = at_rows(kind, low_of(kind, c, nb), span(kind, nb))
            made.append(
                remote(
                    grad.at[s, at, lanes[c]],
                    zbuf.at[j, pl.ds(base, span(kind, nb)), lanes[c]],
                    r_s.at[kind, j, nb, c],
                    r_r.at[kind, j, nb, c],
                    tensor=s,
                )
            )
        return made

    def r_out(kind, j):
        for copy in r_z(kind, j):
            copy.start()

    def r_total(kind):
        base = sum(span(i, nb) for i in range(kind))
        n = span(kind, nb)
        for j in range(1, blocks):
            for copy in r_z(kind, j):
                copy.wait_recv()
        for c in range(2):
            at = at_rows(kind, low_of(kind, c, nb), n)
            total = grad[t, at, lanes[c]].astype(F32)
            for j in range(1, blocks):
                total = total + zbuf[j, pl.ds(base, n), lanes[c]].astype(F32)
            fin[at, lanes[c]] = total.astype(BF16)

    def a_step(kind, k):
        if k == 0:
            ref = fin.at[at_rows(kind, low_of(kind, 0, 1), span(kind, 1)), :]
            return [remote(ref, ref, a_s.at[kind, 0, 0], a_r.at[kind, 0, 0], dp=flip(p, 0))]
        made = []
        for c in range(2):
            ref = fin.at[at_rows(kind, low_of(kind, c, k + 1), span(kind, k + 1)), lanes[c]]
            made.append(remote(ref, ref, a_s.at[kind, k, c], a_r.at[kind, k, c], dp=flip(p, orders[c][k])))
        return made

    def a_start(kind, k):
        for copy in a_step(kind, k):
            copy.start()

    def a_wait(kind, k):
        for copy in a_step(kind, k):
            copy.wait_recv()

    def r_middle(kind, j):
        for k in range(1, nb - 1):
            r_finish(kind, j, k)
            r_start(kind, j, k + 1)

    def r_first(kind, j):
        r_finish(kind, j, 0)
        r_start(kind, j, 1)

    def r_last(kind, j, shard_known=None):
        r_finish(kind, j, nb - 1)
        if shard_known is None:
            @pl.when(j > 0)
            def _():
                r_out(kind, j)
        elif shard_known > 0:
            r_out(kind, j)

    def s_step(which, k):
        total, got = ((gsum, grecv), (csum, crecv))[which]
        dev = {"dp": flip(p, k)} if k < nb else {"tensor": flip(t, k - nb)}
        return remote(total.at[k], got.at[k], s_s.at[which, k], s_r.at[which, k], **dev)

    def s_next(which, k):
        total, got = ((gsum, grecv), (csum, crecv))[which]
        s_step(which, k).wait_recv()
        total[k + 1] = total[k] + got[k]
        if k + 1 < nb + 2:
            s_step(which, k + 1).start()

    def local(src, dst_, i):
        return pltpu.make_async_copy(src, dst_, lsem.at[i])

    loads = [
        local(win_hbm, w_all.at[t, pl.ds(o_in, d), :], 0),
        local(wout_hbm, w_all.at[t, pl.ds(o_out, ch), :], 1),
        local(wup_hbm, w_all.at[t, pl.ds(o_up, ff), :], 2),
        local(wdown_hbm, w_all.at[t, pl.ds(o_down, ff), :], 3),
        local(x_hbm, dproj.at[0], 4),
        local(cot_hbm, dproj.at[1], 5),
    ]
    for copy in loads:
        copy.start()
    cb[0, pl.ds(0, 4), :] = conv_ref[...]
    cb[0, pl.ds(4, 1), :] = bias_ref[...]
    barrier = pltpu.get_barrier_semaphore()
    for b in range(nb):
        pl.semaphore_signal(barrier, inc=1, device_id={"dp": flip(p, b)}, device_id_type=MESH)
    for j in range(1, blocks):
        pl.semaphore_signal(barrier, inc=1, device_id={"tensor": zflip(j)}, device_id_type=MESH)
    pl.semaphore_wait(barrier, nb + blocks - 1)

    def c_copy(j):
        return remote(cb.at[0], cb.at[j], csem.at[0, j], csem.at[1, j], tensor=zflip(j))

    hcopy = remote(dproj.at[0, pl.ds(rows - 16, 16), :], halo, zsem.at[0], zsem.at[1], tensor=partner)
    loads[0].wait()
    for j in range(1, blocks):
        for copy in w_sources(IN, j):
            copy.start()
    for j in range(1, blocks):
        c_copy(j).start()
    loads[4].wait()
    hcopy.start()
    loads[1].wait()
    for j in range(1, blocks):
        for copy in w_sources(OUT, j):
            copy.start()
    loads[2].wait()
    loads[3].wait()
    for j in range(1, blocks):
        for copy in w_sources(FF, j):
            copy.start()

    nlane = d // LANES

    def spread(ref):
        for seg in range(SEGS):
            v = ref[pl.ds(seg * steps, steps), :].astype(F32)
            for i in range(nlane):
                perm[i, pl.ds(seg, steps, stride=SEGS), :] = v[:, i * LANES : (i + 1) * LANES]

    def gather(ref):
        for seg in range(SEGS):
            for i in range(nlane):
                v = perm[i, pl.ds(seg, steps, stride=SEGS), :]
                ref[pl.ds(seg * steps, steps), i * LANES : (i + 1) * LANES] = v.astype(ref.dtype)

    def perm_rows(at):
        return jnp.concatenate([perm[i, pl.ds(at, CHUNK), :] for i in range(nlane)], axis=1)

    def put_perm(at, v):
        for i in range(nlane):
            perm[i, pl.ds(at, CHUNK), :] = v[:, i * LANES : (i + 1) * LANES]

    spread(dproj.at[0])
    limit = jnp.where(
        t == 0,
        short_ref[0],
        jnp.where(t == 1, short_ref[1], jnp.where(t == 2, long_ref[0], long_ref[0] - rows)),
    )

    def norm_rows(r, _):
        at = pl.multiple_of(r * CHUNK, CHUNK)
        xv = perm_rows(at)
        xp[pl.ds(at, CHUNK), :] = xv.astype(BF16)
        fv = xv * scale_of(xv) * g1_ref[...]
        lhs[pl.ds(at, CHUNK), :] = fv.astype(BF16)
        first_t[:, pl.ds(at, CHUNK)] = fv.T.astype(BF16)
        return 0

    lax.fori_loop(0, nchunk, norm_rows, 0)
    loads[5].wait()
    spread(dproj.at[1])
    w_all_j(IN, halves[IN] - 1)

    def dout_rows(r, _):
        at = pl.multiple_of(r * CHUNK, CHUNK)
        place = at + lax.broadcasted_iota(jnp.int32, (CHUNK, d), 0)
        pos = lax.rem(place, SEGS) * steps + place // SEGS
        dv = jnp.where(pos < limit, perm_rows(at), 0.0)
        dout[pl.ds(at, CHUNK), :] = dv.astype(BF16)
        dout_t[:, pl.ds(at, CHUNK)] = dv.T.astype(BF16)
        return 0

    lax.fori_loop(0, nchunk, dout_rows, 0)
    hcopy.wait()
    hv = halo[...].astype(F32)
    lhs[pl.ds(rows, 16), :] = (hv * scale_of(hv) * g1_ref[...]).astype(BF16)
    for j in range(1, blocks):
        c_copy(j).wait()

    seg_id = lax.broadcasted_iota(jnp.int32, (SEGS, ch), 0)
    has_prev = jnp.where(t == 3, 1.0, 0.0).astype(F32)
    has_next = jnp.where(t == 2, 1.0, 0.0).astype(F32)

    def forward_block(j, _):
        s_ = zflip(j)

        @pl.when(j > 0)
        def _():
            w_wait(IN, j, 0)

        def project(r, _):
            at = pl.multiple_of(r * CHUNK, CHUNK)
            v = dot(lhs[pl.ds(at, CHUNK), :], w_all[s_, pl.ds(o_in, d), :])
            bufa[pl.ds(at, CHUNK), :ch] = v[:, :ch]
            cand[j, pl.ds(at + 3 * SEGS, CHUNK), :] = v[:, ch:]
            return 0

        lax.fori_loop(0, nchunk, project, 0)

        @pl.when(j == 0)
        def _():
            for k in range(halves[IN] - 2, 0, -1):
                w_all_j(IN, k)

        @pl.when(j == 1)
        def _():
            for kind in (OUT, FF):
                for k in range(halves[kind] - 2, 0, -1):
                    w_all_j(kind, k)

        ph = dot(lhs[pl.ds(rows, 16), :], w_all[s_, pl.ds(o_in, d), ch:])
        for back in range(3):
            last = cand[j, pl.ds((steps + back) * SEGS, SEGS), :]
            rolled = pltpu.roll(last, 1, 0)
            edge = ph[13 + back : 14 + back, :] * has_prev
            cand[j, pl.ds(back * SEGS, SEGS), :] = jnp.where(seg_id == 0, edge, rolled)
        k_ = [jnp.broadcast_to(cb[j, pl.ds(i, 1), :], (SEGS, ch)) for i in range(4)]
        bias = jnp.broadcast_to(cb[j, pl.ds(4, 1), :], (SEGS, ch))

        def step4(i, carry):
            s, q_ = carry
            for q in range(4):
                at = pl.multiple_of((i * 4 + q) * SEGS, SEGS)
                u = sigmoid(bufa[pl.ds(at, SEGS), :ch] + bias)
                f = k_[0] * cand[j, pl.ds(at + 3 * SEGS, SEGS), :]
                for lag in range(1, 4):
                    f = f + k_[lag] * cand[j, pl.ds(at + (3 - lag) * SEGS, SEGS), :]
                upd[j, pl.ds(at, SEGS), :] = u
                dst[j, pl.ds(at, SEGS), :] = f
                a = 1.0 - u
                s = a * s + u * f
                q_ = a * q_
            return s, q_

        s, q_ = lax.fori_loop(
            0, steps // 4, step4, (jnp.zeros((SEGS, ch), F32), jnp.ones((SEGS, ch), F32))
        )
        ends[0, j] = s
        ends[1, j] = q_

        @pl.when(j == 0)
        def _():
            w_all_j(IN, 0)
            w_all_j(OUT, halves[OUT] - 1)
            w_all_j(FF, halves[FF] - 1)

        @pl.when(j == 1)
        def _():
            w_all_j(OUT, 0)
            w_all_j(FF, 0)

        return 0

    lax.fori_loop(0, blocks, forward_block, 0)

    def forward_chain(start):
        run = start
        for seg in range(SEGS):
            st[:, pl.ds(seg, 1), :] = run
            run = ends[0, :, pl.ds(seg, 1), :] + ends[1, :, pl.ds(seg, 1), :] * run
        return run

    fsend[...] = jnp.broadcast_to(forward_chain(jnp.zeros((blocks, 1, ch), F32)), (blocks, 8, ch))
    fcopies = [
        remote(fsend.at[j], frecv.at[j ^ 1], zsem.at[2 + 2 * j], zsem.at[3 + 2 * j], tensor=partner)
        for j in range(blocks)
    ]
    waits = [
        remote(fsend.at[j ^ 1], frecv.at[j], zsem.at[2 + 2 * (j ^ 1)], zsem.at[3 + 2 * (j ^ 1)], tensor=partner)
        for j in range(blocks)
    ]
    for copy in fcopies:
        copy.start()
    for j in range(blocks):
        waits[j].wait_recv()
    forward_chain(frecv[:, pl.ds(0, 1), :] * has_prev)

    def forward_fix(b, _):
        def step8(i, s):
            for q in range(8):
                at = pl.multiple_of((i * 8 + q) * SEGS, SEGS)
                u = upd[b, pl.ds(at, SEGS), :]
                s = (1.0 - u) * s + u * dst[b, pl.ds(at, SEGS), :]
                st[b, pl.ds(at + SEGS, SEGS), :] = s
            return s

        lax.fori_loop(0, steps // 8, step8, st[b, pl.ds(0, SEGS), :])
        return 0

    lax.fori_loop(0, blocks, forward_fix, 0)
    for j in range(1, blocks):
        w_wait(OUT, j, 0)
    shards = [zflip(j) for j in range(blocks)]

    def second_rows(r, _):
        at = pl.multiple_of(r * CHUNK, CHUNK)
        m = xp[pl.ds(at, CHUNK), :].astype(F32)
        for j in range(blocks):
            m = m + dot(
                st[j, pl.ds(at + SEGS, CHUNK), :].astype(BF16), w_all[shards[j], pl.ds(o_out, ch), :]
            )
        mid[pl.ds(at, CHUNK), :] = m
        sv = m * scale_of(m) * g2_ref[...]
        lhs[pl.ds(at, CHUNK), :] = sv.astype(BF16)
        second_t[:, pl.ds(at, CHUNK)] = sv.T.astype(BF16)
        bufa[pl.ds(at, CHUNK), :] = m
        bufc[pl.ds(at, CHUNK), :] = jnp.zeros((CHUNK, d), F32)
        return 0

    lax.fori_loop(0, nchunk, second_rows, 0)

    act, din = dproj.at[1], dproj.at[2]

    def ff_block(j, _):
        s_ = zflip(j)

        @pl.when(j > 0)
        def _():
            w_wait(FF, j, 0)

        def ff_rows(r, _):
            at = pl.multiple_of(r * CHUNK, CHUNK)
            wu = w_all[s_, pl.ds(o_up, ff), :]
            wd = w_all[s_, pl.ds(o_down, ff), :]
            inner = dot(lhs[pl.ds(at, CHUNK), :], wu)
            da = dot_t(dout[pl.ds(at, CHUNK), :], wd)
            cdf = 0.5 + 0.5 * lax.erf(inner * np.float32(np.sqrt(0.5)))
            pdf = jnp.exp(inner * inner * -0.5) * np.float32(1.0 / np.sqrt(2.0 * np.pi))
            av = (inner * cdf).astype(BF16)
            dv = (da * (cdf + inner * pdf)).astype(BF16)
            act[pl.ds(at, CHUNK), :] = av
            din[pl.ds(at, CHUNK), :] = dv
            bufa[pl.ds(at, CHUNK), :] += dot(av, wd)
            bufc[pl.ds(at, CHUNK), :] += dot_t(dv, wu)

            @pl.when((r == 0) & (j > 0))
            def _():
                r_first(FF, j - 1)

            @pl.when((r == 1) & (j > 1))
            def _():
                r_last(FF, j - 2)

            @pl.when((r == 2) & (j > 0))
            def _():
                r_middle(FF, j - 1)

            return 0

        lax.fori_loop(0, nchunk, ff_rows, 0)

        def ff_grads(r, _):
            at = pl.multiple_of(r * CHUNK, CHUNK)
            grad[s_, pl.ds(o_up + at, CHUNK), :] = dot(second_t[pl.ds(at, CHUNK), :], din[...]).astype(BF16)
            grad[s_, pl.ds(o_down + at, CHUNK), :] = dot(dout_t[pl.ds(at, CHUNK), :], act[...]).astype(BF16)
            return 0

        lax.fori_loop(0, d // CHUNK, ff_grads, 0)
        r_start(FF, j, 0)
        return 0

    lax.fori_loop(0, blocks, ff_block, 0)

    def second_back(r, gain):
        at = pl.multiple_of(r * CHUNK, CHUNK)
        put_perm(at, bufa[pl.ds(at, CHUNK), :])
        m = mid[pl.ds(at, CHUNK), :]
        s = scale_of(m)
        dn = bufc[pl.ds(at, CHUNK), :]
        gain = gain + jnp.sum(dn * m * s, axis=0, keepdims=True)
        gd = dn * g2_ref[...]
        dm = dout[pl.ds(at, CHUNK), :].astype(F32) + s * gd - m * (s * s * s * jnp.mean(gd * m, axis=-1, keepdims=True))
        mid[pl.ds(at, CHUNK), :] = dm
        lhs[pl.ds(at, CHUNK), :] = dm.astype(BF16)
        second_t[:, pl.ds(at, CHUNK)] = dm.T.astype(BF16)
        bufc[pl.ds(at, CHUNK), :] = jnp.zeros((CHUNK, d), F32)
        return gain

    gain2 = lax.fori_loop(0, nchunk, second_back, jnp.zeros((1, d), F32))
    gsum[0] = jnp.zeros((8, d), F32)
    gsum[0, pl.ds(1, 1), :] = gain2
    gather(dproj.at[0])
    res_copy = pltpu.make_async_copy(dproj.at[0], res_hbm, lsem.at[6])
    res_copy.start()
    r_first(FF, blocks - 1)
    r_last(FF, blocks - 2, blocks - 2)

    def backward_block(i, _):
        j = blocks - 1 - i
        s_ = zflip(j)

        def project(r, _):
            at = pl.multiple_of(r * CHUNK, CHUNK)
            dst[j, pl.ds(at, CHUNK), :] = dot_t(lhs[pl.ds(at, CHUNK), :], w_all[s_, pl.ds(o_out, ch), :])
            return 0

        lax.fori_loop(0, nchunk, project, 0)
        for half in range(2):
            rr = d // 2
            grad[s_, pl.ds(o_out, ch), half * ch : (half + 1) * ch] = dot(
                second_t[half * rr : (half + 1) * rr, :], st[j, pl.ds(SEGS, rows), :].astype(BF16)
            ).astype(BF16)
        r_start(OUT, j, 0)

        @pl.when(i == 0)
        def _():
            r_middle(FF, blocks - 1)

        def one(step, w, q_):
            at = pl.multiple_of(step * SEGS, SEGS)
            a = 1.0 - upd[j, pl.ds(at, SEGS), :]
            c = dst[j, pl.ds(at, SEGS), :] + w
            return c, a * c, q_ * a

        w, q_ = jnp.zeros((SEGS, ch), F32), jnp.ones((SEGS, ch), F32)
        for step in range(steps - 1, steps - 6, -1):
            _, w, q_ = one(step, w, q_)

        def step8(n, carry):
            w, q_ = carry
            for q in range(8):
                _, w, q_ = one(steps - 6 - (n * 8 + q), w, q_)
            return w, q_

        w, q_ = lax.fori_loop(0, (steps - 8) // 8, step8, (w, q_))
        for step in range(2, -1, -1):
            bends[2 * step, j] = q_
            c, w, q_ = one(step, w, q_)
            bends[2 * step + 1, j] = c
        bends[6, j] = w
        bends[7, j] = q_

        @pl.when(i == 1)
        def _():
            r_last(FF, blocks - 1, blocks - 1)

        @pl.when(i > 0)
        def _():
            r_first(OUT, j + 1)

        @pl.when(i > 1)
        def _():
            r_middle(OUT, j + 2)

        @pl.when(i > 2)
        def _():
            r_last(OUT, j + 3)

        return 0

    lax.fori_loop(0, blocks, backward_block, 0)

    def backward_chain(start):
        run = start
        for seg in range(SEGS - 1, -1, -1):
            ends[0, :, pl.ds(seg, 1), :] = run
            run = bends[6, :, pl.ds(seg, 1), :] + bends[7, :, pl.ds(seg, 1), :] * run
        return run

    bsend[:, pl.ds(0, 1), :] = backward_chain(jnp.zeros((blocks, 1, ch), F32))
    for step in range(3):
        bsend[:, pl.ds(step + 1, 1), :] = upd[:, pl.ds(step * SEGS, 1), :] * (
            bends[2 * step + 1, :, pl.ds(0, 1), :]
            + bends[2 * step, :, pl.ds(0, 1), :] * ends[0, :, pl.ds(0, 1), :]
        )
    bcopies = [
        remote(bsend.at[j], brecv.at[j ^ 1], zsem.at[10 + 2 * j], zsem.at[11 + 2 * j], tensor=partner)
        for j in range(blocks)
    ]
    bwaits = [
        remote(bsend.at[j ^ 1], brecv.at[j], zsem.at[10 + 2 * (j ^ 1)], zsem.at[11 + 2 * (j ^ 1)], tensor=partner)
        for j in range(blocks)
    ]
    for copy in bcopies:
        copy.start()
    r_first(OUT, 0)
    r_middle(OUT, 1)
    r_last(OUT, 2, 2)
    for j in range(blocks):
        bwaits[j].wait_recv()
    backward_chain(brecv[:, pl.ds(0, 1), :] * has_next)
    csum[0] = jnp.zeros((blocks, 8, ch), F32)
    res_copy.wait()

    def backward_fix(i, _):
        j = blocks - 1 - i
        s_ = zflip(j)
        w = ends[0, j]
        after = []
        for step in range(3):
            df = upd[j, pl.ds(step * SEGS, SEGS), :] * (bends[2 * step + 1, j] + bends[2 * step, j] * w)
            edge = brecv[j, pl.ds(step + 1, 1), :] * has_next
            after.append(jnp.where(seg_id == SEGS - 1, edge, pltpu.roll(df, SEGS - 1, 0)))
        k_ = [jnp.broadcast_to(cb[j, pl.ds(n, 1), :], (SEGS, ch)) for n in range(4)]
        zero = jnp.zeros((SEGS, ch), F32)

        def pair(n, carry):
            w, d1, d2, d3, c0, c1, c2, k0, k1, k2, k3, gb = carry
            top = steps - 2 - 2 * n
            made = []
            for q in range(2):
                at = pl.multiple_of((top + 1 - q) * SEGS, SEGS)
                u = upd[j, pl.ds(at, SEGS), :]
                c = dst[j, pl.ds(at, SEGS), :] + w
                d0 = c * u
                a = 1.0 - u
                w = a * c
                c3 = cand[j, pl.ds(at, SEGS), :]
                f = k_[0] * c0 + k_[1] * c1 + k_[2] * c2 + k_[3] * c3
                dg = d0 * a * (f - st[j, pl.ds(at, SEGS), :])
                dc = k_[0] * d0 + k_[1] * d1 + k_[2] * d2 + k_[3] * d3
                k0, k1, k2, k3 = k0 + d0 * c0, k1 + d0 * c1, k2 + d0 * c2, k3 + d0 * c3
                gb = gb + dg
                c0, c1, c2 = c1, c2, c3
                d1, d2, d3 = d0, d1, d2
                made.append((dg, dc))
            at = pl.multiple_of(top * SEGS, 2 * SEGS)
            dproj[j, pl.ds(at, 2 * SEGS), :ch] = jnp.concatenate([made[1][0], made[0][0]], axis=0).astype(BF16)
            dproj[j, pl.ds(at, 2 * SEGS), ch:] = jnp.concatenate([made[1][1], made[0][1]], axis=0).astype(BF16)
            return w, d1, d2, d3, c0, c1, c2, k0, k1, k2, k3, gb

        window = [cand[j, pl.ds((steps + 2 - n) * SEGS, SEGS), :] for n in range(3)]
        out = lax.fori_loop(0, steps // 2, pair, (w, *after, *window, zero, zero, zero, zero, zero))
        for n in range(5):
            csum[0, s_, pl.ds(n, 1), :] = jnp.sum(out[7 + n], axis=0, keepdims=True)

        @pl.when(i == 0)
        def _():
            r_middle(OUT, 0)
            r_last(OUT, 1, 1)
            r_total(FF)
            a_start(FF, halves[FF] - 1)

        @pl.when(i == 1)
        def _():
            r_last(OUT, 0, 0)
            for k in range(halves[FF] - 2, 0, -1):
                a_wait(FF, k + 1)
                a_start(FF, k)

        @pl.when(i == 2)
        def _():
            a_wait(FF, 1)
            a_start(FF, 0)
            r_total(OUT)
            a_start(OUT, halves[OUT] - 1)

        @pl.when(i == 3)
        def _():
            for k in range(halves[OUT] - 2, 0, -1):
                a_wait(OUT, k + 1)
                a_start(OUT, k)

        @pl.when(i > 0)
        def _():
            r_first(IN, j + 1)

        @pl.when(i > 1)
        def _():
            r_last(IN, j + 2)

        def first_grad(r, _):
            at = pl.multiple_of(r * CHUNK, CHUNK)
            grad[s_, pl.ds(o_in + at, CHUNK), :] = dot(first_t[pl.ds(at, CHUNK), :], dproj[j]).astype(BF16)
            return 0

        lax.fori_loop(0, d // CHUNK, first_grad, 0)
        r_start(IN, j, 0)

        @pl.when(i > 0)
        def _():
            r_middle(IN, j + 1)

        return 0

    lax.fori_loop(0, blocks, backward_fix, 0)
    s_step(1, 0).start()

    def first_back(r):
        at = r * CHUNK
        v = dot_t(dproj[0, pl.ds(at, CHUNK), :], w_all[shards[0], pl.ds(o_in, d), :])
        for j in range(1, blocks):
            v = v + dot_t(dproj[j, pl.ds(at, CHUNK), :], w_all[shards[j], pl.ds(o_in, d), :])
        bufc[pl.ds(at, CHUNK), :] = v

    first_back(0)
    r_first(IN, 0)
    r_last(IN, 1, 1)
    s_next(1, 0)
    first_back(1)
    a_wait(OUT, 1)
    a_start(OUT, 0)
    s_next(1, 1)
    first_back(2)
    r_middle(IN, 0)
    s_next(1, 2)
    for r in range(3, nchunk):
        first_back(r)

    def first_norm_back(r, gain):
        at = pl.multiple_of(r * CHUNK, CHUNK)
        m = xp[pl.ds(at, CHUNK), :].astype(F32)
        s = scale_of(m)
        dn = bufc[pl.ds(at, CHUNK), :]
        gain = gain + jnp.sum(dn * m * s, axis=0, keepdims=True)
        gd = dn * g1_ref[...]
        dv = s * gd - m * (s * s * s * jnp.mean(gd * m, axis=-1, keepdims=True))
        put_perm(at, mid[pl.ds(at, CHUNK), :] + dv)
        return gain

    gsum[0, pl.ds(0, 1), :] = lax.fori_loop(0, nchunk, first_norm_back, jnp.zeros((1, d), F32))
    s_step(0, 0).start()
    r_last(IN, 0, 0)
    r_total(IN)
    a_start(IN, halves[IN] - 1)
    for k in range(3, nb + 2):
        s_next(1, k)
    gather(mid)
    gx_copy = pltpu.make_async_copy(mid, gx_hbm, lsem.at[7])
    gx_copy.start()
    chan_ref[...] = csum[nb + 2, t]
    s_next(0, 0)
    for k in range(halves[IN] - 2, 0, -1):
        a_wait(IN, k + 1)
        a_start(IN, k)
    a_wait(FF, 0)
    gup_ref[...] = fin[pl.ds(o_up, d), :].astype(F32)
    gdown_ref[...] = fin[pl.ds(o_down, d), :].astype(F32).T
    s_next(0, 1)
    a_wait(OUT, 0)
    gout_ref[:, :half_d] = fin[pl.ds(o_out, ch), :ch].astype(F32).T
    gout_ref[:, half_d:] = fin[pl.ds(o_out, ch), ch:].astype(F32).T
    a_wait(IN, 1)
    a_start(IN, 0)
    for k in range(2, nb + 2):
        s_next(0, k)
    gains_ref[...] = gsum[nb + 2]
    a_wait(IN, 0)
    gin_ref[...] = fin[pl.ds(o_in, d), :].astype(F32)

    gx_copy.wait()
    for copy in fcopies + bcopies:
        copy.wait_send()
    for kind in (IN, OUT, FF):
        def drain(j, _):
            for copy in w_sources(kind, j):
                copy.wait_send()
            for k in range(halves[kind]):
                for copy in w_step(kind, j, k):
                    copy.wait_send()
            for copy in r_z(kind, j):
                copy.wait_send()
            return 0

        lax.fori_loop(1, blocks, drain, 0)

        def drain_halving(j, _):
            for k in range(halves[kind]):
                for copy in r_step(kind, j, k):
                    copy.wait_send()
            return 0

        lax.fori_loop(0, blocks, drain_halving, 0)
        for k in range(halves[kind]):
            for copy in a_step(kind, k):
                copy.wait_send()
    for k in range(nb + 2):
        s_step(0, k).wait_send()
        s_step(1, k).wait_send()


def per_device(
    inputs,
    norm_gain,
    in_weight,
    conv_kernel,
    gate_bias,
    out_weight,
    mlp_gain,
    up_weight,
    down_weight,
    short_lengths,
    long_lengths,
    cotangent,
):
    rows, d = inputs.shape
    ch = in_weight.shape[2]
    ff = up_weight.shape[1]
    blocks = lax.axis_size("tensor")
    dp = lax.axis_size("dp")
    nb = log2(dp)
    assert dp == 1 << nb and blocks == 4 and rows == LSHORT and 2 * rows == LLONG
    assert short_lengths.shape == (2,) and long_lengths.shape == (1,)
    sizes = (d, ch, 2 * ff)
    total = sum(sizes)
    halves = tuple(min(nb, log2(r // TILE)) for r in sizes)

    def span_all(k):
        return sum(r >> min(k, h) for r, h in zip(sizes, halves))

    vm = pl.BlockSpec(memory_space=pltpu.VMEM)
    sm = pl.BlockSpec(memory_space=pltpu.SMEM)
    hb = pl.BlockSpec(memory_space=pl.ANY)
    dma = pltpu.SemaphoreType.DMA
    result, grad_inputs, gin, gout, gup, gdown, gains, chan = pl.pallas_call(
        functools.partial(block_kernel, (rows, d, blocks, ch, ff, nb)),
        out_shape=(
            jax.ShapeDtypeStruct((rows, d), BF16),
            jax.ShapeDtypeStruct((rows, d), F32),
            jax.ShapeDtypeStruct((d, 2 * ch), F32),
            jax.ShapeDtypeStruct((ch, d), F32),
            jax.ShapeDtypeStruct((d, ff), F32),
            jax.ShapeDtypeStruct((ff, d), F32),
            jax.ShapeDtypeStruct((8, d), F32),
            jax.ShapeDtypeStruct((8, ch), F32),
        ),
        in_specs=[sm, sm, hb, hb, vm, vm, vm, vm, hb, hb, hb, hb],
        out_specs=(hb, hb) + (vm,) * 6,
        scratch_shapes=[
            pltpu.VMEM((blocks, total, d), BF16),
            pltpu.VMEM((blocks, total, d), BF16),
            pltpu.VMEM((total, d), BF16),
            pltpu.VMEM((rows, d), BF16),
            pltpu.VMEM((blocks, rows + 3 * SEGS, ch), F32),
            pltpu.VMEM((blocks, rows, ch), F32),
            pltpu.VMEM((blocks, rows + SEGS, ch), F32),
            pltpu.VMEM((blocks, rows, ch), F32),
            pltpu.VMEM((rows + 16, d), BF16),
            pltpu.VMEM((d, rows), BF16),
            pltpu.VMEM((d, rows), BF16),
            pltpu.VMEM((rows, d), BF16),
            pltpu.VMEM((d, rows), BF16),
            pltpu.VMEM((rows, d), F32),
            pltpu.VMEM((rows, d), F32),
            pltpu.VMEM((rows, d), F32),
            pltpu.VMEM((blocks, rows, d), BF16),
            pltpu.VMEM((d // LANES, rows, LANES), F32),
            pltpu.VMEM((16, d), BF16),
            pltpu.VMEM((blocks, 8, ch), F32),
            pltpu.VMEM((2, blocks, SEGS, ch), F32),
            pltpu.VMEM((8, blocks, SEGS, ch), F32),
            pltpu.VMEM((blocks, 8, ch), F32),
            pltpu.VMEM((blocks, 8, ch), F32),
            pltpu.VMEM((blocks, 8, ch), F32),
            pltpu.VMEM((blocks, 8, ch), F32),
            pltpu.VMEM((blocks, span_all(nb), d), BF16),
            pltpu.VMEM((nb + 3, 8, d), F32),
            pltpu.VMEM((nb + 2, 8, d), F32),
            pltpu.VMEM((nb + 3, blocks, 8, ch), F32),
            pltpu.VMEM((nb + 2, blocks, 8, ch), F32),
            dma((8,)),
            dma((2, blocks)),
            dma((18,)),
            dma((3, blocks, nb + 1, 2)),
            dma((3, blocks, nb + 1, 2)),
            dma((3, blocks, nb + 1, 2)),
            dma((3, blocks, nb + 1, 2)),
            dma((3, nb, 2)),
            dma((3, nb, 2)),
            dma((2, nb + 2)),
            dma((2, nb + 2)),
        ]
        + [pltpu.VMEM((blocks, span_all(k + 1), d), BF16) for k in range(nb)],
        compiler_params=pltpu.CompilerParams(
            collective_id=0, has_side_effects=True, vmem_limit_bytes=67043328
        ),
        name="block",
    )(
        short_lengths,
        long_lengths,
        inputs,
        cotangent,
        norm_gain[None],
        mlp_gain[None],
        conv_kernel,
        gate_bias[None],
        in_weight.reshape(d, 2 * ch),
        out_weight,
        up_weight,
        down_weight,
    )
    return (
        result,
        grad_inputs,
        gains[0],
        gin.reshape(d, 2, ch),
        chan[:4],
        chan[4],
        gout,
        gains[1],
        gup,
        gdown,
    )


def solution(mesh):
    placed = (
        P(("dp", "tensor"), None),
        P(),
        P(None, None, "tensor"),
        P(None, "tensor"),
        P("tensor"),
        P("tensor", None),
        P(),
        P(None, "tensor"),
        P("tensor", None),
        P("dp"),
        P("dp"),
        P(("dp", "tensor"), None),
    )
    return jax.shard_map(
        per_device,
        mesh=mesh,
        in_specs=placed,
        out_specs=(
            P(("dp", "tensor"), None),
            P(("dp", "tensor"), None),
            P(),
            P(None, None, "tensor"),
            P(None, "tensor"),
            P("tensor"),
            P("tensor", None),
            P(),
            P(None, "tensor"),
            P("tensor", None),
        ),
        check_vma=False,
    )
```

```python
import functools

import jax
import jax.numpy as jnp
import numpy as np
from jax import lax
from jax.experimental import pallas as pl
from jax.experimental.pallas import tpu as pltpu
from jax.sharding import PartitionSpec as P

LSHORT = 1024
LLONG = 2048
SEGS = 8
EPS = 1e-05
CHUNK = 256
TILE = 16
LANES = 128
F32 = jnp.float32
BF16 = jnp.bfloat16
MESH = pl.DeviceIdType.MESH
IN, OUT, FF = 0, 1, 2


def dot(a, b):
    return jnp.dot(a, b, preferred_element_type=F32)


def dot_t(a, b):
    return lax.dot_general(a, b, (((1,), (1,)), ((), ())), preferred_element_type=F32)


def scale_of(v):
    return lax.rsqrt(jnp.mean(v * v, axis=-1, keepdims=True) + EPS)


def sigmoid(v):
    return 1.0 / (1.0 + jnp.exp(-v))


def bit_of(v, bit):
    return lax.rem(lax.div(v, 1 << bit), 2)


def flip(v, bit):
    return v + (1 << bit) * (1 - 2 * bit_of(v, bit))


def log2(n):
    return int(n).bit_length() - 1


def bit_groups(nb):
    groups = [(0,)] + [tuple(range(b, min(b + 2, nb))) for b in range(1, nb, 2)]
    return groups + [(nb, nb + 1)]


def block_kernel(
    dims,
    short_ref,
    long_ref,
    x_hbm,
    cot_hbm,
    g1_ref,
    g2_ref,
    conv_ref,
    bias_ref,
    win_hbm,
    wout_hbm,
    wup_hbm,
    wdown_hbm,
    res_hbm,
    gx_hbm,
    fin,
    gains_ref,
    chan_ref,
    w_all,
    grad,
    xp,
    cand,
    upd,
    st,
    dst,
    lhs,
    first_t,
    second_t,
    dout,
    dout_t,
    bufa,
    mid,
    bufc,
    dproj,
    perm,
    halo,
    cb,
    ends,
    bends,
    fsend,
    frecv,
    bsend,
    brecv,
    zbuf,
    ssum,
    sgot,
    lsem,
    c_s,
    c_r,
    f_s,
    f_r,
    b_s,
    b_r,
    h_s,
    h_r,
    w_s,
    w_r,
    r_s,
    r_r,
    x_s,
    a_s,
    a_r,
    s_s,
    s_r,
    *stage_bufs,
):
    rows, d, blocks, ch, ff, nb = dims
    steps = rows // SEGS
    t = lax.axis_index("tensor")
    p = lax.axis_index("dp")
    partner = flip(t, 0)
    nchunk = rows // CHUNK
    offs = (0, d, d + ch)
    sizes = (d, ch, 2 * ff)
    o_in, o_out, o_up, o_down = 0, d, d + ch, d + ch + ff
    halves = tuple(min(nb, log2(r // TILE)) for r in sizes)
    half_d = d // 2
    lanes = (pl.ds(0, half_d), pl.ds(half_d, half_d))
    orders = ((0,) + tuple(range(nb - 1, 0, -1)), tuple(range(nb)))
    nstage = len(stage_bufs)

    def zflip(j):
        b0, b1 = lax.rem(j, 2), lax.div(j, 2)
        return t + b0 * (1 - 2 * bit_of(t, 0)) + b1 * (2 - 4 * bit_of(t, 1))

    def low_of(kind, c, k):
        low = 0
        for i in range(min(k, halves[kind])):
            low = low + bit_of(p, orders[c][i]) * (sizes[kind] >> (i + 1))
        return low

    def span(kind, k):
        return sizes[kind] >> min(k, halves[kind])

    def at_rows(kind, start, n):
        return pl.ds(pl.multiple_of(offs[kind] + start, TILE), n)

    def stage_rows(kind, k):
        base = sum(span(i, k + 1) for i in range(kind))
        return pl.ds(base, span(kind, k + 1))

    def remote(src, dst_, ss, rs, **dev):
        return pltpu.make_async_remote_copy(
            src_ref=src, dst_ref=dst_, send_sem=ss, recv_sem=rs, device_id=dev, device_id_type=MESH
        )

    def wait_for(ref, sem):
        pltpu.make_async_copy(ref, ref, sem).wait()

    def w_step(kind, j, k):
        made = []
        for c in range(1 if k == 0 else 2):
            at = at_rows(kind, low_of(kind, c, k + 1), span(kind, k + 1))
            ref = w_all.at[zflip(j), at, slice(None) if k == 0 else lanes[c]]
            made.append(remote(ref, ref, w_s.at[kind, k], w_r.at[kind, j, k], dp=flip(p, orders[c][k])))
        return made

    def w_sources(kind, j):
        made = []
        for c in range(2):
            ref = w_all.at[t, at_rows(kind, low_of(kind, c, nb), span(kind, nb)), lanes[c]]
            made.append(remote(ref, ref, w_s.at[kind, nb], w_r.at[kind, j, nb], tensor=zflip(j)))
        return made

    def w_wait(kind, j, k):
        k_ = nb if k == halves[kind] else k
        wait_for(w_all.at[0, pl.ds(0, span(kind, k + 1))], w_r.at[kind, j, k_])

    def w_forward(kind, j, k):
        w_wait(kind, j, k + 1)
        for copy in w_step(kind, j, k):
            copy.start()

    def w_top(kind, *js):
        for j in js:
            w_forward(kind, j, halves[kind] - 1)

    def w_mid(kind, *js):
        for k in range(halves[kind] - 2, 0, -1):
            for j in js:
                w_forward(kind, j, k)

    def w_end(kind, *js):
        for j in js:
            w_forward(kind, j, 0)

    def r_step(kind, j, k):
        s = zflip(j)
        base = sum(span(i, k + 1) for i in range(kind))
        made = []
        for c in range(1 if k == 0 else 2):
            low = low_of(kind, c, k)
            if k < halves[kind]:
                low = low + (1 - bit_of(p, orders[c][k])) * span(kind, k + 1)
            which = slice(None) if k == 0 else lanes[c]
            made.append(
                remote(
                    grad.at[s, at_rows(kind, low, span(kind, k + 1)), which],
                    stage_bufs[k].at[j, pl.ds(base, span(kind, k + 1)), which],
                    r_s.at[kind, k] if k < halves[kind] else x_s.at[kind, j, k],
                    r_r.at[kind, j, k],
                    dp=flip(p, orders[c][k]),
                )
            )
        return made

    def r_start(kind, j, k):
        for copy in r_step(kind, j, k):
            copy.start()

    def r_finish(kind, j, k):
        s = zflip(j)
        buf = stage_bufs[k]
        base = sum(span(i, k + 1) for i in range(kind))
        n = span(kind, k + 1)
        here = stage_bufs[k].at[j, pl.ds(base, n), :]
        if k >= halves[kind]:
            wait_for(here, x_s.at[kind, j, k])
        wait_for(here, r_r.at[kind, j, k])
        piece = min(n, 128)
        for c in range(2):
            low = low_of(kind, c, k + 1)

            def add(i, _):
                at = at_rows(kind, low + i * piece, piece)
                here = pl.ds(pl.multiple_of(base + i * piece, TILE), piece)
                grad[s, at, lanes[c]] = (
                    grad[s, at, lanes[c]].astype(F32) + buf[j, here, lanes[c]].astype(F32)
                ).astype(BF16)
                return 0

            lax.fori_loop(0, n // piece, add, 0)

    def r_z(kind, j):
        s = zflip(j)
        base = sum(span(i, nb) for i in range(kind))
        made = []
        for c in range(2):
            at = at_rows(kind, low_of(kind, c, nb), span(kind, nb))
            made.append(
                remote(
                    grad.at[s, at, lanes[c]],
                    zbuf.at[j, pl.ds(base, span(kind, nb)), lanes[c]],
                    r_s.at[kind, nb],
                    r_r.at[kind, j, nb],
                    tensor=s,
                )
            )
        return made

    def r_out(kind, j):
        for copy in r_z(kind, j):
            copy.start()

    def r_total(kind):
        base = sum(span(i, nb) for i in range(kind))
        n = span(kind, nb)
        for j in range(1, blocks):
            wait_for(zbuf.at[j, pl.ds(base, n), :], r_r.at[kind, j, nb])
        for c in range(2):
            at = at_rows(kind, low_of(kind, c, nb), n)
            total = grad[t, at, lanes[c]].astype(F32)
            for j in range(1, blocks):
                total = total + zbuf[j, pl.ds(base, n), lanes[c]].astype(F32)
            fin[at, lanes[c]] = total.astype(BF16)

    def a_step(kind, k):
        made = []
        for c in range(1 if k == 0 else 2):
            at = at_rows(kind, low_of(kind, c, k + 1), span(kind, k + 1))
            ref = fin.at[at, slice(None) if k == 0 else lanes[c]]
            made.append(remote(ref, ref, a_s.at[kind, k], a_r.at[kind, k], dp=flip(p, orders[c][k])))
        return made

    def a_start(kind, k):
        for copy in a_step(kind, k):
            copy.start()

    def a_wait(kind, k):
        wait_for(fin.at[pl.ds(0, span(kind, k + 1)), :], a_r.at[kind, k])

    def r_middle(kind, j):
        for k in range(1, nb - 1):
            r_finish(kind, j, k)
            r_start(kind, j, k + 1)

    def r_first(kind, j):
        r_finish(kind, j, 0)
        r_start(kind, j, 1)

    def r_last(kind, j):
        r_finish(kind, j, nb - 1)
        if isinstance(j, int):
            if j > 0:
                r_out(kind, j)
        else:
            pl.when(j > 0)(lambda: r_out(kind, j))

    def a_first(kind):
        r_total(kind)
        a_start(kind, halves[kind] - 1)

    def a_mid(kind):
        for k in range(halves[kind] - 2, 0, -1):
            a_wait(kind, k + 1)
            a_start(kind, k)

    def a_end(kind):
        a_wait(kind, 1)
        a_start(kind, 0)

    groups = bit_groups(nb)

    def s_start(g):
        bits = groups[g]
        for r in range(1, 1 << len(bits)):
            dp_, tensor_ = p, t
            for i, b in enumerate(bits):
                if r >> i & 1:
                    dp_, tensor_ = (flip(dp_, b), tensor_) if b < nb else (dp_, flip(tensor_, b - nb))
            dev = {"dp": dp_} if bits[0] < nb else {"tensor": tensor_}
            remote(ssum.at[g], sgot.at[g, r - 1], s_s.at[g], s_r.at[g, r - 1], **dev).start()

    def s_next(g):
        n = (1 << len(groups[g])) - 1
        for r in range(n):
            wait_for(sgot.at[g, r], s_r.at[g, r])
        v = ssum[g] + sgot[g, 0]
        if n == 3:
            v = v + (sgot[g, 1] + sgot[g, 2])
        ssum[g + 1] = v
        if g + 1 < len(groups):
            s_start(g + 1)

    def local(src, dst_, i):
        return pltpu.make_async_copy(src, dst_, lsem.at[i])

    loads = [
        local(win_hbm, w_all.at[t, pl.ds(o_in, d), :], 0),
        local(wout_hbm, w_all.at[t, pl.ds(o_out, ch), :], 1),
        local(wup_hbm, w_all.at[t, pl.ds(o_up, ff), :], 2),
        local(wdown_hbm, w_all.at[t, pl.ds(o_down, ff), :], 3),
        local(x_hbm, dproj.at[0], 4),
        local(cot_hbm, dproj.at[1], 5),
    ]
    for copy in loads:
        copy.start()
    frecv[...] = jnp.zeros_like(frecv)
    brecv[...] = jnp.zeros_like(brecv)
    halo[...] = jnp.zeros_like(halo)
    cb[0, pl.ds(0, 4), :] = conv_ref[...]
    cb[0, pl.ds(4, 1), :] = bias_ref[...]
    barrier = pltpu.get_barrier_semaphore()
    for b in range(nb):
        pl.semaphore_signal(barrier, inc=1, device_id={"dp": flip(p, b)}, device_id_type=MESH)
    for j in range(1, blocks):
        pl.semaphore_signal(barrier, inc=1, device_id={"tensor": zflip(j)}, device_id_type=MESH)
    pl.semaphore_wait(barrier, nb + blocks - 1)

    def c_copy(j):
        return remote(cb.at[0], cb.at[j], c_s.at[0], c_r.at[j], tensor=zflip(j))

    hcopy = remote(dproj.at[0, pl.ds(rows - 16, 16), :], halo, h_s.at[0], h_r.at[0], tensor=partner)
    for j in range(1, blocks):
        c_copy(j).start()
    loads[0].wait()
    for j in range(1, blocks):
        for copy in w_sources(IN, j):
            copy.start()
    loads[4].wait()
    pl.when(t == 2)(hcopy.start)
    loads[1].wait()
    for j in range(1, blocks):
        for copy in w_sources(OUT, j):
            copy.start()
    loads[2].wait()
    loads[3].wait()
    for j in range(1, blocks):
        for copy in w_sources(FF, j):
            copy.start()

    nlane = d // LANES

    def spread(ref):
        for seg in range(SEGS):
            v = ref[pl.ds(seg * steps, steps), :].astype(F32)
            for i in range(nlane):
                perm[i, pl.ds(seg, steps, stride=SEGS), :] = v[:, i * LANES : (i + 1) * LANES]

    def gather(ref):
        for seg in range(SEGS):
            for i in range(nlane):
                v = perm[i, pl.ds(seg, steps, stride=SEGS), :]
                ref[pl.ds(seg * steps, steps), i * LANES : (i + 1) * LANES] = v.astype(ref.dtype)

    def perm_rows(at):
        return jnp.concatenate([perm[i, pl.ds(at, CHUNK), :] for i in range(nlane)], axis=1)

    def put_perm(at, v):
        for i in range(nlane):
            perm[i, pl.ds(at, CHUNK), :] = v[:, i * LANES : (i + 1) * LANES]

    spread(dproj.at[0])
    limit = jnp.where(
        t == 0,
        short_ref[0],
        jnp.where(t == 1, short_ref[1], jnp.where(t == 2, long_ref[0], long_ref[0] - rows)),
    )

    def norm_rows(r, _):
        at = pl.multiple_of(r * CHUNK, CHUNK)
        xv = perm_rows(at)
        xp[pl.ds(at, CHUNK), :] = xv.astype(BF16)
        fv = xv * scale_of(xv) * g1_ref[...]
        lhs[pl.ds(at, CHUNK), :] = fv.astype(BF16)
        first_t[:, pl.ds(at, CHUNK)] = fv.T.astype(BF16)
        return 0

    lax.fori_loop(0, nchunk, norm_rows, 0)
    loads[5].wait()
    spread(dproj.at[1])

    def dout_rows(r, _):
        at = pl.multiple_of(r * CHUNK, CHUNK)
        place = at + lax.broadcasted_iota(jnp.int32, (CHUNK, d), 0)
        pos = lax.rem(place, SEGS) * steps + place // SEGS
        dv = jnp.where(pos < limit, perm_rows(at), 0.0)
        dout[pl.ds(at, CHUNK), :] = dv.astype(BF16)
        dout_t[:, pl.ds(at, CHUNK)] = dv.T.astype(BF16)
        return 0

    lax.fori_loop(0, nchunk, dout_rows, 0)
    w_top(IN, 1)
    pl.when(t == 3)(hcopy.wait_recv)
    pl.when(t == 2)(hcopy.wait_send)
    hv = halo[...].astype(F32)
    lhs[pl.ds(rows, 16), :] = (hv * scale_of(hv) * g1_ref[...]).astype(BF16)

    seg_id = lax.broadcasted_iota(jnp.int32, (SEGS, ch), 0)
    has_prev = jnp.where(t == 3, 1.0, 0.0).astype(F32)
    has_next = jnp.where(t == 2, 1.0, 0.0).astype(F32)

    def forward_block(j, _):
        s_ = zflip(j)

        @pl.when(j > 0)
        def _():
            c_copy(j).wait_recv()
            w_wait(IN, j, 0)

        def project(r, _):
            at = pl.multiple_of(r * CHUNK, CHUNK)
            v = dot(lhs[pl.ds(at, CHUNK), :], w_all[s_, pl.ds(o_in, d), :])
            bufa[pl.ds(at, CHUNK), :ch] = v[:, :ch]
            cand[j, pl.ds(at + 3 * SEGS, CHUNK), :] = v[:, ch:]
            return 0

        lax.fori_loop(0, nchunk, project, 0)

        @pl.when(j == 0)
        def _():
            w_top(IN, 2)
            w_mid(IN, 1)

        @pl.when(j == 1)
        def _():
            w_end(IN, 2)
            w_mid(IN, 3)

        @pl.when(j == 2)
        def _():
            w_end(IN, 3)
            w_top(OUT, 1, 2, 3)

        @pl.when(j == 3)
        def _():
            w_mid(OUT, 1, 2, 3)
            w_mid(FF, 1)

        ph = dot(lhs[pl.ds(rows, 16), :], w_all[s_, pl.ds(o_in, d), ch:])
        for back in range(3):
            last = cand[j, pl.ds((steps + back) * SEGS, SEGS), :]
            rolled = pltpu.roll(last, 1, 0)
            edge = ph[13 + back : 14 + back, :] * has_prev
            cand[j, pl.ds(back * SEGS, SEGS), :] = jnp.where(seg_id == 0, edge, rolled)
        k_ = [jnp.broadcast_to(cb[j, pl.ds(i, 1), :], (SEGS, ch)) for i in range(4)]
        bias = jnp.broadcast_to(cb[j, pl.ds(4, 1), :], (SEGS, ch))

        def step4(i, carry):
            s, q_ = carry
            for q in range(4):
                at = pl.multiple_of((i * 4 + q) * SEGS, SEGS)
                u = sigmoid(bufa[pl.ds(at, SEGS), :ch] + bias)
                f = k_[0] * cand[j, pl.ds(at + 3 * SEGS, SEGS), :]
                for lag in range(1, 4):
                    f = f + k_[lag] * cand[j, pl.ds(at + (3 - lag) * SEGS, SEGS), :]
                upd[j, pl.ds(at, SEGS), :] = u
                dst[j, pl.ds(at, SEGS), :] = f
                a = 1.0 - u
                s = a * s + u * f
                q_ = a * q_
            return s, q_

        s, q_ = lax.fori_loop(
            0, steps // 4, step4, (jnp.zeros((SEGS, ch), F32), jnp.ones((SEGS, ch), F32))
        )
        ends[0, j] = s
        ends[1, j] = q_
        fsend[j] = jnp.broadcast_to(forward_chain(j, jnp.zeros((1, ch), F32)), (8, ch))
        pl.when(t == 2)(f_copy(j).start)

        @pl.when(j == 0)
        def _():
            w_mid(IN, 2)
            w_top(IN, 3)
            w_end(IN, 1)

        @pl.when(j == 2)
        def _():
            w_top(FF, 1)

        @pl.when(j == 3)
        def _():
            w_end(OUT, 1, 2, 3)
            w_top(FF, 2)

        return 0

    def forward_chain(j, start):
        run = start
        for seg in range(SEGS):
            st[j, pl.ds(seg, 1), :] = run
            run = ends[0, j, pl.ds(seg, 1), :] + ends[1, j, pl.ds(seg, 1), :] * run
        return run

    def f_copy(j):
        there = flip(j, 0)
        return remote(fsend.at[j], frecv.at[there], f_s.at[0], f_r.at[there], tensor=partner)

    lax.fori_loop(0, blocks, forward_block, 0)
    w_mid(FF, 2)
    w_top(FF, 3)
    w_end(FF, 1)

    def forward_fix(i, _):
        b = flip(i, 0)

        @pl.when(t == 3)
        def _():
            wait_for(frecv.at[b], f_r.at[b])

        forward_chain(b, frecv[b, pl.ds(0, 1), :] * has_prev)

        def step8(i, s):
            for q in range(8):
                at = pl.multiple_of((i * 8 + q) * SEGS, SEGS)
                u = upd[b, pl.ds(at, SEGS), :]
                s = (1.0 - u) * s + u * dst[b, pl.ds(at, SEGS), :]
                st[b, pl.ds(at + SEGS, SEGS), :] = s
            return s

        lax.fori_loop(0, steps // 8, step8, st[b, pl.ds(0, SEGS), :])
        return 0

    lax.fori_loop(0, blocks, forward_fix, 0)
    for j in range(1, blocks):
        w_wait(OUT, j, 0)
    shards = [zflip(j) for j in range(blocks)]

    def second_rows(r, _):
        at = pl.multiple_of(r * CHUNK, CHUNK)
        m = xp[pl.ds(at, CHUNK), :].astype(F32)
        for j in range(blocks):
            m = m + dot(
                st[j, pl.ds(at + SEGS, CHUNK), :].astype(BF16), w_all[shards[j], pl.ds(o_out, ch), :]
            )
        mid[pl.ds(at, CHUNK), :] = m
        sv = m * scale_of(m) * g2_ref[...]
        lhs[pl.ds(at, CHUNK), :] = sv.astype(BF16)
        second_t[:, pl.ds(at, CHUNK)] = sv.T.astype(BF16)
        bufa[pl.ds(at, CHUNK), :] = m
        bufc[pl.ds(at, CHUNK), :] = jnp.zeros((CHUNK, d), F32)
        return 0

    lax.fori_loop(0, nchunk, second_rows, 0)

    act, din = dproj.at[1], dproj.at[2]

    def ff_block(j, _):
        s_ = zflip(j)

        @pl.when(j > 0)
        def _():
            w_wait(FF, j, 0)

        def ff_rows(r, _):
            at = pl.multiple_of(r * CHUNK, CHUNK)
            wu = w_all[s_, pl.ds(o_up, ff), :]
            wd = w_all[s_, pl.ds(o_down, ff), :]
            inner = dot(lhs[pl.ds(at, CHUNK), :], wu)
            da = dot_t(dout[pl.ds(at, CHUNK), :], wd)
            cdf = 0.5 + 0.5 * lax.erf(inner * np.float32(np.sqrt(0.5)))
            pdf = jnp.exp(inner * inner * -0.5) * np.float32(1.0 / np.sqrt(2.0 * np.pi))
            av = (inner * cdf).astype(BF16)
            dv = (da * (cdf + inner * pdf)).astype(BF16)
            act[pl.ds(at, CHUNK), :] = av
            din[pl.ds(at, CHUNK), :] = dv
            bufa[pl.ds(at, CHUNK), :] += dot(av, wd)
            bufc[pl.ds(at, CHUNK), :] += dot_t(dv, wu)

            @pl.when((r == 0) & (j == 0))
            def _():
                w_end(FF, 2)
                w_mid(FF, 3)

            @pl.when((r == 0) & (j == 1))
            def _():
                w_end(FF, 3)

            @pl.when((r == 2) & (j > 0))
            def _():
                r_first(FF, j - 1)

            @pl.when((r == 3) & (j > 1))
            def _():
                r_middle(FF, j - 2)

            @pl.when((r == 3) & (j > 2))
            def _():
                r_last(FF, j - 3)

            return 0

        lax.fori_loop(0, nchunk, ff_rows, 0)

        def ff_grads(r, _):
            at = pl.multiple_of(r * CHUNK, CHUNK)
            grad[s_, pl.ds(o_up + at, CHUNK), :] = dot(second_t[pl.ds(at, CHUNK), :], din[...]).astype(BF16)
            grad[s_, pl.ds(o_down + at, CHUNK), :] = dot(dout_t[pl.ds(at, CHUNK), :], act[...]).astype(BF16)
            return 0

        lax.fori_loop(0, d // CHUNK, ff_grads, 0)
        r_start(FF, j, 0)
        return 0

    lax.fori_loop(0, blocks, ff_block, 0)

    def second_back(r, gain):
        at = pl.multiple_of(r * CHUNK, CHUNK)
        put_perm(at, bufa[pl.ds(at, CHUNK), :])
        m = mid[pl.ds(at, CHUNK), :]
        s = scale_of(m)
        dn = bufc[pl.ds(at, CHUNK), :]
        gain = gain + jnp.sum(dn * m * s, axis=0, keepdims=True)
        gd = dn * g2_ref[...]
        dm = dout[pl.ds(at, CHUNK), :].astype(F32) + s * gd - m * (s * s * s * jnp.mean(gd * m, axis=-1, keepdims=True))
        mid[pl.ds(at, CHUNK), :] = dm
        lhs[pl.ds(at, CHUNK), :] = dm.astype(BF16)
        second_t[:, pl.ds(at, CHUNK)] = dm.T.astype(BF16)
        bufc[pl.ds(at, CHUNK), :] = jnp.zeros((CHUNK, d), F32)
        return gain

    gain2 = lax.fori_loop(0, nchunk, second_back, jnp.zeros((1, d), F32))
    ssum[0] = jnp.zeros((16, d), F32)
    ssum[0, pl.ds(1, 1), :] = gain2
    gather(dproj.at[0])
    res_copy = pltpu.make_async_copy(dproj.at[0], res_hbm, lsem.at[6])
    res_copy.start()
    r_middle(FF, 2)
    r_first(FF, 3)
    r_last(FF, 1)

    def backward_block(i, _):
        j = blocks - 1 - i
        s_ = zflip(j)

        def project(r, _):
            at = pl.multiple_of(r * CHUNK, CHUNK)
            dst[j, pl.ds(at, CHUNK), :] = dot_t(lhs[pl.ds(at, CHUNK), :], w_all[s_, pl.ds(o_out, ch), :])
            return 0

        lax.fori_loop(0, nchunk, project, 0)
        for half in range(2):
            rr = d // 2
            grad[s_, pl.ds(o_out, ch), half * ch : (half + 1) * ch] = dot(
                second_t[half * rr : (half + 1) * rr, :], st[j, pl.ds(SEGS, rows), :].astype(BF16)
            ).astype(BF16)
        r_start(OUT, j, 0)

        def one(step, w, q_):
            at = pl.multiple_of(step * SEGS, SEGS)
            a = 1.0 - upd[j, pl.ds(at, SEGS), :]
            c = dst[j, pl.ds(at, SEGS), :] + w
            return c, a * c, q_ * a

        w, q_ = jnp.zeros((SEGS, ch), F32), jnp.ones((SEGS, ch), F32)
        for step in range(steps - 1, steps - 6, -1):
            _, w, q_ = one(step, w, q_)

        def step8(n, carry):
            w, q_ = carry
            for q in range(8):
                _, w, q_ = one(steps - 6 - (n * 8 + q), w, q_)
            return w, q_

        w, q_ = lax.fori_loop(0, (steps - 8) // 8, step8, (w, q_))
        for step in range(2, -1, -1):
            bends[2 * step, j] = q_
            c, w, q_ = one(step, w, q_)
            bends[2 * step + 1, j] = c
        bends[6, j] = w
        bends[7, j] = q_
        bsend[j, pl.ds(0, 1), :] = backward_chain(j, jnp.zeros((1, ch), F32))
        for step in range(3):
            bsend[j, pl.ds(step + 1, 1), :] = upd[j, pl.ds(step * SEGS, 1), :] * (
                bends[2 * step + 1, j, pl.ds(0, 1), :]
                + bends[2 * step, j, pl.ds(0, 1), :] * ends[0, j, pl.ds(0, 1), :]
            )
        pl.when(t == 3)(b_copy(j).start)

        @pl.when(i == 1)
        def _():
            r_last(FF, 2)

        @pl.when(i == 2)
        def _():
            r_middle(FF, 3)

        @pl.when(i > 0)
        def _():
            r_first(OUT, j + 1)

        @pl.when(i > 1)
        def _():
            r_middle(OUT, j + 2)

        @pl.when(i > 2)
        def _():
            r_last(OUT, j + 3)

        return 0

    def backward_chain(j, start):
        run = start
        for seg in range(SEGS - 1, -1, -1):
            ends[0, j, pl.ds(seg, 1), :] = run
            run = bends[6, j, pl.ds(seg, 1), :] + bends[7, j, pl.ds(seg, 1), :] * run
        return run

    def b_copy(j):
        there = flip(j, 0)
        return remote(bsend.at[j], brecv.at[there], b_s.at[0], b_r.at[there], tensor=partner)

    lax.fori_loop(0, blocks, backward_block, 0)

    r_last(FF, 3)
    res_copy.wait()

    def backward_fix(i, _):
        j = blocks - 1 - i
        s_ = zflip(j)

        @pl.when(t == 2)
        def _():
            wait_for(brecv.at[j], b_r.at[j])

        backward_chain(j, brecv[j, pl.ds(0, 1), :] * has_next)
        w = ends[0, j]
        after = []
        for step in range(3):
            df = upd[j, pl.ds(step * SEGS, SEGS), :] * (bends[2 * step + 1, j] + bends[2 * step, j] * w)
            edge = brecv[j, pl.ds(step + 1, 1), :] * has_next
            after.append(jnp.where(seg_id == SEGS - 1, edge, pltpu.roll(df, SEGS - 1, 0)))
        k_ = [jnp.broadcast_to(cb[j, pl.ds(n, 1), :], (SEGS, ch)) for n in range(4)]
        zero = jnp.zeros((SEGS, ch), F32)

        def pair(n, carry):
            w, d1, d2, d3, c0, c1, c2, k0, k1, k2, k3, gb = carry
            top = steps - 2 - 2 * n
            made = []
            for q in range(2):
                at = pl.multiple_of((top + 1 - q) * SEGS, SEGS)
                u = upd[j, pl.ds(at, SEGS), :]
                c = dst[j, pl.ds(at, SEGS), :] + w
                d0 = c * u
                a = 1.0 - u
                w = a * c
                c3 = cand[j, pl.ds(at, SEGS), :]
                f = k_[0] * c0 + k_[1] * c1 + k_[2] * c2 + k_[3] * c3
                dg = d0 * a * (f - st[j, pl.ds(at, SEGS), :])
                dc = k_[0] * d0 + k_[1] * d1 + k_[2] * d2 + k_[3] * d3
                k0, k1, k2, k3 = k0 + d0 * c0, k1 + d0 * c1, k2 + d0 * c2, k3 + d0 * c3
                gb = gb + dg
                c0, c1, c2 = c1, c2, c3
                d1, d2, d3 = d0, d1, d2
                made.append((dg, dc))
            at = pl.multiple_of(top * SEGS, 2 * SEGS)
            dproj[j, pl.ds(at, 2 * SEGS), :ch] = jnp.concatenate([made[1][0], made[0][0]], axis=0).astype(BF16)
            dproj[j, pl.ds(at, 2 * SEGS), ch:] = jnp.concatenate([made[1][1], made[0][1]], axis=0).astype(BF16)
            return w, d1, d2, d3, c0, c1, c2, k0, k1, k2, k3, gb

        window = [cand[j, pl.ds((steps + 2 - n) * SEGS, SEGS), :] for n in range(3)]
        out = lax.fori_loop(0, steps // 2, pair, (w, *after, *window, zero, zero, zero, zero, zero))
        for n in range(5):
            at = 2 + 2 * n + bit_of(s_, 1)
            ssum[0, pl.ds(at, 1), pl.ds(pl.multiple_of(bit_of(s_, 0) * ch, LANES), ch)] = jnp.sum(
                out[7 + n], axis=0, keepdims=True
            )

        @pl.when(i == 0)
        def _():
            r_first(OUT, 0)
            r_middle(OUT, 1)
            r_last(OUT, 2)

        @pl.when(i == 1)
        def _():
            r_middle(OUT, 0)
            r_last(OUT, 1)

        @pl.when(i == 2)
        def _():
            r_last(OUT, 0)

        def first_grad(r, _):
            at = pl.multiple_of(r * CHUNK, CHUNK)
            grad[s_, pl.ds(o_in + at, CHUNK), :] = dot(first_t[pl.ds(at, CHUNK), :], dproj[j]).astype(BF16)
            return 0

        lax.fori_loop(0, d // CHUNK, first_grad, 0)
        r_start(IN, j, 0)


        @pl.when(i > 0)
        def _():
            r_first(IN, j + 1)

        @pl.when(i > 1)
        def _():
            r_middle(IN, j + 2)

        @pl.when(i > 2)
        def _():
            r_last(IN, j + 3)

        @pl.when(i == 2)
        def _():
            a_first(FF)

        @pl.when(i == 3)
        def _():
            a_mid(FF)
            a_first(OUT)

        return 0

    lax.fori_loop(0, blocks, backward_fix, 0)

    def first_back(r):
        at = r * CHUNK
        v = dot_t(dproj[0, pl.ds(at, CHUNK), :], w_all[shards[0], pl.ds(o_in, d), :])
        for j in range(1, blocks):
            v = v + dot_t(dproj[j, pl.ds(at, CHUNK), :], w_all[shards[j], pl.ds(o_in, d), :])
        bufc[pl.ds(at, CHUNK), :] = v

    first_back(0)
    r_last(IN, 2)
    first_back(1)
    r_first(IN, 0)
    r_middle(IN, 1)
    a_end(FF)
    first_back(2)
    a_mid(OUT)
    first_back(3)
    for r in range(4, nchunk):
        first_back(r)

    def first_norm_back(r, gain):
        at = pl.multiple_of(r * CHUNK, CHUNK)
        m = xp[pl.ds(at, CHUNK), :].astype(F32)
        s = scale_of(m)
        dn = bufc[pl.ds(at, CHUNK), :]
        gain = gain + jnp.sum(dn * m * s, axis=0, keepdims=True)
        gd = dn * g1_ref[...]
        dv = s * gd - m * (s * s * s * jnp.mean(gd * m, axis=-1, keepdims=True))
        put_perm(at, mid[pl.ds(at, CHUNK), :] + dv)
        return gain

    ssum[0, pl.ds(0, 1), :] = lax.fori_loop(0, nchunk, first_norm_back, jnp.zeros((1, d), F32))
    s_start(0)
    r_middle(IN, 0)
    r_last(IN, 1)
    gather(mid)
    gx_copy = pltpu.make_async_copy(mid, gx_hbm, lsem.at[7])
    gx_copy.start()
    a_end(OUT)
    s_next(0)
    r_last(IN, 0)
    a_first(IN)
    for g in range(1, len(groups) - 1):
        s_next(g)
    a_mid(IN)
    a_end(IN)
    s_next(len(groups) - 1)
    gains_ref[...] = ssum[len(groups), pl.ds(0, 8), :]
    for n in range(5):
        at = 2 + 2 * n + bit_of(t, 1)
        chan_ref[pl.ds(n, 1), :] = ssum[
            len(groups), pl.ds(at, 1), pl.ds(pl.multiple_of(bit_of(t, 0) * ch, LANES), ch)
        ]
    a_wait(FF, 0)
    a_wait(OUT, 0)
    a_wait(IN, 0)

    gx_copy.wait()
    wait_for(cb.at[pl.ds(0, blocks - 1)], c_s.at[0])
    pl.when(t == 2)(lambda: wait_for(fsend, f_s.at[0]))
    pl.when(t == 3)(lambda: wait_for(bsend, b_s.at[0]))
    for kind in (IN, OUT, FF):
        for k in range(halves[kind]):
            n = span(kind, k + 1)
            wait_for(w_all.at[0, pl.ds(0, (blocks - 1) * n), :], w_s.at[kind, k])
            wait_for(grad.at[pl.ds(0, 2), pl.ds(0, blocks // 2 * n), :], r_s.at[kind, k])
            wait_for(fin.at[pl.ds(0, n), :], a_s.at[kind, k])
        n = span(kind, nb)
        wait_for(w_all.at[0, pl.ds(0, (blocks - 1) * n), :], w_s.at[kind, nb])
        wait_for(w_all.at[0, pl.ds(0, (blocks - 1) * n), :], r_s.at[kind, nb])
    for g in range(len(groups)):
        wait_for(sgot.at[g, pl.ds(0, (1 << len(groups[g])) - 1)], s_s.at[g])


def finish_kernel(dims, gains, chan, res, gx, fin, res_out, gx_out, gin_o, gout_o, gup_o, gdown_o, gnorm, gmlp, taps, gbias,
                  rbuf, gbuf, fbuf, gin, gout, gup, gdown, sem):
    rows, d, ch, ff = dims
    cuts = ((d + ch, ff), (d + ch + ff, ff), (d, ch), (0, d))
    parts = [pltpu.make_async_copy(fin.at[pl.ds(a, n)], fbuf.at[pl.ds(a, n)], sem.at[i]) for i, (a, n) in enumerate(cuts)]
    ins = [pltpu.make_async_copy(gx, gbuf, sem.at[4]), pltpu.make_async_copy(res, rbuf, sem.at[5])]
    for copy in parts + ins:
        copy.start()
    outs = []

    def put(src, dst):
        copy = pltpu.make_async_copy(src, dst, sem.at[6 + len(outs)])
        copy.start()
        outs.append(copy)

    gnorm[...] = gains[pl.ds(0, 1), :]
    gmlp[...] = gains[pl.ds(1, 1), :]
    taps[...] = chan[pl.ds(0, 4), :]
    gbias[...] = chan[pl.ds(4, 1), :]
    parts[0].wait()
    gup[...] = fbuf[pl.ds(d + ch, d), :].astype(F32)
    put(gup, gup_o)
    parts[1].wait()
    gdown[...] = fbuf[pl.ds(d + ch + ff, d), :].astype(F32).T
    put(gdown, gdown_o)
    ins[0].wait()
    put(gbuf, gx_out)
    ins[1].wait()
    put(rbuf, res_out)
    parts[2].wait()
    gout[:, : d // 2] = fbuf[pl.ds(d, ch), :ch].astype(F32).T
    gout[:, d // 2 :] = fbuf[pl.ds(d, ch), ch:].astype(F32).T
    put(gout, gout_o)
    parts[3].wait()
    gin[:, 0, :] = fbuf[pl.ds(0, d), :ch].astype(F32)
    gin[:, 1, :] = fbuf[pl.ds(0, d), ch:].astype(F32)
    put(gin, gin_o)
    for copy in outs:
        copy.wait()


def per_device(
    inputs,
    norm_gain,
    in_weight,
    conv_kernel,
    gate_bias,
    out_weight,
    mlp_gain,
    up_weight,
    down_weight,
    short_lengths,
    long_lengths,
    cotangent,
):
    rows, d = inputs.shape
    ch = in_weight.shape[2]
    ff = up_weight.shape[1]
    blocks = lax.axis_size("tensor")
    dp = lax.axis_size("dp")
    nb = log2(dp)
    assert dp == 1 << nb and blocks == 4 and rows == LSHORT and 2 * rows == LLONG
    assert short_lengths.shape == (2,) and long_lengths.shape == (1,)
    sizes = (d, ch, 2 * ff)
    total = sum(sizes)
    halves = tuple(min(nb, log2(r // TILE)) for r in sizes)

    def span_all(k):
        return sum(r >> min(k, h) for r, h in zip(sizes, halves))

    ngroups = len(bit_groups(nb))
    vm = pl.BlockSpec(memory_space=pltpu.VMEM)
    sm = pl.BlockSpec(memory_space=pltpu.SMEM)
    hb = pl.BlockSpec(memory_space=pl.ANY)
    dma = pltpu.SemaphoreType.DMA
    res, gx, fin, gains, chan = pl.pallas_call(
        functools.partial(block_kernel, (rows, d, blocks, ch, ff, nb)),
        out_shape=(
            jax.ShapeDtypeStruct((rows, d), BF16),
            jax.ShapeDtypeStruct((rows, d), F32),
            jax.ShapeDtypeStruct((total, d), BF16),
            jax.ShapeDtypeStruct((8, d), F32),
            jax.ShapeDtypeStruct((8, ch), F32),
        ),
        in_specs=[sm, sm, hb, hb, vm, vm, vm, vm, hb, hb, hb, hb],
        out_specs=(hb, hb) + (vm,) * 3,
        scratch_shapes=[
            pltpu.VMEM((blocks, total, d), BF16),
            pltpu.VMEM((blocks, total, d), BF16),
            pltpu.VMEM((rows, d), BF16),
            pltpu.VMEM((blocks, rows + 3 * SEGS, ch), F32),
            pltpu.VMEM((blocks, rows, ch), F32),
            pltpu.VMEM((blocks, rows + SEGS, ch), F32),
            pltpu.VMEM((blocks, rows, ch), F32),
            pltpu.VMEM((rows + 16, d), BF16),
            pltpu.VMEM((d, rows), BF16),
            pltpu.VMEM((d, rows), BF16),
            pltpu.VMEM((rows, d), BF16),
            pltpu.VMEM((d, rows), BF16),
            pltpu.VMEM((rows, d), F32),
            pltpu.VMEM((rows, d), F32),
            pltpu.VMEM((rows, d), F32),
            pltpu.VMEM((blocks, rows, d), BF16),
            pltpu.VMEM((d // LANES, rows, LANES), F32),
            pltpu.VMEM((16, d), BF16),
            pltpu.VMEM((blocks, 8, ch), F32),
            pltpu.VMEM((2, blocks, SEGS, ch), F32),
            pltpu.VMEM((8, blocks, SEGS, ch), F32),
            pltpu.VMEM((blocks, 8, ch), F32),
            pltpu.VMEM((blocks, 8, ch), F32),
            pltpu.VMEM((blocks, 8, ch), F32),
            pltpu.VMEM((blocks, 8, ch), F32),
            pltpu.VMEM((blocks, span_all(nb), d), BF16),
            pltpu.VMEM((ngroups + 1, 16, d), F32),
            pltpu.VMEM((ngroups, 3, 16, d), F32),
            dma((8,)),
            dma((1,)),
            dma((blocks,)),
            dma((1,)),
            dma((blocks,)),
            dma((1,)),
            dma((blocks,)),
            dma((1,)),
            dma((1,)),
            dma((3, nb + 1)),
            dma((3, blocks, nb + 1)),
            dma((3, nb + 1)),
            dma((3, blocks, nb + 1)),
            dma((3, blocks, nb)),
            dma((3, nb)),
            dma((3, nb)),
            dma((ngroups,)),
            dma((ngroups, 3)),
        ]
        + [pltpu.VMEM((blocks, span_all(k + 1), d), BF16) for k in range(nb)],
        compiler_params=pltpu.CompilerParams(
            collective_id=0, has_side_effects=True, vmem_limit_bytes=67043328
        ),
        name="block",
    )(
        short_lengths,
        long_lengths,
        inputs,
        cotangent,
        norm_gain[None],
        mlp_gain[None],
        conv_kernel,
        gate_bias[None],
        in_weight.reshape(d, 2 * ch),
        out_weight,
        up_weight,
        down_weight,
    )
    result, grad_inputs, gin, gout, gup, gdown, gnorm, gmlp, taps, gbias = pl.pallas_call(
        functools.partial(finish_kernel, (rows, d, ch, ff)),
        out_shape=(
            jax.ShapeDtypeStruct((rows, d), BF16),
            jax.ShapeDtypeStruct((rows, d), F32),
            jax.ShapeDtypeStruct((d, 2, ch), F32),
            jax.ShapeDtypeStruct((ch, d), F32),
            jax.ShapeDtypeStruct((d, ff), F32),
            jax.ShapeDtypeStruct((ff, d), F32),
            jax.ShapeDtypeStruct((1, d), F32),
            jax.ShapeDtypeStruct((1, d), F32),
            jax.ShapeDtypeStruct((4, ch), F32),
            jax.ShapeDtypeStruct((1, ch), F32),
        ),
        in_specs=[vm, vm, hb, hb, hb],
        out_specs=(hb,) * 6 + (vm,) * 4,
        scratch_shapes=[
            pltpu.VMEM((rows, d), BF16),
            pltpu.VMEM((rows, d), F32),
            pltpu.VMEM((total, d), BF16),
            pltpu.VMEM((d, 2, ch), F32),
            pltpu.VMEM((ch, d), F32),
            pltpu.VMEM((d, ff), F32),
            pltpu.VMEM((ff, d), F32),
            dma((12,)),
        ],
        compiler_params=pltpu.CompilerParams(vmem_limit_bytes=67043328),
        name="finish",
    )(gains, chan, res, gx, fin)
    return (result, grad_inputs, gnorm[0], gin, taps, gbias[0], gout, gmlp[0], gup, gdown)


def solution(mesh):
    placed = (
        P(("dp", "tensor"), None),
        P(),
        P(None, None, "tensor"),
        P(None, "tensor"),
        P("tensor"),
        P("tensor", None),
        P(),
        P(None, "tensor"),
        P("tensor", None),
        P("dp"),
        P("dp"),
        P(("dp", "tensor"), None),
    )
    return jax.shard_map(
        per_device,
        mesh=mesh,
        in_specs=placed,
        out_specs=(
            P(("dp", "tensor"), None),
            P(("dp", "tensor"), None),
            P(),
            P(None, None, "tensor"),
            P(None, "tensor"),
            P("tensor"),
            P("tensor", None),
            P(),
            P(None, "tensor"),
            P("tensor", None),
        ),
        check_vma=False,
    )
```

```python
import functools

import jax
import jax.numpy as jnp
import numpy as np
from jax import lax
from jax.experimental import pallas as pl
from jax.experimental.pallas import tpu as pltpu
from jax.sharding import PartitionSpec as P

LSHORT = 1024
LLONG = 2048
SEGS = 8
EPS = 1e-05
CHUNK = 256
TILE = 16
LANES = 128
F32 = jnp.float32
BF16 = jnp.bfloat16
MESH = pl.DeviceIdType.MESH
IN, OUT, FF = 0, 1, 2


def dot(a, b):
    return jnp.dot(a, b, preferred_element_type=F32)


def dot_t(a, b):
    return lax.dot_general(a, b, (((1,), (1,)), ((), ())), preferred_element_type=F32)


def scale_of(v):
    return lax.rsqrt(jnp.mean(v * v, axis=-1, keepdims=True) + EPS)


def sigmoid(v):
    return 1.0 / (1.0 + jnp.exp(-v))


def bit_of(v, bit):
    return lax.rem(lax.div(v, 1 << bit), 2)


def flip(v, bit):
    return v + (1 << bit) * (1 - 2 * bit_of(v, bit))


def log2(n):
    return int(n).bit_length() - 1


def bit_groups(nb):
    groups = [(0,)] + [tuple(range(b, min(b + 2, nb))) for b in range(1, nb, 2)]
    return groups + [(nb, nb + 1)]


def block_kernel(
    dims,
    short_ref,
    long_ref,
    x_hbm,
    cot_hbm,
    g1_ref,
    g2_ref,
    conv_ref,
    bias_ref,
    win_hbm,
    wout_hbm,
    wup_hbm,
    wdown_hbm,
    res_hbm,
    gx_hbm,
    fin,
    gains_ref,
    chan_ref,
    w_all,
    grad,
    xp,
    cand,
    upd,
    st,
    dst,
    lhs,
    first_t,
    second_t,
    dout,
    dout_t,
    bufa,
    mid,
    bufc,
    dproj,
    perm,
    halo,
    cb,
    ends,
    bends,
    fsend,
    frecv,
    bsend,
    brecv,
    zbuf,
    ssum,
    sgot,
    lsem,
    c_s,
    c_r,
    f_s,
    f_r,
    b_s,
    b_r,
    h_s,
    h_r,
    w_s,
    w_r,
    r_s,
    r_r,
    x_s,
    a_s,
    a_r,
    s_s,
    s_r,
    *stage_bufs,
):
    rows, d, blocks, ch, ff, nb = dims
    steps = rows // SEGS
    t = lax.axis_index("tensor")
    p = lax.axis_index("dp")
    partner = flip(t, 0)
    nchunk = rows // CHUNK
    offs = (0, d, d + ch)
    sizes = (d, ch, 2 * ff)
    o_in, o_out, o_up, o_down = 0, d, d + ch, d + ch + ff
    halves = tuple(min(nb, log2(r // TILE)) for r in sizes)
    half_d = d // 2
    lanes = (pl.ds(0, half_d), pl.ds(half_d, half_d))
    orders = ((0,) + tuple(range(nb - 1, 0, -1)), tuple(range(nb)))
    nstage = len(stage_bufs)

    def zflip(j):
        b0, b1 = lax.rem(j, 2), lax.div(j, 2)
        return t + b0 * (1 - 2 * bit_of(t, 0)) + b1 * (2 - 4 * bit_of(t, 1))

    def low_of(kind, c, k):
        low = 0
        for i in range(min(k, halves[kind])):
            low = low + bit_of(p, orders[c][i]) * (sizes[kind] >> (i + 1))
        return low

    def span(kind, k):
        return sizes[kind] >> min(k, halves[kind])

    def at_rows(kind, start, n):
        return pl.ds(pl.multiple_of(offs[kind] + start, TILE), n)

    def stage_rows(kind, k):
        base = sum(span(i, k + 1) for i in range(kind))
        return pl.ds(base, span(kind, k + 1))

    def remote(src, dst_, ss, rs, **dev):
        return pltpu.make_async_remote_copy(
            src_ref=src, dst_ref=dst_, send_sem=ss, recv_sem=rs, device_id=dev, device_id_type=MESH
        )

    def wait_for(ref, sem):
        pltpu.make_async_copy(ref, ref, sem).wait()

    def w_step(kind, j, k):
        made = []
        for c in range(1 if k == 0 else 2):
            at = at_rows(kind, low_of(kind, c, k + 1), span(kind, k + 1))
            ref = w_all.at[zflip(j), at, slice(None) if k == 0 else lanes[c]]
            made.append(remote(ref, ref, w_s.at[kind, k], w_r.at[kind, j, k], dp=flip(p, orders[c][k])))
        return made

    def w_sources(kind, j):
        made = []
        for c in range(2):
            ref = w_all.at[t, at_rows(kind, low_of(kind, c, nb), span(kind, nb)), lanes[c]]
            made.append(remote(ref, ref, w_s.at[kind, nb], w_r.at[kind, j, nb], tensor=zflip(j)))
        return made

    def w_wait(kind, j, k):
        k_ = nb if k == halves[kind] else k
        wait_for(w_all.at[0, pl.ds(0, span(kind, k + 1))], w_r.at[kind, j, k_])

    def w_forward(kind, j, k):
        w_wait(kind, j, k + 1)
        for copy in w_step(kind, j, k):
            copy.start()

    def w_top(kind, *js):
        for j in js:
            w_forward(kind, j, halves[kind] - 1)

    def w_mid(kind, *js):
        for k in range(halves[kind] - 2, 0, -1):
            for j in js:
                w_forward(kind, j, k)

    def w_end(kind, *js):
        for j in js:
            w_forward(kind, j, 0)

    def r_step(kind, j, k):
        s = zflip(j)
        base = sum(span(i, k + 1) for i in range(kind))
        made = []
        for c in range(1 if k == 0 else 2):
            low = low_of(kind, c, k)
            if k < halves[kind]:
                low = low + (1 - bit_of(p, orders[c][k])) * span(kind, k + 1)
            which = slice(None) if k == 0 else lanes[c]
            made.append(
                remote(
                    grad.at[s, at_rows(kind, low, span(kind, k + 1)), which],
                    stage_bufs[k].at[j, pl.ds(base, span(kind, k + 1)), which],
                    r_s.at[kind, k] if k < halves[kind] else x_s.at[kind, j, k],
                    r_r.at[kind, j, k],
                    dp=flip(p, orders[c][k]),
                )
            )
        return made

    def r_start(kind, j, k):
        for copy in r_step(kind, j, k):
            copy.start()

    def r_finish(kind, j, k):
        s = zflip(j)
        buf = stage_bufs[k]
        base = sum(span(i, k + 1) for i in range(kind))
        n = span(kind, k + 1)
        here = stage_bufs[k].at[j, pl.ds(base, n), :]
        if k >= halves[kind]:
            wait_for(here, x_s.at[kind, j, k])
        wait_for(here, r_r.at[kind, j, k])
        piece = min(n, 128)
        for c in range(2):
            low = low_of(kind, c, k + 1)

            def add(i, _):
                at = at_rows(kind, low + i * piece, piece)
                here = pl.ds(pl.multiple_of(base + i * piece, TILE), piece)
                grad[s, at, lanes[c]] = (
                    grad[s, at, lanes[c]].astype(F32) + buf[j, here, lanes[c]].astype(F32)
                ).astype(BF16)
                return 0

            lax.fori_loop(0, n // piece, add, 0)

    def r_z(kind, j):
        s = zflip(j)
        base = sum(span(i, nb) for i in range(kind))
        made = []
        for c in range(2):
            at = at_rows(kind, low_of(kind, c, nb), span(kind, nb))
            made.append(
                remote(
                    grad.at[s, at, lanes[c]],
                    zbuf.at[j, pl.ds(base, span(kind, nb)), lanes[c]],
                    r_s.at[kind, nb],
                    r_r.at[kind, j, nb],
                    tensor=s,
                )
            )
        return made

    def r_out(kind, j):
        for copy in r_z(kind, j):
            copy.start()

    def r_total(kind):
        base = sum(span(i, nb) for i in range(kind))
        n = span(kind, nb)
        for j in range(1, blocks):
            wait_for(zbuf.at[j, pl.ds(base, n), :], r_r.at[kind, j, nb])
        for c in range(2):
            at = at_rows(kind, low_of(kind, c, nb), n)
            total = grad[t, at, lanes[c]].astype(F32)
            for j in range(1, blocks):
                total = total + zbuf[j, pl.ds(base, n), lanes[c]].astype(F32)
            fin[at, lanes[c]] = total.astype(BF16)

    def a_step(kind, k):
        made = []
        for c in range(1 if k == 0 else 2):
            at = at_rows(kind, low_of(kind, c, k + 1), span(kind, k + 1))
            ref = fin.at[at, slice(None) if k == 0 else lanes[c]]
            made.append(remote(ref, ref, a_s.at[kind, k], a_r.at[kind, k], dp=flip(p, orders[c][k])))
        return made

    def a_start(kind, k):
        for copy in a_step(kind, k):
            copy.start()

    def a_wait(kind, k):
        wait_for(fin.at[pl.ds(0, span(kind, k + 1)), :], a_r.at[kind, k])

    def r_middle(kind, j):
        for k in range(1, nb - 1):
            r_finish(kind, j, k)
            r_start(kind, j, k + 1)

    def r_first(kind, j):
        r_finish(kind, j, 0)
        r_start(kind, j, 1)

    def r_last(kind, j):
        r_finish(kind, j, nb - 1)
        if isinstance(j, int):
            if j > 0:
                r_out(kind, j)
        else:
            pl.when(j > 0)(lambda: r_out(kind, j))

    def a_first(kind):
        r_total(kind)
        a_start(kind, halves[kind] - 1)

    def a_mid(kind):
        for k in range(halves[kind] - 2, 0, -1):
            a_wait(kind, k + 1)
            a_start(kind, k)

    def a_end(kind):
        a_wait(kind, 1)
        a_start(kind, 0)

    groups = bit_groups(nb)

    def s_start(g):
        bits = groups[g]
        for r in range(1, 1 << len(bits)):
            dp_, tensor_ = p, t
            for i, b in enumerate(bits):
                if r >> i & 1:
                    dp_, tensor_ = (flip(dp_, b), tensor_) if b < nb else (dp_, flip(tensor_, b - nb))
            dev = {"dp": dp_} if bits[0] < nb else {"tensor": tensor_}
            remote(ssum.at[g], sgot.at[g, r - 1], s_s.at[g], s_r.at[g, r - 1], **dev).start()

    def s_next(g):
        n = (1 << len(groups[g])) - 1
        for r in range(n):
            wait_for(sgot.at[g, r], s_r.at[g, r])
        v = ssum[g] + sgot[g, 0]
        if n == 3:
            v = v + (sgot[g, 1] + sgot[g, 2])
        ssum[g + 1] = v
        if g + 1 < len(groups):
            s_start(g + 1)

    def local(src, dst_, i):
        return pltpu.make_async_copy(src, dst_, lsem.at[i])

    loads = [
        local(win_hbm, w_all.at[t, pl.ds(o_in, d), :], 0),
        local(x_hbm, dproj.at[0], 1),
        local(cot_hbm, dproj.at[1], 2),
        local(wout_hbm, w_all.at[t, pl.ds(o_out, ch), :], 3),
        local(wup_hbm, w_all.at[t, pl.ds(o_up, ff), :], 4),
        local(wdown_hbm, w_all.at[t, pl.ds(o_down, ff), :], 5),
    ]
    for copy in loads:
        copy.start()
    frecv[...] = jnp.zeros_like(frecv)
    brecv[...] = jnp.zeros_like(brecv)
    halo[...] = jnp.zeros_like(halo)
    cb[0, pl.ds(0, 4), :] = conv_ref[...]
    cb[0, pl.ds(4, 1), :] = bias_ref[...]
    barrier = pltpu.get_barrier_semaphore()
    for b in range(nb):
        pl.semaphore_signal(barrier, inc=1, device_id={"dp": flip(p, b)}, device_id_type=MESH)
    for j in range(1, blocks):
        pl.semaphore_signal(barrier, inc=1, device_id={"tensor": zflip(j)}, device_id_type=MESH)
    pl.semaphore_wait(barrier, nb + blocks - 1)

    def c_copy(j):
        return remote(cb.at[0], cb.at[j], c_s.at[0], c_r.at[j], tensor=zflip(j))

    hcopy = remote(x_hbm.at[pl.ds(rows - 16, 16), :], halo, h_s.at[0], h_r.at[0], tensor=partner)
    pl.when(t == 2)(hcopy.start)
    for j in range(1, blocks):
        c_copy(j).start()
    loads[0].wait()
    for j in range(1, blocks):
        for copy in w_sources(IN, j):
            copy.start()
    loads[1].wait()

    nlane = d // LANES

    def spread(ref):
        for seg in range(SEGS):
            v = ref[pl.ds(seg * steps, steps), :].astype(F32)
            for i in range(nlane):
                perm[i, pl.ds(seg, steps, stride=SEGS), :] = v[:, i * LANES : (i + 1) * LANES]

    def gather(ref):
        for seg in range(SEGS):
            for i in range(nlane):
                v = perm[i, pl.ds(seg, steps, stride=SEGS), :]
                ref[pl.ds(seg * steps, steps), i * LANES : (i + 1) * LANES] = v.astype(ref.dtype)

    def perm_rows(at):
        return jnp.concatenate([perm[i, pl.ds(at, CHUNK), :] for i in range(nlane)], axis=1)

    def put_perm(at, v):
        for i in range(nlane):
            perm[i, pl.ds(at, CHUNK), :] = v[:, i * LANES : (i + 1) * LANES]

    spread(dproj.at[0])
    limit = jnp.where(
        t == 0,
        short_ref[0],
        jnp.where(t == 1, short_ref[1], jnp.where(t == 2, long_ref[0], long_ref[0] - rows)),
    )

    def norm_rows(r, _):
        at = pl.multiple_of(r * CHUNK, CHUNK)
        xv = perm_rows(at)
        xp[pl.ds(at, CHUNK), :] = xv.astype(BF16)
        fv = xv * scale_of(xv) * g1_ref[...]
        lhs[pl.ds(at, CHUNK), :] = fv.astype(BF16)
        first_t[:, pl.ds(at, CHUNK)] = fv.T.astype(BF16)
        return 0

    lax.fori_loop(0, nchunk, norm_rows, 0)
    loads[2].wait()
    spread(dproj.at[1])

    def dout_rows(r, _):
        at = pl.multiple_of(r * CHUNK, CHUNK)
        place = at + lax.broadcasted_iota(jnp.int32, (CHUNK, d), 0)
        pos = lax.rem(place, SEGS) * steps + place // SEGS
        dv = jnp.where(pos < limit, perm_rows(at), 0.0)
        dout[pl.ds(at, CHUNK), :] = dv.astype(BF16)
        dout_t[:, pl.ds(at, CHUNK)] = dv.T.astype(BF16)
        return 0

    lax.fori_loop(0, nchunk, dout_rows, 0)
    seg_id = lax.broadcasted_iota(jnp.int32, (SEGS, ch), 0)
    has_prev = jnp.where(t == 3, 1.0, 0.0).astype(F32)
    has_next = jnp.where(t == 2, 1.0, 0.0).astype(F32)

    def forward_block(j, _):
        s_ = zflip(j)

        @pl.when(j == 1)
        def _():
            w_top(IN, 3)
            w_mid(IN, 2)
            w_end(IN, 1)
            w_mid(IN, 3)

        @pl.when(j > 0)
        def _():
            c_copy(j).wait_recv()
            w_wait(IN, j, 0)

        def project(r, _):
            at = pl.multiple_of(r * CHUNK, CHUNK)
            v = dot(lhs[pl.ds(at, CHUNK), :], w_all[s_, pl.ds(o_in, d), :])
            bufa[pl.ds(at, CHUNK), :ch] = v[:, :ch]
            cand[j, pl.ds(at + 3 * SEGS, CHUNK), :] = v[:, ch:]

            @pl.when((j == 0) & (r == 1))
            def _():
                w_top(IN, 1)

            return 0

        lax.fori_loop(0, nchunk, project, 0)

        @pl.when(j == 0)
        def _():
            pl.when(t == 3)(hcopy.wait_recv)
            hv = halo[...].astype(F32)
            lhs[pl.ds(rows, 16), :] = (hv * scale_of(hv) * g1_ref[...]).astype(BF16)

        @pl.when(j == 1)
        def _():
            w_end(IN, 2)

        @pl.when(j == 2)
        def _():
            w_end(IN, 3)

        @pl.when(j == 3)
        def _():
            w_top(FF, 2)

        ph = dot(lhs[pl.ds(rows, 16), :], w_all[s_, pl.ds(o_in, d), ch:])
        for back in range(3):
            last = cand[j, pl.ds((steps + back) * SEGS, SEGS), :]
            rolled = pltpu.roll(last, 1, 0)
            edge = ph[13 + back : 14 + back, :] * has_prev
            cand[j, pl.ds(back * SEGS, SEGS), :] = jnp.where(seg_id == 0, edge, rolled)
        k_ = [jnp.broadcast_to(cb[j, pl.ds(i, 1), :], (SEGS, ch)) for i in range(4)]
        bias = jnp.broadcast_to(cb[j, pl.ds(4, 1), :], (SEGS, ch))

        def step4(i, carry):
            s, q_ = carry
            for q in range(4):
                at = pl.multiple_of((i * 4 + q) * SEGS, SEGS)
                u = sigmoid(bufa[pl.ds(at, SEGS), :ch] + bias)
                f = k_[0] * cand[j, pl.ds(at + 3 * SEGS, SEGS), :]
                for lag in range(1, 4):
                    f = f + k_[lag] * cand[j, pl.ds(at + (3 - lag) * SEGS, SEGS), :]
                upd[j, pl.ds(at, SEGS), :] = u
                dst[j, pl.ds(at, SEGS), :] = f
                a = 1.0 - u
                s = a * s + u * f
                q_ = a * q_
            return s, q_

        half = lax.fori_loop(
            0, steps // 8, step4, (jnp.zeros((SEGS, ch), F32), jnp.ones((SEGS, ch), F32))
        )

        @pl.when(j == 0)
        def _():
            w_top(IN, 2)

        s, q_ = lax.fori_loop(steps // 8, steps // 4, step4, half)
        ends[0, j] = s
        ends[1, j] = q_
        fsend[j] = jnp.broadcast_to(forward_chain(j, jnp.zeros((1, ch), F32)), (8, ch))
        pl.when(t == 2)(f_copy(j).start)

        @pl.when(j == 0)
        def _():
            w_mid(IN, 1)
            for i in range(3, 6):
                loads[i].wait()
            for kind in (OUT, FF):
                for i in (2, 3, 1):
                    for copy in w_sources(kind, i):
                        copy.start()

        @pl.when(j == 1)
        def _():
            w_top(OUT, 1, 2, 3)

        @pl.when(j == 2)
        def _():
            w_mid(OUT, 1, 2, 3)

        return 0

    def forward_chain(j, start):
        run = start
        for seg in range(SEGS):
            st[j, pl.ds(seg, 1), :] = run
            run = ends[0, j, pl.ds(seg, 1), :] + ends[1, j, pl.ds(seg, 1), :] * run
        return run

    def f_copy(j):
        there = flip(j, 0)
        return remote(fsend.at[j], frecv.at[there], f_s.at[0], f_r.at[there], tensor=partner)

    lax.fori_loop(0, blocks, forward_block, 0)
    w_top(FF, 3)

    def forward_fix(i, _):
        b = flip(i, 0)

        @pl.when(t == 3)
        def _():
            wait_for(frecv.at[b], f_r.at[b])

        forward_chain(b, frecv[b, pl.ds(0, 1), :] * has_prev)

        def step8(i, s):
            for q in range(8):
                at = pl.multiple_of((i * 8 + q) * SEGS, SEGS)
                u = upd[b, pl.ds(at, SEGS), :]
                s = (1.0 - u) * s + u * dst[b, pl.ds(at, SEGS), :]
                st[b, pl.ds(at + SEGS, SEGS), :] = s
            return s

        lax.fori_loop(0, steps // 8, step8, st[b, pl.ds(0, SEGS), :])

        @pl.when(i == 0)
        def _():
            w_end(OUT, 1, 2, 3)

        return 0

    lax.fori_loop(0, blocks, forward_fix, 0)
    w_mid(FF, 2)
    for j in range(1, blocks):
        w_wait(OUT, j, 0)
    shards = [zflip(j) for j in range(blocks)]

    def second_rows(r, _):
        at = pl.multiple_of(r * CHUNK, CHUNK)
        m = xp[pl.ds(at, CHUNK), :].astype(F32)
        for j in range(blocks):
            m = m + dot(
                st[j, pl.ds(at + SEGS, CHUNK), :].astype(BF16), w_all[shards[j], pl.ds(o_out, ch), :]
            )
        mid[pl.ds(at, CHUNK), :] = m
        sv = m * scale_of(m) * g2_ref[...]
        lhs[pl.ds(at, CHUNK), :] = sv.astype(BF16)
        second_t[:, pl.ds(at, CHUNK)] = sv.T.astype(BF16)
        bufa[pl.ds(at, CHUNK), :] = m
        bufc[pl.ds(at, CHUNK), :] = jnp.zeros((CHUNK, d), F32)
        return 0

    lax.fori_loop(0, nchunk, second_rows, 0)

    w_mid(FF, 3)
    act, din = dproj.at[1], dproj.at[2]

    def ff_place(i):
        return lax.div(i + 3, 4) * (1 + lax.rem(i, 3))

    def ff_block(i, _):
        j, before, earlier = ff_place(i), ff_place(i - 1), ff_place(i - 2)
        s_ = zflip(j)

        @pl.when(i > 0)
        def _():
            w_wait(FF, j, 0)

        def ff_rows(r, _):
            at = pl.multiple_of(r * CHUNK, CHUNK)
            wu = w_all[s_, pl.ds(o_up, ff), :]
            wd = w_all[s_, pl.ds(o_down, ff), :]
            inner = dot(lhs[pl.ds(at, CHUNK), :], wu)
            da = dot_t(dout[pl.ds(at, CHUNK), :], wd)
            cdf = 0.5 + 0.5 * lax.erf(inner * np.float32(np.sqrt(0.5)))
            pdf = jnp.exp(inner * inner * -0.5) * np.float32(1.0 / np.sqrt(2.0 * np.pi))
            av = (inner * cdf).astype(BF16)
            dv = (da * (cdf + inner * pdf)).astype(BF16)
            act[pl.ds(at, CHUNK), :] = av
            din[pl.ds(at, CHUNK), :] = dv
            bufa[pl.ds(at, CHUNK), :] += dot(av, wd)
            bufc[pl.ds(at, CHUNK), :] += dot_t(dv, wu)

            @pl.when((r == 1) & (i == 0))
            def _():
                w_end(FF, 2)

            @pl.when((r == 2) & (i == 0))
            def _():
                w_top(FF, 1)

            @pl.when((r == 3) & (i == 0))
            def _():
                w_end(FF, 3)

            @pl.when((r == 0) & (i == 1))
            def _():
                w_mid(FF, 1)

            @pl.when((r == 1) & (i == 2))
            def _():
                w_end(FF, 1)

            @pl.when((r == 3) & (i > 1))
            def _():
                r_middle(FF, earlier)

            @pl.when((r == 3) & (i > 0))
            def _():
                r_first(FF, before)

            return 0

        lax.fori_loop(0, nchunk, ff_rows, 0)

        def ff_grads(r, _):
            at = pl.multiple_of(r * CHUNK, CHUNK)
            grad[s_, pl.ds(o_up + at, CHUNK), :] = dot(second_t[pl.ds(at, CHUNK), :], din[...]).astype(BF16)
            grad[s_, pl.ds(o_down + at, CHUNK), :] = dot(dout_t[pl.ds(at, CHUNK), :], act[...]).astype(BF16)
            return 0

        lax.fori_loop(0, d // CHUNK, ff_grads, 0)
        r_start(FF, j, 0)
        return 0

    lax.fori_loop(0, blocks, ff_block, 0)

    def second_back(r, gain):
        at = pl.multiple_of(r * CHUNK, CHUNK)
        put_perm(at, bufa[pl.ds(at, CHUNK), :])
        m = mid[pl.ds(at, CHUNK), :]
        s = scale_of(m)
        dn = bufc[pl.ds(at, CHUNK), :]
        gain = gain + jnp.sum(dn * m * s, axis=0, keepdims=True)
        gd = dn * g2_ref[...]
        dm = dout[pl.ds(at, CHUNK), :].astype(F32) + s * gd - m * (s * s * s * jnp.mean(gd * m, axis=-1, keepdims=True))
        mid[pl.ds(at, CHUNK), :] = dm
        lhs[pl.ds(at, CHUNK), :] = dm.astype(BF16)
        second_t[:, pl.ds(at, CHUNK)] = dm.T.astype(BF16)
        bufc[pl.ds(at, CHUNK), :] = jnp.zeros((CHUNK, d), F32)
        return gain

    gain2 = lax.fori_loop(0, nchunk, second_back, jnp.zeros((1, d), F32))
    ssum[0] = jnp.zeros((16, d), F32)
    ssum[0, pl.ds(1, 1), :] = gain2
    gather(dproj.at[0])
    res_copy = pltpu.make_async_copy(dproj.at[0], res_hbm, lsem.at[6])
    res_copy.start()
    r_first(FF, 1)

    def backward_block(i, _):
        j = blocks - 1 - i
        s_ = zflip(j)

        def project(r, _):
            at = pl.multiple_of(r * CHUNK, CHUNK)
            dst[j, pl.ds(at, CHUNK), :] = dot_t(lhs[pl.ds(at, CHUNK), :], w_all[s_, pl.ds(o_out, ch), :])
            return 0

        lax.fori_loop(0, nchunk, project, 0)
        for half in range(2):
            rr = d // 2
            grad[s_, pl.ds(o_out, ch), half * ch : (half + 1) * ch] = dot(
                second_t[half * rr : (half + 1) * rr, :], st[j, pl.ds(SEGS, rows), :].astype(BF16)
            ).astype(BF16)
        r_start(OUT, j, 0)

        @pl.when(i == 0)
        def _():
            r_last(FF, 2)
            r_middle(FF, 3)

        @pl.when(i == 1)
        def _():
            r_last(FF, 0)

        @pl.when(i == 2)
        def _():
            r_last(FF, 3)
            r_middle(FF, 1)

        @pl.when(i == 3)
        def _():
            r_middle(OUT, 3)

        def one(step, w, q_):
            at = pl.multiple_of(step * SEGS, SEGS)
            a = 1.0 - upd[j, pl.ds(at, SEGS), :]
            c = dst[j, pl.ds(at, SEGS), :] + w
            return c, a * c, q_ * a

        w, q_ = jnp.zeros((SEGS, ch), F32), jnp.ones((SEGS, ch), F32)
        for step in range(steps - 1, steps - 6, -1):
            _, w, q_ = one(step, w, q_)

        def step8(n, carry):
            w, q_ = carry
            for q in range(8):
                _, w, q_ = one(steps - 6 - (n * 8 + q), w, q_)
            return w, q_

        w, q_ = lax.fori_loop(0, (steps - 8) // 8, step8, (w, q_))
        for step in range(2, -1, -1):
            bends[2 * step, j] = q_
            c, w, q_ = one(step, w, q_)
            bends[2 * step + 1, j] = c
        bends[6, j] = w
        bends[7, j] = q_
        bsend[j, pl.ds(0, 1), :] = backward_chain(j, jnp.zeros((1, ch), F32))
        for step in range(3):
            bsend[j, pl.ds(step + 1, 1), :] = upd[j, pl.ds(step * SEGS, 1), :] * (
                bends[2 * step + 1, j, pl.ds(0, 1), :]
                + bends[2 * step, j, pl.ds(0, 1), :] * ends[0, j, pl.ds(0, 1), :]
            )
        pl.when(t == 3)(b_copy(j).start)

        @pl.when(i > 0)
        def _():
            r_first(OUT, j + 1)

        @pl.when(i == 3)
        def _():
            r_middle(OUT, 2)

        return 0

    def backward_chain(j, start):
        run = start
        for seg in range(SEGS - 1, -1, -1):
            ends[0, j, pl.ds(seg, 1), :] = run
            run = bends[6, j, pl.ds(seg, 1), :] + bends[7, j, pl.ds(seg, 1), :] * run
        return run

    def b_copy(j):
        there = flip(j, 0)
        return remote(bsend.at[j], brecv.at[there], b_s.at[0], b_r.at[there], tensor=partner)

    lax.fori_loop(0, blocks, backward_block, 0)

    res_copy.wait()

    def backward_fix(i, _):
        j = blocks - 1 - i
        s_ = zflip(j)

        @pl.when(t == 2)
        def _():
            wait_for(brecv.at[j], b_r.at[j])

        backward_chain(j, brecv[j, pl.ds(0, 1), :] * has_next)
        w = ends[0, j]
        after = []
        for step in range(3):
            df = upd[j, pl.ds(step * SEGS, SEGS), :] * (bends[2 * step + 1, j] + bends[2 * step, j] * w)
            edge = brecv[j, pl.ds(step + 1, 1), :] * has_next
            after.append(jnp.where(seg_id == SEGS - 1, edge, pltpu.roll(df, SEGS - 1, 0)))
        k_ = [jnp.broadcast_to(cb[j, pl.ds(n, 1), :], (SEGS, ch)) for n in range(4)]
        zero = jnp.zeros((SEGS, ch), F32)

        def pair(n, carry):
            w, d1, d2, d3, c0, c1, c2, k0, k1, k2, k3, gb = carry
            top = steps - 2 - 2 * n
            made = []
            for q in range(2):
                at = pl.multiple_of((top + 1 - q) * SEGS, SEGS)
                u = upd[j, pl.ds(at, SEGS), :]
                c = dst[j, pl.ds(at, SEGS), :] + w
                d0 = c * u
                a = 1.0 - u
                w = a * c
                c3 = cand[j, pl.ds(at, SEGS), :]
                f = k_[0] * c0 + k_[1] * c1 + k_[2] * c2 + k_[3] * c3
                dg = d0 * a * (f - st[j, pl.ds(at, SEGS), :])
                dc = k_[0] * d0 + k_[1] * d1 + k_[2] * d2 + k_[3] * d3
                k0, k1, k2, k3 = k0 + d0 * c0, k1 + d0 * c1, k2 + d0 * c2, k3 + d0 * c3
                gb = gb + dg
                c0, c1, c2 = c1, c2, c3
                d1, d2, d3 = d0, d1, d2
                made.append((dg, dc))
            at = pl.multiple_of(top * SEGS, 2 * SEGS)
            dproj[j, pl.ds(at, 2 * SEGS), :ch] = jnp.concatenate([made[1][0], made[0][0]], axis=0).astype(BF16)
            dproj[j, pl.ds(at, 2 * SEGS), ch:] = jnp.concatenate([made[1][1], made[0][1]], axis=0).astype(BF16)
            return w, d1, d2, d3, c0, c1, c2, k0, k1, k2, k3, gb

        window = [cand[j, pl.ds((steps + 2 - n) * SEGS, SEGS), :] for n in range(3)]
        half = lax.fori_loop(0, steps // 4, pair, (w, *after, *window, zero, zero, zero, zero, zero))

        @pl.when(i == 0)
        def _():
            r_last(FF, 1)
            r_first(OUT, 0)
            r_last(OUT, 3)

        @pl.when(i == 1)
        def _():
            r_last(OUT, 2)
            r_middle(OUT, 0)

        @pl.when(i == 2)
        def _():
            r_last(OUT, 0)
            a_first(FF)

        @pl.when(i == 3)
        def _():
            r_middle(IN, 3)
            a_first(OUT)

        out = lax.fori_loop(steps // 4, steps // 2, pair, half)
        for n in range(5):
            at = 2 + 2 * n + bit_of(s_, 1)
            ssum[0, pl.ds(at, 1), pl.ds(pl.multiple_of(bit_of(s_, 0) * ch, LANES), ch)] = jnp.sum(
                out[7 + n], axis=0, keepdims=True
            )

        @pl.when(i > 1)
        def _():
            r_first(IN, j + 1)

        def first_grad(r, _):
            at = pl.multiple_of(r * CHUNK, CHUNK)
            grad[s_, pl.ds(o_in + at, CHUNK), :] = dot(first_t[pl.ds(at, CHUNK), :], dproj[j]).astype(BF16)
            return 0

        lax.fori_loop(0, d // CHUNK, first_grad, 0)
        r_start(IN, j, 0)


        @pl.when(i == 0)
        def _():
            r_middle(OUT, 1)

        @pl.when(i == 1)
        def _():
            r_first(IN, 3)
            r_last(OUT, 1)

        @pl.when(i == 3)
        def _():
            r_middle(IN, 2)

        return 0

    lax.fori_loop(0, blocks, backward_fix, 0)

    def first_back(r):
        at = r * CHUNK
        v = dot_t(dproj[0, pl.ds(at, CHUNK), :], w_all[shards[0], pl.ds(o_in, d), :])
        for j in range(1, blocks):
            v = v + dot_t(dproj[j, pl.ds(at, CHUNK), :], w_all[shards[j], pl.ds(o_in, d), :])
        bufc[pl.ds(at, CHUNK), :] = v

    first_back(0)
    r_last(IN, 3)
    first_back(1)
    r_first(IN, 0)
    first_back(2)
    r_middle(IN, 1)
    a_mid(FF)
    first_back(3)
    for r in range(4, nchunk):
        first_back(r)
    r_last(IN, 2)

    def first_norm_back(r, gain):
        at = pl.multiple_of(r * CHUNK, CHUNK)
        m = xp[pl.ds(at, CHUNK), :].astype(F32)
        s = scale_of(m)
        dn = bufc[pl.ds(at, CHUNK), :]
        gain = gain + jnp.sum(dn * m * s, axis=0, keepdims=True)
        gd = dn * g1_ref[...]
        dv = s * gd - m * (s * s * s * jnp.mean(gd * m, axis=-1, keepdims=True))
        put_perm(at, mid[pl.ds(at, CHUNK), :] + dv)
        return gain

    ssum[0, pl.ds(0, 1), :] = lax.fori_loop(0, nchunk, first_norm_back, jnp.zeros((1, d), F32))
    s_start(0)
    r_last(IN, 1)
    r_middle(IN, 0)
    a_mid(OUT)
    gather(mid)
    gx_copy = pltpu.make_async_copy(mid, gx_hbm, lsem.at[7])
    gx_copy.start()
    s_next(0)
    a_end(FF)
    r_last(IN, 0)
    a_first(IN)
    for g in range(1, len(groups) - 1):
        s_next(g)
    a_mid(IN)
    a_end(IN)
    a_end(OUT)
    s_next(len(groups) - 1)
    gains_ref[...] = ssum[len(groups), pl.ds(0, 8), :]
    for n in range(5):
        at = 2 + 2 * n + bit_of(t, 1)
        chan_ref[pl.ds(n, 1), :] = ssum[
            len(groups), pl.ds(at, 1), pl.ds(pl.multiple_of(bit_of(t, 0) * ch, LANES), ch)
        ]
    a_wait(FF, 0)
    a_wait(OUT, 0)
    a_wait(IN, 0)

    gx_copy.wait()
    pl.when(t == 2)(hcopy.wait_send)
    wait_for(cb.at[pl.ds(0, blocks - 1)], c_s.at[0])
    pl.when(t == 2)(lambda: wait_for(fsend, f_s.at[0]))
    pl.when(t == 3)(lambda: wait_for(bsend, b_s.at[0]))
    for kind in (IN, OUT, FF):
        for k in range(halves[kind]):
            n = span(kind, k + 1)
            wait_for(w_all.at[0, pl.ds(0, (blocks - 1) * n), :], w_s.at[kind, k])
            wait_for(grad.at[pl.ds(0, 2), pl.ds(0, blocks // 2 * n), :], r_s.at[kind, k])
            wait_for(fin.at[pl.ds(0, n), :], a_s.at[kind, k])
        n = span(kind, nb)
        wait_for(w_all.at[0, pl.ds(0, (blocks - 1) * n), :], w_s.at[kind, nb])
        wait_for(w_all.at[0, pl.ds(0, (blocks - 1) * n), :], r_s.at[kind, nb])
    for g in range(len(groups)):
        wait_for(sgot.at[g, pl.ds(0, (1 << len(groups[g])) - 1)], s_s.at[g])


def finish_kernel(dims, gains, chan, res, gx, fin, res_out, gx_out, gin_o, gout_o, gup_o, gdown_o, gnorm, gmlp, taps, gbias,
                  rbuf, gbuf, fbuf, gin, gout, gup, gdown, sem):
    rows, d, ch, ff = dims
    cuts = ((d + ch, ff), (d + ch + ff, ff), (d, ch), (0, d))
    parts = [pltpu.make_async_copy(fin.at[pl.ds(a, n)], fbuf.at[pl.ds(a, n)], sem.at[i]) for i, (a, n) in enumerate(cuts)]
    ins = [pltpu.make_async_copy(gx, gbuf, sem.at[4]), pltpu.make_async_copy(res, rbuf, sem.at[5])]
    for copy in parts + ins:
        copy.start()
    outs = []

    def put(src, dst):
        copy = pltpu.make_async_copy(src, dst, sem.at[6 + len(outs)])
        copy.start()
        outs.append(copy)

    gnorm[...] = gains[pl.ds(0, 1), :]
    gmlp[...] = gains[pl.ds(1, 1), :]
    taps[...] = chan[pl.ds(0, 4), :]
    gbias[...] = chan[pl.ds(4, 1), :]
    parts[0].wait()
    gup[...] = fbuf[pl.ds(d + ch, d), :].astype(F32)
    put(gup, gup_o)
    parts[1].wait()
    gdown[...] = fbuf[pl.ds(d + ch + ff, d), :].astype(F32).T
    put(gdown, gdown_o)
    ins[0].wait()
    put(gbuf, gx_out)
    ins[1].wait()
    put(rbuf, res_out)
    parts[2].wait()
    gout[:, : d // 2] = fbuf[pl.ds(d, ch), :ch].astype(F32).T
    gout[:, d // 2 :] = fbuf[pl.ds(d, ch), ch:].astype(F32).T
    put(gout, gout_o)
    parts[3].wait()
    gin[:, 0, :] = fbuf[pl.ds(0, d), :ch].astype(F32)
    gin[:, 1, :] = fbuf[pl.ds(0, d), ch:].astype(F32)
    put(gin, gin_o)
    for copy in outs:
        copy.wait()


def per_device(
    inputs,
    norm_gain,
    in_weight,
    conv_kernel,
    gate_bias,
    out_weight,
    mlp_gain,
    up_weight,
    down_weight,
    short_lengths,
    long_lengths,
    cotangent,
):
    rows, d = inputs.shape
    ch = in_weight.shape[2]
    ff = up_weight.shape[1]
    blocks = lax.axis_size("tensor")
    dp = lax.axis_size("dp")
    nb = log2(dp)
    assert dp == 1 << nb and blocks == 4 and rows == LSHORT and 2 * rows == LLONG
    assert short_lengths.shape == (2,) and long_lengths.shape == (1,)
    sizes = (d, ch, 2 * ff)
    total = sum(sizes)
    halves = tuple(min(nb, log2(r // TILE)) for r in sizes)

    def span_all(k):
        return sum(r >> min(k, h) for r, h in zip(sizes, halves))

    ngroups = len(bit_groups(nb))
    vm = pl.BlockSpec(memory_space=pltpu.VMEM)
    sm = pl.BlockSpec(memory_space=pltpu.SMEM)
    hb = pl.BlockSpec(memory_space=pl.ANY)
    dma = pltpu.SemaphoreType.DMA
    res, gx, fin, gains, chan = pl.pallas_call(
        functools.partial(block_kernel, (rows, d, blocks, ch, ff, nb)),
        out_shape=(
            jax.ShapeDtypeStruct((rows, d), BF16),
            jax.ShapeDtypeStruct((rows, d), F32),
            jax.ShapeDtypeStruct((total, d), BF16),
            jax.ShapeDtypeStruct((8, d), F32),
            jax.ShapeDtypeStruct((8, ch), F32),
        ),
        in_specs=[sm, sm, hb, hb, vm, vm, vm, vm, hb, hb, hb, hb],
        out_specs=(hb, hb) + (vm,) * 3,
        scratch_shapes=[
            pltpu.VMEM((blocks, total, d), BF16),
            pltpu.VMEM((blocks, total, d), BF16),
            pltpu.VMEM((rows, d), BF16),
            pltpu.VMEM((blocks, rows + 3 * SEGS, ch), F32),
            pltpu.VMEM((blocks, rows, ch), F32),
            pltpu.VMEM((blocks, rows + SEGS, ch), F32),
            pltpu.VMEM((blocks, rows, ch), F32),
            pltpu.VMEM((rows + 16, d), BF16),
            pltpu.VMEM((d, rows), BF16),
            pltpu.VMEM((d, rows), BF16),
            pltpu.VMEM((rows, d), BF16),
            pltpu.VMEM((d, rows), BF16),
            pltpu.VMEM((rows, d), F32),
            pltpu.VMEM((rows, d), F32),
            pltpu.VMEM((rows, d), F32),
            pltpu.VMEM((blocks, rows, d), BF16),
            pltpu.VMEM((d // LANES, rows, LANES), F32),
            pltpu.VMEM((16, d), BF16),
            pltpu.VMEM((blocks, 8, ch), F32),
            pltpu.VMEM((2, blocks, SEGS, ch), F32),
            pltpu.VMEM((8, blocks, SEGS, ch), F32),
            pltpu.VMEM((blocks, 8, ch), F32),
            pltpu.VMEM((blocks, 8, ch), F32),
            pltpu.VMEM((blocks, 8, ch), F32),
            pltpu.VMEM((blocks, 8, ch), F32),
            pltpu.VMEM((blocks, span_all(nb), d), BF16),
            pltpu.VMEM((ngroups + 1, 16, d), F32),
            pltpu.VMEM((ngroups, 3, 16, d), F32),
            dma((8,)),
            dma((1,)),
            dma((blocks,)),
            dma((1,)),
            dma((blocks,)),
            dma((1,)),
            dma((blocks,)),
            dma((1,)),
            dma((1,)),
            dma((3, nb + 1)),
            dma((3, blocks, nb + 1)),
            dma((3, nb + 1)),
            dma((3, blocks, nb + 1)),
            dma((3, blocks, nb)),
            dma((3, nb)),
            dma((3, nb)),
            dma((ngroups,)),
            dma((ngroups, 3)),
        ]
        + [pltpu.VMEM((blocks, span_all(k + 1), d), BF16) for k in range(nb)],
        compiler_params=pltpu.CompilerParams(
            collective_id=0, has_side_effects=True, vmem_limit_bytes=67043328
        ),
        name="block",
    )(
        short_lengths,
        long_lengths,
        inputs,
        cotangent,
        norm_gain[None],
        mlp_gain[None],
        conv_kernel,
        gate_bias[None],
        in_weight.reshape(d, 2 * ch),
        out_weight,
        up_weight,
        down_weight,
    )
    result, grad_inputs, gin, gout, gup, gdown, gnorm, gmlp, taps, gbias = pl.pallas_call(
        functools.partial(finish_kernel, (rows, d, ch, ff)),
        out_shape=(
            jax.ShapeDtypeStruct((rows, d), BF16),
            jax.ShapeDtypeStruct((rows, d), F32),
            jax.ShapeDtypeStruct((d, 2, ch), F32),
            jax.ShapeDtypeStruct((ch, d), F32),
            jax.ShapeDtypeStruct((d, ff), F32),
            jax.ShapeDtypeStruct((ff, d), F32),
            jax.ShapeDtypeStruct((1, d), F32),
            jax.ShapeDtypeStruct((1, d), F32),
            jax.ShapeDtypeStruct((4, ch), F32),
            jax.ShapeDtypeStruct((1, ch), F32),
        ),
        in_specs=[vm, vm, hb, hb, hb],
        out_specs=(hb,) * 6 + (vm,) * 4,
        scratch_shapes=[
            pltpu.VMEM((rows, d), BF16),
            pltpu.VMEM((rows, d), F32),
            pltpu.VMEM((total, d), BF16),
            pltpu.VMEM((d, 2, ch), F32),
            pltpu.VMEM((ch, d), F32),
            pltpu.VMEM((d, ff), F32),
            pltpu.VMEM((ff, d), F32),
            dma((12,)),
        ],
        compiler_params=pltpu.CompilerParams(vmem_limit_bytes=67043328),
        name="finish",
    )(gains, chan, res, gx, fin)
    return (result, grad_inputs, gnorm[0], gin, taps, gbias[0], gout, gmlp[0], gup, gdown)


def solution(mesh):
    placed = (
        P(("dp", "tensor"), None),
        P(),
        P(None, None, "tensor"),
        P(None, "tensor"),
        P("tensor"),
        P("tensor", None),
        P(),
        P(None, "tensor"),
        P("tensor", None),
        P("dp"),
        P("dp"),
        P(("dp", "tensor"), None),
    )
    return jax.shard_map(
        per_device,
        mesh=mesh,
        in_specs=placed,
        out_specs=(
            P(("dp", "tensor"), None),
            P(("dp", "tensor"), None),
            P(),
            P(None, None, "tensor"),
            P(None, "tensor"),
            P("tensor"),
            P("tensor", None),
            P(),
            P(None, "tensor"),
            P("tensor", None),
        ),
        check_vma=False,
    )
```

```python
import functools

import jax
import jax.numpy as jnp
import numpy as np
from jax import lax
from jax.experimental import pallas as pl
from jax.experimental.pallas import tpu as pltpu
from jax.sharding import PartitionSpec as P

LSHORT = 1024
LLONG = 2048
SEGS = 8
EPS = 1e-05
CHUNK = 256
TILE = 16
LANES = 128
F32 = jnp.float32
BF16 = jnp.bfloat16
MESH = pl.DeviceIdType.MESH
IN, OUT, FF = 0, 1, 2


def dot(a, b):
    return jnp.dot(a, b, preferred_element_type=F32)


def dot_t(a, b):
    return lax.dot_general(a, b, (((1,), (1,)), ((), ())), preferred_element_type=F32)


def scale_of(v):
    return lax.rsqrt(jnp.mean(v * v, axis=-1, keepdims=True) + EPS)


def sigmoid(v):
    return 1.0 / (1.0 + jnp.exp(-v))


def bit_of(v, bit):
    return lax.rem(lax.div(v, 1 << bit), 2)


def flip(v, bit):
    return v + (1 << bit) * (1 - 2 * bit_of(v, bit))


def log2(n):
    return int(n).bit_length() - 1


def bit_groups(nb):
    groups = [(0,)] + [tuple(range(b, min(b + 2, nb))) for b in range(1, nb, 2)]
    return groups + [(nb, nb + 1)]


def block_kernel(
    dims,
    short_ref,
    long_ref,
    x_hbm,
    cot_hbm,
    g1_ref,
    g2_ref,
    conv_ref,
    bias_ref,
    win_hbm,
    wout_hbm,
    wup_hbm,
    wdown_hbm,
    res,
    mid,
    fin,
    gains_ref,
    chan_ref,
    w_all,
    grad,
    win,
    xp,
    cand,
    upd,
    st,
    dst,
    lhs,
    first_t,
    second_t,
    dout,
    dout_t,
    bufa,
    bufc,
    dproj,
    perm,
    halo,
    cb,
    ends,
    bends,
    fsend,
    frecv,
    bsend,
    brecv,
    zbuf,
    ssum,
    sgot,
    lsem,
    c_s,
    c_r,
    f_s,
    f_r,
    b_s,
    b_r,
    h_s,
    h_r,
    w_s,
    w_r,
    r_s,
    r_r,
    x_s,
    a_s,
    a_r,
    s_s,
    s_r,
    *stage_bufs,
):
    rows, d, blocks, ch, ff, nb = dims
    steps = rows // SEGS
    t = lax.axis_index("tensor")
    p = lax.axis_index("dp")
    partner = flip(t, 0)
    nchunk = rows // CHUNK
    offs = (0, d, d + ch)
    sizes = (d, ch, 2 * ff)
    o_in, o_out, o_up, o_down = 0, d, d + ch, d + ch + ff
    halves = tuple(min(nb, log2(r // TILE)) for r in sizes)
    half_d = d // 2
    lanes = (pl.ds(0, half_d), pl.ds(half_d, half_d))
    orders = ((0,) + tuple(range(nb - 1, 0, -1)), tuple(range(nb)))
    nstage = len(stage_bufs)

    def zflip(j):
        b0, b1 = lax.rem(j, 2), lax.div(j, 2)
        return t + b0 * (1 - 2 * bit_of(t, 0)) + b1 * (2 - 4 * bit_of(t, 1))

    def low_of(kind, c, k):
        low = 0
        for i in range(min(k, halves[kind])):
            low = low + bit_of(p, orders[c][i]) * (sizes[kind] >> (i + 1))
        return low

    def span(kind, k):
        return sizes[kind] >> min(k, halves[kind])

    def at_rows(kind, start, n):
        return pl.ds(pl.multiple_of(offs[kind] + start, TILE), n)

    def stage_rows(kind, k):
        base = sum(span(i, k + 1) for i in range(kind))
        return pl.ds(base, span(kind, k + 1))

    def remote(src, dst_, ss, rs, **dev):
        return pltpu.make_async_remote_copy(
            src_ref=src, dst_ref=dst_, send_sem=ss, recv_sem=rs, device_id=dev, device_id_type=MESH
        )

    def wait_for(ref, sem):
        pltpu.make_async_copy(ref, ref, sem).wait()

    def w_step(kind, j, k):
        made = []
        for c in range(1 if k == 0 else 2):
            at = at_rows(kind, low_of(kind, c, k + 1), span(kind, k + 1))
            ref = w_all.at[zflip(j), at, slice(None) if k == 0 else lanes[c]]
            made.append(remote(ref, ref, w_s.at[kind, k], w_r.at[kind, j, k], dp=flip(p, orders[c][k])))
        return made

    def w_sources(kind, j):
        made = []
        for c in range(2):
            ref = w_all.at[t, at_rows(kind, low_of(kind, c, nb), span(kind, nb)), lanes[c]]
            made.append(remote(ref, ref, w_s.at[kind, nb], w_r.at[kind, j, nb], tensor=zflip(j)))
        return made

    def w_wait(kind, j, k):
        k_ = nb if k == halves[kind] else k
        wait_for(w_all.at[0, pl.ds(0, span(kind, k + 1))], w_r.at[kind, j, k_])

    def w_forward(kind, j, k):
        w_wait(kind, j, k + 1)
        for copy in w_step(kind, j, k):
            copy.start()

    def w_top(kind, *js):
        for j in js:
            w_forward(kind, j, halves[kind] - 1)

    def w_mid(kind, *js):
        for k in range(halves[kind] - 2, 0, -1):
            for j in js:
                w_forward(kind, j, k)

    def w_end(kind, *js):
        for j in js:
            w_forward(kind, j, 0)

    def r_step(kind, j, k):
        s = zflip(j)
        base = sum(span(i, k + 1) for i in range(kind))
        made = []
        for c in range(1 if k == 0 else 2):
            low = low_of(kind, c, k)
            if k < halves[kind]:
                low = low + (1 - bit_of(p, orders[c][k])) * span(kind, k + 1)
            which = slice(None) if k == 0 else lanes[c]
            made.append(
                remote(
                    grad.at[s, at_rows(kind, low, span(kind, k + 1)), which],
                    stage_bufs[k].at[j, pl.ds(base, span(kind, k + 1)), which],
                    r_s.at[kind, k] if k < halves[kind] else x_s.at[kind, j, k],
                    r_r.at[kind, j, k],
                    dp=flip(p, orders[c][k]),
                )
            )
        return made

    def r_start(kind, j, k):
        for copy in r_step(kind, j, k):
            copy.start()

    def r_finish(kind, j, k):
        s = zflip(j)
        buf = stage_bufs[k]
        base = sum(span(i, k + 1) for i in range(kind))
        n = span(kind, k + 1)
        here = stage_bufs[k].at[j, pl.ds(base, n), :]
        if k >= halves[kind]:
            wait_for(here, x_s.at[kind, j, k])
        wait_for(here, r_r.at[kind, j, k])
        piece = min(n, 128)
        for c in range(2):
            low = low_of(kind, c, k + 1)

            def add(i, _):
                at = at_rows(kind, low + i * piece, piece)
                here = pl.ds(pl.multiple_of(base + i * piece, TILE), piece)
                grad[s, at, lanes[c]] = (
                    grad[s, at, lanes[c]].astype(F32) + buf[j, here, lanes[c]].astype(F32)
                ).astype(BF16)
                return 0

            lax.fori_loop(0, n // piece, add, 0)

    def r_z(kind, j):
        s = zflip(j)
        base = sum(span(i, nb) for i in range(kind))
        made = []
        for c in range(2):
            at = at_rows(kind, low_of(kind, c, nb), span(kind, nb))
            made.append(
                remote(
                    grad.at[s, at, lanes[c]],
                    zbuf.at[j, pl.ds(base, span(kind, nb)), lanes[c]],
                    r_s.at[kind, nb],
                    r_r.at[kind, j, nb],
                    tensor=s,
                )
            )
        return made

    def r_out(kind, j):
        for copy in r_z(kind, j):
            copy.start()

    def r_total(kind):
        base = sum(span(i, nb) for i in range(kind))
        n = span(kind, nb)
        for j in range(1, blocks):
            wait_for(zbuf.at[j, pl.ds(base, n), :], r_r.at[kind, j, nb])
        for c in range(2):
            at = at_rows(kind, low_of(kind, c, nb), n)
            total = grad[t, at, lanes[c]].astype(F32)
            for j in range(1, blocks):
                total = total + zbuf[j, pl.ds(base, n), lanes[c]].astype(F32)
            fin[at, lanes[c]] = total.astype(BF16)

    def a_step(kind, k):
        made = []
        for c in range(1 if k == 0 else 2):
            at = at_rows(kind, low_of(kind, c, k + 1), span(kind, k + 1))
            ref = fin.at[at, slice(None) if k == 0 else lanes[c]]
            made.append(remote(ref, ref, a_s.at[kind, k], a_r.at[kind, k], dp=flip(p, orders[c][k])))
        return made

    def a_start(kind, k):
        for copy in a_step(kind, k):
            copy.start()

    def a_wait(kind, k):
        wait_for(fin.at[pl.ds(0, span(kind, k + 1)), :], a_r.at[kind, k])

    def r_middle(kind, j):
        for k in range(1, nb - 1):
            r_finish(kind, j, k)
            r_start(kind, j, k + 1)

    def r_first(kind, j):
        r_finish(kind, j, 0)
        r_start(kind, j, 1)

    def r_last(kind, j):
        r_finish(kind, j, nb - 1)
        if isinstance(j, int):
            if j > 0:
                r_out(kind, j)
        else:
            pl.when(j > 0)(lambda: r_out(kind, j))

    def a_first(kind):
        r_total(kind)
        a_start(kind, halves[kind] - 1)

    def a_mid(kind):
        for k in range(halves[kind] - 2, 0, -1):
            a_wait(kind, k + 1)
            a_start(kind, k)

    def a_end(kind):
        a_wait(kind, 1)
        a_start(kind, 0)

    groups = bit_groups(nb)

    def s_start(g):
        bits = groups[g]
        for r in range(1, 1 << len(bits)):
            dp_, tensor_ = p, t
            for i, b in enumerate(bits):
                if r >> i & 1:
                    dp_, tensor_ = (flip(dp_, b), tensor_) if b < nb else (dp_, flip(tensor_, b - nb))
            dev = {"dp": dp_} if bits[0] < nb else {"tensor": tensor_}
            remote(ssum.at[g], sgot.at[g, r - 1], s_s.at[g], s_r.at[g, r - 1], **dev).start()

    def s_next(g):
        n = (1 << len(groups[g])) - 1
        for r in range(n):
            wait_for(sgot.at[g, r], s_r.at[g, r])
        v = ssum[g] + sgot[g, 0]
        if n == 3:
            v = v + (sgot[g, 1] + sgot[g, 2])
        ssum[g + 1] = v
        if g + 1 < len(groups):
            s_start(g + 1)

    def local(src, dst_, i):
        return pltpu.make_async_copy(src, dst_, lsem.at[i])

    loads = [
        local(win_hbm, win, 0),
        local(x_hbm, dproj.at[0], 1),
        local(cot_hbm, dproj.at[1], 2),
        local(wout_hbm, w_all.at[t, pl.ds(o_out, ch), :], 3),
        local(wup_hbm, w_all.at[t, pl.ds(o_up, ff), :], 4),
        local(wdown_hbm, w_all.at[t, pl.ds(o_down, ff), :], 5),
    ]
    for copy in loads:
        copy.start()
    frecv[...] = jnp.zeros_like(frecv)
    brecv[...] = jnp.zeros_like(brecv)
    halo[...] = jnp.zeros_like(halo)
    cb[0, pl.ds(0, 4), :] = conv_ref[...]
    cb[0, pl.ds(4, 1), :] = bias_ref[...]
    barrier = pltpu.get_barrier_semaphore()
    for b in range(nb):
        pl.semaphore_signal(barrier, inc=1, device_id={"dp": flip(p, b)}, device_id_type=MESH)
    for j in range(1, blocks):
        pl.semaphore_signal(barrier, inc=1, device_id={"tensor": zflip(j)}, device_id_type=MESH)
    pl.semaphore_wait(barrier, nb + blocks - 1)

    def c_copy(j):
        return remote(cb.at[0], cb.at[j], c_s.at[0], c_r.at[j], tensor=zflip(j))

    hcopy = remote(x_hbm.at[pl.ds(rows - 16, 16), :], halo, h_s.at[0], h_r.at[0], tensor=partner)
    pl.when(t == 2)(hcopy.start)
    for j in range(1, blocks):
        c_copy(j).start()
    loads[0].wait()

    piece = span(IN, nb)

    def part(c, start):
        w_all[t, at_rows(IN, start, piece), lanes[c]] = win[pl.ds(start, piece), c, :]

    for c in range(2):
        part(c, low_of(IN, c, nb))
    for j in range(1, blocks):
        for copy in w_sources(IN, j):
            copy.start()

    def other_part(i, _):
        for c in range(2):
            part(c, lax.rem(low_of(IN, c, nb) + (i + 1) * piece, d))
        return 0

    lax.fori_loop(0, d // piece - 1, other_part, 0)
    loads[1].wait()

    nlane = d // LANES

    def spread(ref):
        for seg in range(SEGS):
            v = ref[pl.ds(seg * steps, steps), :].astype(F32)
            for i in range(nlane):
                perm[i, pl.ds(seg, steps, stride=SEGS), :] = v[:, i * LANES : (i + 1) * LANES]

    def gather(ref):
        for seg in range(SEGS):
            for i in range(nlane):
                v = perm[i, pl.ds(seg, steps, stride=SEGS), :]
                ref[pl.ds(seg * steps, steps), i * LANES : (i + 1) * LANES] = v.astype(ref.dtype)

    def perm_rows(at):
        return jnp.concatenate([perm[i, pl.ds(at, CHUNK), :] for i in range(nlane)], axis=1)

    def put_perm(at, v):
        for i in range(nlane):
            perm[i, pl.ds(at, CHUNK), :] = v[:, i * LANES : (i + 1) * LANES]

    spread(dproj.at[0])
    limit = jnp.where(
        t == 0,
        short_ref[0],
        jnp.where(t == 1, short_ref[1], jnp.where(t == 2, long_ref[0], long_ref[0] - rows)),
    )

    def norm_rows(r, _):
        at = pl.multiple_of(r * CHUNK, CHUNK)
        xv = perm_rows(at)
        xp[pl.ds(at, CHUNK), :] = xv.astype(BF16)
        fv = xv * scale_of(xv) * g1_ref[...]
        lhs[pl.ds(at, CHUNK), :] = fv.astype(BF16)
        first_t[:, pl.ds(at, CHUNK)] = fv.T.astype(BF16)
        return 0

    lax.fori_loop(0, nchunk, norm_rows, 0)
    loads[2].wait()
    spread(dproj.at[1])

    def dout_rows(r, _):
        at = pl.multiple_of(r * CHUNK, CHUNK)
        place = at + lax.broadcasted_iota(jnp.int32, (CHUNK, d), 0)
        pos = lax.rem(place, SEGS) * steps + place // SEGS
        dv = jnp.where(pos < limit, perm_rows(at), 0.0)
        dout[pl.ds(at, CHUNK), :] = dv.astype(BF16)
        dout_t[:, pl.ds(at, CHUNK)] = dv.T.astype(BF16)
        return 0

    lax.fori_loop(0, nchunk, dout_rows, 0)
    seg_id = lax.broadcasted_iota(jnp.int32, (SEGS, ch), 0)
    has_prev = jnp.where(t == 3, 1.0, 0.0).astype(F32)
    has_next = jnp.where(t == 2, 1.0, 0.0).astype(F32)

    def forward_block(j, _):
        s_ = zflip(j)

        @pl.when(j == 1)
        def _():
            w_top(IN, 3)
            w_mid(IN, 2)
            w_end(IN, 1)
            w_mid(IN, 3)

        @pl.when(j > 0)
        def _():
            c_copy(j).wait_recv()
            w_wait(IN, j, 0)

        def project(r, _):
            at = pl.multiple_of(r * CHUNK, CHUNK)
            v = dot(lhs[pl.ds(at, CHUNK), :], w_all[s_, pl.ds(o_in, d), :])
            bufa[pl.ds(at, CHUNK), :ch] = v[:, :ch]
            cand[j, pl.ds(at + 3 * SEGS, CHUNK), :] = v[:, ch:]

            @pl.when((j == 0) & (r == 1))
            def _():
                w_top(IN, 1)

            return 0

        lax.fori_loop(0, nchunk, project, 0)

        @pl.when(j == 0)
        def _():
            pl.when(t == 3)(hcopy.wait_recv)
            hv = halo[...].astype(F32)
            lhs[pl.ds(rows, 16), :] = (hv * scale_of(hv) * g1_ref[...]).astype(BF16)

        @pl.when(j == 1)
        def _():
            w_end(IN, 2)

        @pl.when(j == 2)
        def _():
            w_end(IN, 3)

        @pl.when(j == 3)
        def _():
            w_top(FF, 2)

        ph = dot(lhs[pl.ds(rows, 16), :], w_all[s_, pl.ds(o_in, d), ch:])
        for back in range(3):
            last = cand[j, pl.ds((steps + back) * SEGS, SEGS), :]
            rolled = pltpu.roll(last, 1, 0)
            edge = ph[13 + back : 14 + back, :] * has_prev
            cand[j, pl.ds(back * SEGS, SEGS), :] = jnp.where(seg_id == 0, edge, rolled)
        k_ = [jnp.broadcast_to(cb[j, pl.ds(i, 1), :], (SEGS, ch)) for i in range(4)]
        bias = jnp.broadcast_to(cb[j, pl.ds(4, 1), :], (SEGS, ch))

        def step4(i, carry):
            s, q_ = carry
            for q in range(4):
                at = pl.multiple_of((i * 4 + q) * SEGS, SEGS)
                u = sigmoid(bufa[pl.ds(at, SEGS), :ch] + bias)
                f = k_[0] * cand[j, pl.ds(at + 3 * SEGS, SEGS), :]
                for lag in range(1, 4):
                    f = f + k_[lag] * cand[j, pl.ds(at + (3 - lag) * SEGS, SEGS), :]
                upd[j, pl.ds(at, SEGS), :] = u
                dst[j, pl.ds(at, SEGS), :] = f
                a = 1.0 - u
                s = a * s + u * f
                q_ = a * q_
            return s, q_

        half = lax.fori_loop(
            0, steps // 8, step4, (jnp.zeros((SEGS, ch), F32), jnp.ones((SEGS, ch), F32))
        )

        @pl.when(j == 0)
        def _():
            w_top(IN, 2)

        s, q_ = lax.fori_loop(steps // 8, steps // 4, step4, half)
        ends[0, j] = s
        ends[1, j] = q_
        fsend[j] = jnp.broadcast_to(forward_chain(j, jnp.zeros((1, ch), F32)), (8, ch))
        pl.when(t == 2)(f_copy(j).start)

        @pl.when(j == 0)
        def _():
            w_mid(IN, 1)
            for i in range(3, 6):
                loads[i].wait()
            for kind in (OUT, FF):
                for i in (2, 3, 1):
                    for copy in w_sources(kind, i):
                        copy.start()

        @pl.when(j == 1)
        def _():
            w_top(OUT, 1, 2, 3)

        @pl.when(j == 2)
        def _():
            w_mid(OUT, 1, 2, 3)

        return 0

    def forward_chain(j, start):
        run = start
        for seg in range(SEGS):
            st[j, pl.ds(seg, 1), :] = run
            run = ends[0, j, pl.ds(seg, 1), :] + ends[1, j, pl.ds(seg, 1), :] * run
        return run

    def f_copy(j):
        there = flip(j, 0)
        return remote(fsend.at[j], frecv.at[there], f_s.at[0], f_r.at[there], tensor=partner)

    lax.fori_loop(0, blocks, forward_block, 0)
    w_top(FF, 3)

    def forward_fix(i, _):
        b = flip(i, 0)

        @pl.when(t == 3)
        def _():
            wait_for(frecv.at[b], f_r.at[b])

        forward_chain(b, frecv[b, pl.ds(0, 1), :] * has_prev)

        def step8(i, s):
            for q in range(8):
                at = pl.multiple_of((i * 8 + q) * SEGS, SEGS)
                u = upd[b, pl.ds(at, SEGS), :]
                s = (1.0 - u) * s + u * dst[b, pl.ds(at, SEGS), :]
                st[b, pl.ds(at + SEGS, SEGS), :] = s
            return s

        lax.fori_loop(0, steps // 8, step8, st[b, pl.ds(0, SEGS), :])

        @pl.when(i == 1)
        def _():
            w_end(OUT, 1, 2, 3)

        return 0

    lax.fori_loop(0, blocks, forward_fix, 0)
    w_mid(FF, 2)
    for j in range(1, blocks):
        w_wait(OUT, j, 0)
    shards = [zflip(j) for j in range(blocks)]

    def second_rows(r, _):
        at = pl.multiple_of(r * CHUNK, CHUNK)
        m = xp[pl.ds(at, CHUNK), :].astype(F32)
        for j in range(blocks):
            m = m + dot(
                st[j, pl.ds(at + SEGS, CHUNK), :].astype(BF16), w_all[shards[j], pl.ds(o_out, ch), :]
            )
        mid[pl.ds(at, CHUNK), :] = m
        sv = m * scale_of(m) * g2_ref[...]
        lhs[pl.ds(at, CHUNK), :] = sv.astype(BF16)
        second_t[:, pl.ds(at, CHUNK)] = sv.T.astype(BF16)
        bufa[pl.ds(at, CHUNK), :] = m
        bufc[pl.ds(at, CHUNK), :] = jnp.zeros((CHUNK, d), F32)
        return 0

    lax.fori_loop(0, nchunk, second_rows, 0)

    w_mid(FF, 3)
    act, din = dproj.at[1], dproj.at[2]

    def ff_place(i):
        return lax.div(i + 3, 4) * (1 + lax.rem(i, 3))

    def ff_block(i, _):
        j, before, earlier = ff_place(i), ff_place(i - 1), ff_place(i - 2)
        s_ = zflip(j)

        @pl.when(i > 0)
        def _():
            w_wait(FF, j, 0)

        def ff_rows(r, _):
            at = pl.multiple_of(r * CHUNK, CHUNK)
            wu = w_all[s_, pl.ds(o_up, ff), :]
            wd = w_all[s_, pl.ds(o_down, ff), :]
            inner = dot(lhs[pl.ds(at, CHUNK), :], wu)
            da = dot_t(dout[pl.ds(at, CHUNK), :], wd)
            cdf = 0.5 + 0.5 * lax.erf(inner * np.float32(np.sqrt(0.5)))
            pdf = jnp.exp(inner * inner * -0.5) * np.float32(1.0 / np.sqrt(2.0 * np.pi))
            av = (inner * cdf).astype(BF16)
            dv = (da * (cdf + inner * pdf)).astype(BF16)
            act[pl.ds(at, CHUNK), :] = av
            din[pl.ds(at, CHUNK), :] = dv
            bufa[pl.ds(at, CHUNK), :] += dot(av, wd)
            bufc[pl.ds(at, CHUNK), :] += dot_t(dv, wu)

            @pl.when((r == 1) & (i == 0))
            def _():
                w_end(FF, 2)

            @pl.when((r == 2) & (i == 0))
            def _():
                w_top(FF, 1)

            @pl.when((r == 0) & (i == 1))
            def _():
                w_end(FF, 3)

            @pl.when((r == 1) & (i == 1))
            def _():
                w_mid(FF, 1)

            @pl.when((r == 1) & (i == 2))
            def _():
                w_end(FF, 1)

            @pl.when((r == 3) & (i > 1))
            def _():
                r_middle(FF, earlier)

            @pl.when((r == 3) & (i > 0))
            def _():
                r_first(FF, before)

            return 0

        lax.fori_loop(0, nchunk, ff_rows, 0)

        def ff_grads(r, _):
            at = pl.multiple_of(r * CHUNK, CHUNK)
            grad[s_, pl.ds(o_up + at, CHUNK), :] = dot(second_t[pl.ds(at, CHUNK), :], din[...]).astype(BF16)
            grad[s_, pl.ds(o_down + at, CHUNK), :] = dot(dout_t[pl.ds(at, CHUNK), :], act[...]).astype(BF16)
            return 0

        lax.fori_loop(0, d // CHUNK, ff_grads, 0)
        r_start(FF, j, 0)
        return 0

    lax.fori_loop(0, blocks, ff_block, 0)

    def second_back(r, gain):
        at = pl.multiple_of(r * CHUNK, CHUNK)
        put_perm(at, bufa[pl.ds(at, CHUNK), :])
        m = mid[pl.ds(at, CHUNK), :]
        s = scale_of(m)
        dn = bufc[pl.ds(at, CHUNK), :]
        gain = gain + jnp.sum(dn * m * s, axis=0, keepdims=True)
        gd = dn * g2_ref[...]
        dm = dout[pl.ds(at, CHUNK), :].astype(F32) + s * gd - m * (s * s * s * jnp.mean(gd * m, axis=-1, keepdims=True))
        mid[pl.ds(at, CHUNK), :] = dm
        lhs[pl.ds(at, CHUNK), :] = dm.astype(BF16)
        second_t[:, pl.ds(at, CHUNK)] = dm.T.astype(BF16)
        bufc[pl.ds(at, CHUNK), :] = jnp.zeros((CHUNK, d), F32)
        return gain

    gain2 = lax.fori_loop(0, nchunk, second_back, jnp.zeros((1, d), F32))
    ssum[0] = jnp.zeros((16, d), F32)
    ssum[0, pl.ds(1, 1), :] = gain2
    gather(res)
    r_first(FF, 1)

    def backward_block(i, _):
        j = blocks - 1 - i
        s_ = zflip(j)

        def project(r, _):
            at = pl.multiple_of(r * CHUNK, CHUNK)
            dst[j, pl.ds(at, CHUNK), :] = dot_t(lhs[pl.ds(at, CHUNK), :], w_all[s_, pl.ds(o_out, ch), :])
            return 0

        lax.fori_loop(0, nchunk, project, 0)
        for half in range(2):
            rr = d // 2
            grad[s_, pl.ds(o_out, ch), half * ch : (half + 1) * ch] = dot(
                second_t[half * rr : (half + 1) * rr, :], st[j, pl.ds(SEGS, rows), :].astype(BF16)
            ).astype(BF16)
        r_start(OUT, j, 0)

        @pl.when(i == 0)
        def _():
            r_last(FF, 2)
            r_middle(FF, 3)

        @pl.when(i == 1)
        def _():
            r_last(FF, 0)

        @pl.when(i == 2)
        def _():
            r_last(FF, 3)
            r_middle(FF, 1)

        @pl.when(i == 3)
        def _():
            r_middle(OUT, 3)

        def one(step, w, q_):
            at = pl.multiple_of(step * SEGS, SEGS)
            a = 1.0 - upd[j, pl.ds(at, SEGS), :]
            c = dst[j, pl.ds(at, SEGS), :] + w
            return c, a * c, q_ * a

        w, q_ = jnp.zeros((SEGS, ch), F32), jnp.ones((SEGS, ch), F32)
        for step in range(steps - 1, steps - 6, -1):
            _, w, q_ = one(step, w, q_)

        def step8(n, carry):
            w, q_ = carry
            for q in range(8):
                _, w, q_ = one(steps - 6 - (n * 8 + q), w, q_)
            return w, q_

        w, q_ = lax.fori_loop(0, (steps - 8) // 8, step8, (w, q_))
        for step in range(2, -1, -1):
            bends[2 * step, j] = q_
            c, w, q_ = one(step, w, q_)
            bends[2 * step + 1, j] = c
        bends[6, j] = w
        bends[7, j] = q_
        bsend[j, pl.ds(0, 1), :] = backward_chain(j, jnp.zeros((1, ch), F32))
        for step in range(3):
            bsend[j, pl.ds(step + 1, 1), :] = upd[j, pl.ds(step * SEGS, 1), :] * (
                bends[2 * step + 1, j, pl.ds(0, 1), :]
                + bends[2 * step, j, pl.ds(0, 1), :] * ends[0, j, pl.ds(0, 1), :]
            )
        pl.when(t == 3)(b_copy(j).start)

        @pl.when(i > 0)
        def _():
            r_first(OUT, j + 1)

        return 0

    def backward_chain(j, start):
        run = start
        for seg in range(SEGS - 1, -1, -1):
            ends[0, j, pl.ds(seg, 1), :] = run
            run = bends[6, j, pl.ds(seg, 1), :] + bends[7, j, pl.ds(seg, 1), :] * run
        return run

    def b_copy(j):
        there = flip(j, 0)
        return remote(bsend.at[j], brecv.at[there], b_s.at[0], b_r.at[there], tensor=partner)

    lax.fori_loop(0, blocks, backward_block, 0)


    def backward_fix(i, _):
        j = blocks - 1 - i
        s_ = zflip(j)

        @pl.when(t == 2)
        def _():
            wait_for(brecv.at[j], b_r.at[j])

        backward_chain(j, brecv[j, pl.ds(0, 1), :] * has_next)
        w = ends[0, j]
        after = []
        for step in range(3):
            df = upd[j, pl.ds(step * SEGS, SEGS), :] * (bends[2 * step + 1, j] + bends[2 * step, j] * w)
            edge = brecv[j, pl.ds(step + 1, 1), :] * has_next
            after.append(jnp.where(seg_id == SEGS - 1, edge, pltpu.roll(df, SEGS - 1, 0)))
        k_ = [jnp.broadcast_to(cb[j, pl.ds(n, 1), :], (SEGS, ch)) for n in range(4)]
        zero = jnp.zeros((SEGS, ch), F32)

        def pair(n, carry):
            w, d1, d2, d3, c0, c1, c2, k0, k1, k2, k3, gb = carry
            top = steps - 2 - 2 * n
            made = []
            for q in range(2):
                at = pl.multiple_of((top + 1 - q) * SEGS, SEGS)
                u = upd[j, pl.ds(at, SEGS), :]
                c = dst[j, pl.ds(at, SEGS), :] + w
                d0 = c * u
                a = 1.0 - u
                w = a * c
                c3 = cand[j, pl.ds(at, SEGS), :]
                f = k_[0] * c0 + k_[1] * c1 + k_[2] * c2 + k_[3] * c3
                dg = d0 * a * (f - st[j, pl.ds(at, SEGS), :])
                dc = k_[0] * d0 + k_[1] * d1 + k_[2] * d2 + k_[3] * d3
                k0, k1, k2, k3 = k0 + d0 * c0, k1 + d0 * c1, k2 + d0 * c2, k3 + d0 * c3
                gb = gb + dg
                c0, c1, c2 = c1, c2, c3
                d1, d2, d3 = d0, d1, d2
                made.append((dg, dc))
            at = pl.multiple_of(top * SEGS, 2 * SEGS)
            dproj[j, pl.ds(at, 2 * SEGS), :ch] = jnp.concatenate([made[1][0], made[0][0]], axis=0).astype(BF16)
            dproj[j, pl.ds(at, 2 * SEGS), ch:] = jnp.concatenate([made[1][1], made[0][1]], axis=0).astype(BF16)
            return w, d1, d2, d3, c0, c1, c2, k0, k1, k2, k3, gb

        window = [cand[j, pl.ds((steps + 2 - n) * SEGS, SEGS), :] for n in range(3)]
        half = lax.fori_loop(0, steps // 4, pair, (w, *after, *window, zero, zero, zero, zero, zero))

        @pl.when(i == 0)
        def _():
            r_middle(OUT, 2)
            r_last(FF, 1)
            r_first(OUT, 0)
            r_last(OUT, 3)

        @pl.when(i == 1)
        def _():
            r_last(OUT, 2)
            r_middle(OUT, 0)

        @pl.when(i == 2)
        def _():
            r_last(OUT, 0)
            a_first(FF)

        @pl.when(i == 3)
        def _():
            r_middle(IN, 3)
            a_first(OUT)

        out = lax.fori_loop(steps // 4, steps // 2, pair, half)
        for n in range(5):
            at = 2 + 2 * n + bit_of(s_, 1)
            ssum[0, pl.ds(at, 1), pl.ds(pl.multiple_of(bit_of(s_, 0) * ch, LANES), ch)] = jnp.sum(
                out[7 + n], axis=0, keepdims=True
            )

        @pl.when(i > 1)
        def _():
            r_first(IN, j + 1)

        def first_grad(r, _):
            at = pl.multiple_of(r * CHUNK, CHUNK)
            grad[s_, pl.ds(o_in + at, CHUNK), :] = dot(first_t[pl.ds(at, CHUNK), :], dproj[j]).astype(BF16)
            return 0

        lax.fori_loop(0, d // CHUNK, first_grad, 0)
        r_start(IN, j, 0)


        @pl.when(i == 0)
        def _():
            r_middle(OUT, 1)

        @pl.when(i == 1)
        def _():
            r_first(IN, 3)
            r_last(OUT, 1)

        @pl.when(i == 3)
        def _():
            r_middle(IN, 2)

        return 0

    lax.fori_loop(0, blocks, backward_fix, 0)

    def first_back(r):
        at = r * CHUNK
        v = dot_t(dproj[0, pl.ds(at, CHUNK), :], w_all[shards[0], pl.ds(o_in, d), :])
        for j in range(1, blocks):
            v = v + dot_t(dproj[j, pl.ds(at, CHUNK), :], w_all[shards[j], pl.ds(o_in, d), :])
        bufc[pl.ds(at, CHUNK), :] = v

    first_back(0)
    r_last(IN, 3)
    first_back(1)
    r_first(IN, 0)
    first_back(2)
    r_middle(IN, 1)
    first_back(3)
    for r in range(4, nchunk):
        first_back(r)
    r_last(IN, 2)

    def first_norm_back(r, gain):
        at = pl.multiple_of(r * CHUNK, CHUNK)
        m = xp[pl.ds(at, CHUNK), :].astype(F32)
        s = scale_of(m)
        dn = bufc[pl.ds(at, CHUNK), :]
        gain = gain + jnp.sum(dn * m * s, axis=0, keepdims=True)
        gd = dn * g1_ref[...]
        dv = s * gd - m * (s * s * s * jnp.mean(gd * m, axis=-1, keepdims=True))
        put_perm(at, mid[pl.ds(at, CHUNK), :] + dv)
        return gain

    ssum[0, pl.ds(0, 1), :] = lax.fori_loop(0, nchunk, first_norm_back, jnp.zeros((1, d), F32))
    s_start(0)
    r_last(IN, 1)
    r_middle(IN, 0)
    a_mid(FF)
    a_mid(OUT)
    gather(mid)
    s_next(0)
    r_last(IN, 0)
    a_first(IN)
    a_end(FF)
    for g in range(1, len(groups) - 1):
        s_next(g)
    a_mid(IN)
    a_end(IN)
    a_end(OUT)
    s_next(len(groups) - 1)
    gains_ref[...] = ssum[len(groups), pl.ds(0, 8), :]
    for n in range(5):
        at = 2 + 2 * n + bit_of(t, 1)
        chan_ref[pl.ds(n, 1), :] = ssum[
            len(groups), pl.ds(at, 1), pl.ds(pl.multiple_of(bit_of(t, 0) * ch, LANES), ch)
        ]
    a_wait(FF, 0)
    a_wait(OUT, 0)
    a_wait(IN, 0)

    pl.when(t == 2)(hcopy.wait_send)
    wait_for(cb.at[pl.ds(0, blocks - 1)], c_s.at[0])
    pl.when(t == 2)(lambda: wait_for(fsend, f_s.at[0]))
    pl.when(t == 3)(lambda: wait_for(bsend, b_s.at[0]))
    for kind in (IN, OUT, FF):
        for k in range(halves[kind]):
            n = span(kind, k + 1)
            wait_for(w_all.at[0, pl.ds(0, (blocks - 1) * n), :], w_s.at[kind, k])
            wait_for(grad.at[pl.ds(0, 2), pl.ds(0, blocks // 2 * n), :], r_s.at[kind, k])
            wait_for(fin.at[pl.ds(0, n), :], a_s.at[kind, k])
        n = span(kind, nb)
        wait_for(w_all.at[0, pl.ds(0, (blocks - 1) * n), :], w_s.at[kind, nb])
        wait_for(w_all.at[0, pl.ds(0, (blocks - 1) * n), :], r_s.at[kind, nb])
    for g in range(len(groups)):
        wait_for(sgot.at[g, pl.ds(0, (1 << len(groups[g])) - 1)], s_s.at[g])


def finish_kernel(
    dims, gains, chan, res, gx, fin, res_out, gx_out, gin_o, gout_o, gup_o, gdown_o, gnorm, gmlp, taps, gbias,
    gin, gout, gup, gdown, sem,
):
    rows, d, ch, ff = dims
    outs = []

    def put(src, dst):
        copy = pltpu.make_async_copy(src, dst, sem.at[len(outs)])
        copy.start()
        outs.append(copy)

    put(gx, gx_out)
    put(res, res_out)
    gup[...] = fin[pl.ds(d + ch, d), :].astype(F32)
    put(gup, gup_o)
    gin[:, 0, :] = fin[pl.ds(0, d), :ch].astype(F32)
    gin[:, 1, :] = fin[pl.ds(0, d), ch:].astype(F32)
    put(gin, gin_o)
    gdown[...] = fin[pl.ds(d + ch + ff, d), :].astype(F32).T
    put(gdown, gdown_o)
    gout[:, : d // 2] = fin[pl.ds(d, ch), :ch].astype(F32).T
    gout[:, d // 2 :] = fin[pl.ds(d, ch), ch:].astype(F32).T
    put(gout, gout_o)
    gnorm[...] = gains[pl.ds(0, 1), :]
    gmlp[...] = gains[pl.ds(1, 1), :]
    taps[...] = chan[pl.ds(0, 4), :]
    gbias[...] = chan[pl.ds(4, 1), :]
    for copy in outs:
        copy.wait()


def per_device(
    inputs,
    norm_gain,
    in_weight,
    conv_kernel,
    gate_bias,
    out_weight,
    mlp_gain,
    up_weight,
    down_weight,
    short_lengths,
    long_lengths,
    cotangent,
):
    rows, d = inputs.shape
    ch = in_weight.shape[2]
    ff = up_weight.shape[1]
    blocks = lax.axis_size("tensor")
    dp = lax.axis_size("dp")
    nb = log2(dp)
    assert dp == 1 << nb and blocks == 4 and rows == LSHORT and 2 * rows == LLONG
    assert 2 * ch == d and short_lengths.shape == (2,) and long_lengths.shape == (1,)
    sizes = (d, ch, 2 * ff)
    total = sum(sizes)
    halves = tuple(min(nb, log2(r // TILE)) for r in sizes)

    def span_all(k):
        return sum(r >> min(k, h) for r, h in zip(sizes, halves))

    ngroups = len(bit_groups(nb))
    vm = pl.BlockSpec(memory_space=pltpu.VMEM)
    sm = pl.BlockSpec(memory_space=pltpu.SMEM)
    hb = pl.BlockSpec(memory_space=pl.ANY)
    dma = pltpu.SemaphoreType.DMA
    res, gx, fin, gains, chan = pl.pallas_call(
        functools.partial(block_kernel, (rows, d, blocks, ch, ff, nb)),
        out_shape=(
            pltpu.VMEM((rows, d), BF16),
            pltpu.VMEM((rows, d), F32),
            pltpu.VMEM((total, d), BF16),
            pltpu.VMEM((8, d), F32),
            pltpu.VMEM((8, ch), F32),
        ),
        in_specs=[sm, sm, hb, hb, vm, vm, vm, vm, hb, hb, hb, hb],
        out_specs=(vm,) * 5,
        scratch_shapes=[
            pltpu.VMEM((blocks, total, d), BF16),
            pltpu.VMEM((blocks, total, d), BF16),
            pltpu.VMEM((d, 2, ch), BF16),
            pltpu.VMEM((rows, d), BF16),
            pltpu.VMEM((blocks, rows + 3 * SEGS, ch), F32),
            pltpu.VMEM((blocks, rows, ch), F32),
            pltpu.VMEM((blocks, rows + SEGS, ch), F32),
            pltpu.VMEM((blocks, rows, ch), F32),
            pltpu.VMEM((rows + 16, d), BF16),
            pltpu.VMEM((d, rows), BF16),
            pltpu.VMEM((d, rows), BF16),
            pltpu.VMEM((rows, d), BF16),
            pltpu.VMEM((d, rows), BF16),
            pltpu.VMEM((rows, d), F32),
            pltpu.VMEM((rows, d), F32),
            pltpu.VMEM((blocks, rows, d), BF16),
            pltpu.VMEM((d // LANES, rows, LANES), F32),
            pltpu.VMEM((16, d), BF16),
            pltpu.VMEM((blocks, 8, ch), F32),
            pltpu.VMEM((2, blocks, SEGS, ch), F32),
            pltpu.VMEM((8, blocks, SEGS, ch), F32),
            pltpu.VMEM((blocks, 8, ch), F32),
            pltpu.VMEM((blocks, 8, ch), F32),
            pltpu.VMEM((blocks, 8, ch), F32),
            pltpu.VMEM((blocks, 8, ch), F32),
            pltpu.VMEM((blocks, span_all(nb), d), BF16),
            pltpu.VMEM((ngroups + 1, 16, d), F32),
            pltpu.VMEM((ngroups, 3, 16, d), F32),
            dma((6,)),
            dma((1,)),
            dma((blocks,)),
            dma((1,)),
            dma((blocks,)),
            dma((1,)),
            dma((blocks,)),
            dma((1,)),
            dma((1,)),
            dma((3, nb + 1)),
            dma((3, blocks, nb + 1)),
            dma((3, nb + 1)),
            dma((3, blocks, nb + 1)),
            dma((3, blocks, nb)),
            dma((3, nb)),
            dma((3, nb)),
            dma((ngroups,)),
            dma((ngroups, 3)),
        ]
        + [pltpu.VMEM((blocks, span_all(k + 1), d), BF16) for k in range(nb)],
        compiler_params=pltpu.CompilerParams(
            collective_id=0, has_side_effects=True, vmem_limit_bytes=58 << 20
        ),
        name="block",
    )(
        short_lengths,
        long_lengths,
        inputs,
        cotangent,
        norm_gain[None],
        mlp_gain[None],
        conv_kernel,
        gate_bias[None],
        in_weight,
        out_weight,
        up_weight,
        down_weight,
    )
    result, grad_inputs, gin, gout, gup, gdown, gnorm, gmlp, taps, gbias = pl.pallas_call(
        functools.partial(finish_kernel, (rows, d, ch, ff)),
        out_shape=(
            jax.ShapeDtypeStruct((rows, d), BF16),
            jax.ShapeDtypeStruct((rows, d), F32),
            jax.ShapeDtypeStruct((d, 2, ch), F32),
            jax.ShapeDtypeStruct((ch, d), F32),
            jax.ShapeDtypeStruct((d, ff), F32),
            jax.ShapeDtypeStruct((ff, d), F32),
            jax.ShapeDtypeStruct((1, d), F32),
            jax.ShapeDtypeStruct((1, d), F32),
            jax.ShapeDtypeStruct((4, ch), F32),
            jax.ShapeDtypeStruct((1, ch), F32),
        ),
        in_specs=[vm] * 5,
        out_specs=(hb,) * 6 + (vm,) * 4,
        scratch_shapes=[
            pltpu.VMEM((d, 2, ch), F32),
            pltpu.VMEM((ch, d), F32),
            pltpu.VMEM((d, ff), F32),
            pltpu.VMEM((ff, d), F32),
            dma((6,)),
        ],
        compiler_params=pltpu.CompilerParams(vmem_limit_bytes=32 << 20),
        name="finish",
    )(gains, chan, res, gx, fin)
    return (result, grad_inputs, gnorm[0], gin, taps, gbias[0], gout, gmlp[0], gup, gdown)


def solution(mesh):
    placed = (
        P(("dp", "tensor"), None),
        P(),
        P(None, None, "tensor"),
        P(None, "tensor"),
        P("tensor"),
        P("tensor", None),
        P(),
        P(None, "tensor"),
        P("tensor", None),
        P("dp"),
        P("dp"),
        P(("dp", "tensor"), None),
    )
    return jax.shard_map(
        per_device,
        mesh=mesh,
        in_specs=placed,
        out_specs=(
            P(("dp", "tensor"), None),
            P(("dp", "tensor"), None),
            P(),
            P(None, None, "tensor"),
            P(None, "tensor"),
            P("tensor"),
            P("tensor", None),
            P(),
            P(None, "tensor"),
            P("tensor", None),
        ),
        check_vma=False,
    )
```

```python
import functools

import jax
import jax.numpy as jnp
import numpy as np
from jax import lax
from jax.experimental import pallas as pl
from jax.experimental.pallas import tpu as pltpu
from jax.sharding import PartitionSpec as P

LSHORT = 1024
LLONG = 2048
SEGS = 8
EPS = 1e-05
CHUNK = 256
WIDE = 1024
TILE = 16
LANES = 128
F32 = jnp.float32
BF16 = jnp.bfloat16
MESH = pl.DeviceIdType.MESH
IN, OUT, FF = 0, 1, 2


def dot(a, b):
    return jnp.dot(a, b, preferred_element_type=F32)


def dot_t(a, b):
    return lax.dot_general(a, b, (((1,), (1,)), ((), ())), preferred_element_type=F32)


def scale_of(v):
    return lax.rsqrt(jnp.mean(v * v, axis=-1, keepdims=True) + EPS)


def sigmoid(v):
    return 1.0 / (1.0 + jnp.exp(-v))


def bit_of(v, bit):
    return lax.rem(lax.div(v, 1 << bit), 2)


def flip(v, bit):
    return v + (1 << bit) * (1 - 2 * bit_of(v, bit))


def log2(n):
    return int(n).bit_length() - 1


def bit_groups(nb):
    groups = [(0,)] + [tuple(range(b, min(b + 2, nb))) for b in range(1, nb, 2)]
    return groups + [(nb, nb + 1)]


def block_kernel(
    dims,
    short_ref,
    long_ref,
    x_hbm,
    cot_hbm,
    g1_ref,
    g2_ref,
    conv_ref,
    bias_ref,
    win_hbm,
    wout_hbm,
    wup_hbm,
    wdown_hbm,
    res,
    mid,
    fin,
    gains_ref,
    chan_ref,
    w_all,
    grad,
    win,
    xp,
    cand,
    upd,
    st,
    dst,
    edge_rows,
    first_t,
    second_t,
    dout,
    dout_t,
    bufa,
    bufc,
    dproj,
    perm,
    halo,
    cb,
    ends,
    bends,
    fsend,
    frecv,
    bsend,
    brecv,
    zbuf,
    ssum,
    sgot,
    lsem,
    c_s,
    c_r,
    f_s,
    f_r,
    b_s,
    b_r,
    h_s,
    h_r,
    w_s,
    w_r,
    r_s,
    r_r,
    x_s,
    a_s,
    a_r,
    s_s,
    s_r,
    *stage_bufs,
):
    rows, d, blocks, ch, ff, nb = dims
    steps = rows // SEGS
    t = lax.axis_index("tensor")
    p = lax.axis_index("dp")
    partner = flip(t, 0)
    nchunk = rows // CHUNK
    offs = (0, d, d + ch)
    sizes = (d, ch, 2 * ff)
    o_in, o_out, o_up, o_down = 0, d, d + ch, d + ch + ff
    halves = tuple(min(nb, log2(r // TILE)) for r in sizes)
    half_d = d // 2
    lanes = (pl.ds(0, half_d), pl.ds(half_d, half_d))
    orders = ((0,) + tuple(range(nb - 1, 0, -1)), tuple(range(nb)))
    lhs = dproj.at[3]

    def zflip(j):
        b0, b1 = lax.rem(j, 2), lax.div(j, 2)
        return t + b0 * (1 - 2 * bit_of(t, 0)) + b1 * (2 - 4 * bit_of(t, 1))

    def low_of(kind, c, k):
        low = 0
        for i in range(min(k, halves[kind])):
            low = low + bit_of(p, orders[c][i]) * (sizes[kind] >> (i + 1))
        return low

    def span(kind, k):
        return sizes[kind] >> min(k, halves[kind])

    def at_rows(kind, start, n):
        return pl.ds(pl.multiple_of(offs[kind] + start, TILE), n)

    def stage_rows(kind, k):
        base = sum(span(i, k + 1) for i in range(kind))
        return pl.ds(base, span(kind, k + 1))

    def remote(src, dst_, ss, rs, **dev):
        return pltpu.make_async_remote_copy(
            src_ref=src, dst_ref=dst_, send_sem=ss, recv_sem=rs, device_id=dev, device_id_type=MESH
        )

    def wait_for(ref, sem):
        pltpu.make_async_copy(ref, ref, sem).wait()

    def w_step(kind, j, k):
        made = []
        for c in range(1 if k == 0 else 2):
            at = at_rows(kind, low_of(kind, c, k + 1), span(kind, k + 1))
            ref = w_all.at[zflip(j), at, slice(None) if k == 0 else lanes[c]]
            made.append(remote(ref, ref, w_s.at[kind, k], w_r.at[kind, j, k], dp=flip(p, orders[c][k])))
        return made

    def w_sources(kind, j):
        made = []
        for c in range(2):
            ref = w_all.at[t, at_rows(kind, low_of(kind, c, nb), span(kind, nb)), lanes[c]]
            made.append(remote(ref, ref, w_s.at[kind, nb], w_r.at[kind, j, nb], tensor=zflip(j)))
        return made

    def w_wait(kind, j, k):
        k_ = nb if k == halves[kind] else k
        wait_for(w_all.at[0, pl.ds(0, span(kind, k + 1))], w_r.at[kind, j, k_])

    def w_forward(kind, j, k):
        w_wait(kind, j, k + 1)
        for copy in w_step(kind, j, k):
            copy.start()

    def w_top(kind, *js):
        for j in js:
            w_forward(kind, j, halves[kind] - 1)

    def w_mid(kind, *js):
        for k in range(halves[kind] - 2, 0, -1):
            for j in js:
                w_forward(kind, j, k)

    def w_end(kind, *js):
        for j in js:
            w_forward(kind, j, 0)

    def r_step(kind, j, k):
        s = zflip(j)
        base = sum(span(i, k + 1) for i in range(kind))
        made = []
        for c in range(1 if k == 0 else 2):
            low = low_of(kind, c, k)
            if k < halves[kind]:
                low = low + (1 - bit_of(p, orders[c][k])) * span(kind, k + 1)
            which = slice(None) if k == 0 else lanes[c]
            made.append(
                remote(
                    grad.at[s, at_rows(kind, low, span(kind, k + 1)), which],
                    stage_bufs[k].at[j, pl.ds(base, span(kind, k + 1)), which],
                    r_s.at[kind, k] if k < halves[kind] else x_s.at[kind, j, k],
                    r_r.at[kind, j, k],
                    dp=flip(p, orders[c][k]),
                )
            )
        return made

    def r_start(kind, j, k):
        for copy in r_step(kind, j, k):
            copy.start()

    def r_finish(kind, j, k):
        s = zflip(j)
        buf = stage_bufs[k]
        base = sum(span(i, k + 1) for i in range(kind))
        n = span(kind, k + 1)
        here = stage_bufs[k].at[j, pl.ds(base, n), :]
        if k >= halves[kind]:
            wait_for(here, x_s.at[kind, j, k])
        wait_for(here, r_r.at[kind, j, k])
        piece = min(n, 128)
        for c in range(2):
            low = low_of(kind, c, k + 1)

            def add(i, _):
                at = at_rows(kind, low + i * piece, piece)
                here = pl.ds(pl.multiple_of(base + i * piece, TILE), piece)
                grad[s, at, lanes[c]] = (
                    grad[s, at, lanes[c]].astype(F32) + buf[j, here, lanes[c]].astype(F32)
                ).astype(BF16)
                return 0

            lax.fori_loop(0, n // piece, add, 0)

    def r_z(kind, j):
        s = zflip(j)
        base = sum(span(i, nb) for i in range(kind))
        made = []
        for c in range(2):
            at = at_rows(kind, low_of(kind, c, nb), span(kind, nb))
            made.append(
                remote(
                    grad.at[s, at, lanes[c]],
                    zbuf.at[j, pl.ds(base, span(kind, nb)), lanes[c]],
                    r_s.at[kind, nb],
                    r_r.at[kind, j, nb],
                    tensor=s,
                )
            )
        return made

    def r_out(kind, j):
        for copy in r_z(kind, j):
            copy.start()

    def r_total(kind):
        base = sum(span(i, nb) for i in range(kind))
        n = span(kind, nb)
        for j in range(1, blocks):
            wait_for(zbuf.at[j, pl.ds(base, n), :], r_r.at[kind, j, nb])
        for c in range(2):
            at = at_rows(kind, low_of(kind, c, nb), n)
            total = grad[t, at, lanes[c]].astype(F32)
            for j in range(1, blocks):
                total = total + zbuf[j, pl.ds(base, n), lanes[c]].astype(F32)
            fin[at, lanes[c]] = total.astype(BF16)

    def a_step(kind, k):
        made = []
        for c in range(1 if k == 0 else 2):
            at = at_rows(kind, low_of(kind, c, k + 1), span(kind, k + 1))
            ref = fin.at[at, slice(None) if k == 0 else lanes[c]]
            made.append(remote(ref, ref, a_s.at[kind, k], a_r.at[kind, k], dp=flip(p, orders[c][k])))
        return made

    def a_start(kind, k):
        for copy in a_step(kind, k):
            copy.start()

    def a_wait(kind, k):
        wait_for(fin.at[pl.ds(0, span(kind, k + 1)), :], a_r.at[kind, k])

    def r_middle(kind, j):
        for k in range(1, nb - 1):
            r_finish(kind, j, k)
            r_start(kind, j, k + 1)

    def r_first(kind, j):
        r_finish(kind, j, 0)
        r_start(kind, j, 1)

    def r_last(kind, j):
        r_finish(kind, j, nb - 1)
        if isinstance(j, int):
            if j > 0:
                r_out(kind, j)
        else:
            pl.when(j > 0)(lambda: r_out(kind, j))

    def a_first(kind):
        r_total(kind)
        a_start(kind, halves[kind] - 1)

    def a_mid(kind):
        for k in range(halves[kind] - 2, 0, -1):
            a_wait(kind, k + 1)
            a_start(kind, k)

    def a_end(kind):
        a_wait(kind, 1)
        a_start(kind, 0)

    groups = bit_groups(nb)

    def s_start(g):
        bits = groups[g]
        for r in range(1, 1 << len(bits)):
            dp_, tensor_ = p, t
            for i, b in enumerate(bits):
                if r >> i & 1:
                    dp_, tensor_ = (flip(dp_, b), tensor_) if b < nb else (dp_, flip(tensor_, b - nb))
            dev = {"dp": dp_} if bits[0] < nb else {"tensor": tensor_}
            remote(ssum.at[g], sgot.at[g, r - 1], s_s.at[g], s_r.at[g, r - 1], **dev).start()

    def s_next(g):
        n = (1 << len(groups[g])) - 1
        for r in range(n):
            wait_for(sgot.at[g, r], s_r.at[g, r])
        v = ssum[g] + sgot[g, 0]
        if n == 3:
            v = v + (sgot[g, 1] + sgot[g, 2])
        ssum[g + 1] = v
        if g + 1 < len(groups):
            s_start(g + 1)

    def local(src, dst_, i):
        return pltpu.make_async_copy(src, dst_, lsem.at[i])

    loads = [
        local(win_hbm, win, 0),
        local(x_hbm, dproj.at[0], 1),
        local(cot_hbm, dproj.at[1], 2),
        local(wout_hbm, w_all.at[t, pl.ds(o_out, ch), :], 3),
        local(wup_hbm, w_all.at[t, pl.ds(o_up, ff), :], 4),
        local(wdown_hbm, w_all.at[t, pl.ds(o_down, ff), :], 5),
    ]
    for copy in loads:
        copy.start()
    frecv[...] = jnp.zeros_like(frecv)
    brecv[...] = jnp.zeros_like(brecv)
    halo[...] = jnp.zeros_like(halo)
    cb[0, pl.ds(0, 4), :] = conv_ref[...]
    cb[0, pl.ds(4, 1), :] = bias_ref[...]
    barrier = pltpu.get_barrier_semaphore()
    for b in range(nb):
        pl.semaphore_signal(barrier, inc=1, device_id={"dp": flip(p, b)}, device_id_type=MESH)
    for j in range(1, blocks):
        pl.semaphore_signal(barrier, inc=1, device_id={"tensor": zflip(j)}, device_id_type=MESH)
    pl.semaphore_wait(barrier, nb + blocks - 1)

    def c_copy(j):
        return remote(cb.at[0], cb.at[j], c_s.at[0], c_r.at[j], tensor=zflip(j))

    hcopy = remote(x_hbm.at[pl.ds(rows - 16, 16), :], halo, h_s.at[0], h_r.at[0], tensor=partner)
    pl.when(t == 2)(hcopy.start)
    for j in range(1, blocks):
        c_copy(j).start()
    loads[0].wait()

    piece = span(IN, nb)

    def part(c, start):
        w_all[t, at_rows(IN, start, piece), lanes[c]] = win[pl.ds(start, piece), c, :]

    for c in range(2):
        part(c, low_of(IN, c, nb))
    for j in range(1, blocks):
        for copy in w_sources(IN, j):
            copy.start()

    def other_part(i, _):
        for c in range(2):
            part(c, lax.rem(low_of(IN, c, nb) + (i + 1) * piece, d))
        return 0

    lax.fori_loop(0, d // piece - 1, other_part, 0)
    loads[1].wait()

    nlane = d // LANES

    def spread(ref):
        for seg in range(SEGS):
            v = ref[pl.ds(seg * steps, steps), :].astype(F32)
            for i in range(nlane):
                perm[i, pl.ds(seg, steps, stride=SEGS), :] = v[:, i * LANES : (i + 1) * LANES]

    def gather(ref):
        for seg in range(SEGS):
            for i in range(nlane):
                v = perm[i, pl.ds(seg, steps, stride=SEGS), :]
                ref[pl.ds(seg * steps, steps), i * LANES : (i + 1) * LANES] = v.astype(ref.dtype)

    def perm_rows(at):
        return jnp.concatenate([perm[i, pl.ds(at, CHUNK), :] for i in range(nlane)], axis=1)

    def put_perm(at, v):
        for i in range(nlane):
            perm[i, pl.ds(at, CHUNK), :] = v[:, i * LANES : (i + 1) * LANES]

    spread(dproj.at[0])
    limit = jnp.where(
        t == 0,
        short_ref[0],
        jnp.where(t == 1, short_ref[1], jnp.where(t == 2, long_ref[0], long_ref[0] - rows)),
    )

    def norm_rows(r, _):
        at = pl.multiple_of(r * CHUNK, CHUNK)
        xv = perm_rows(at)
        xp[pl.ds(at, CHUNK), :] = xv.astype(BF16)
        fv = xv * scale_of(xv) * g1_ref[...]
        lhs[pl.ds(at, CHUNK), :] = fv.astype(BF16)
        first_t[:, pl.ds(at, CHUNK)] = fv.T.astype(BF16)
        return 0

    lax.fori_loop(0, nchunk, norm_rows, 0)
    loads[2].wait()
    spread(dproj.at[1])

    def dout_rows(r, _):
        at = pl.multiple_of(r * CHUNK, CHUNK)
        place = at + lax.broadcasted_iota(jnp.int32, (CHUNK, d), 0)
        pos = lax.rem(place, SEGS) * steps + place // SEGS
        dv = jnp.where(pos < limit, perm_rows(at), 0.0)
        dout[pl.ds(at, CHUNK), :] = dv.astype(BF16)
        dout_t[:, pl.ds(at, CHUNK)] = dv.T.astype(BF16)
        return 0

    lax.fori_loop(0, nchunk, dout_rows, 0)
    seg_id = lax.broadcasted_iota(jnp.int32, (SEGS, ch), 0)
    has_prev = jnp.where(t == 3, 1.0, 0.0).astype(F32)
    has_next = jnp.where(t == 2, 1.0, 0.0).astype(F32)

    def forward_block(j, _):
        s_ = zflip(j)

        @pl.when(j == 1)
        def _():
            w_top(IN, 3)
            w_mid(IN, 2)
            w_end(IN, 1)
            w_mid(IN, 3)

        @pl.when(j > 0)
        def _():
            c_copy(j).wait_recv()
            w_wait(IN, j, 0)

        def project(r, _):
            at = pl.multiple_of(r * WIDE, WIDE)
            v = dot(lhs[pl.ds(at, WIDE), :], w_all[s_, pl.ds(o_in, d), :])
            bufa[pl.ds(at, WIDE), :ch] = v[:, :ch]
            cand[j, pl.ds(at + 3 * SEGS, WIDE), :] = v[:, ch:]

            @pl.when((j == 0) & (r == 0))
            def _():
                w_top(IN, 1)

            return 0

        lax.fori_loop(0, rows // WIDE, project, 0)

        @pl.when(j == 0)
        def _():
            pl.when(t == 3)(hcopy.wait_recv)
            hv = halo[...].astype(F32)
            edge_rows[...] = (hv * scale_of(hv) * g1_ref[...]).astype(BF16)

        @pl.when(j == 1)
        def _():
            w_end(IN, 2)

        @pl.when(j == 2)
        def _():
            w_end(IN, 3)

        @pl.when(j == 3)
        def _():
            w_top(FF, 2)

        ph = dot(edge_rows[...], w_all[s_, pl.ds(o_in, d), ch:])
        for back in range(3):
            last = cand[j, pl.ds((steps + back) * SEGS, SEGS), :]
            rolled = pltpu.roll(last, 1, 0)
            edge = ph[13 + back : 14 + back, :] * has_prev
            cand[j, pl.ds(back * SEGS, SEGS), :] = jnp.where(seg_id == 0, edge, rolled)
        k_ = [jnp.broadcast_to(cb[j, pl.ds(i, 1), :], (SEGS, ch)) for i in range(4)]
        bias = jnp.broadcast_to(cb[j, pl.ds(4, 1), :], (SEGS, ch))

        def step4(i, carry):
            s, q_ = carry
            for q in range(4):
                at = pl.multiple_of((i * 4 + q) * SEGS, SEGS)
                u = sigmoid(bufa[pl.ds(at, SEGS), :ch] + bias)
                f = k_[0] * cand[j, pl.ds(at + 3 * SEGS, SEGS), :]
                for lag in range(1, 4):
                    f = f + k_[lag] * cand[j, pl.ds(at + (3 - lag) * SEGS, SEGS), :]
                upd[j, pl.ds(at, SEGS), :] = u
                dst[j, pl.ds(at, SEGS), :] = f
                a = 1.0 - u
                s = a * s + u * f
                q_ = a * q_
            return s, q_

        half = lax.fori_loop(
            0, steps // 8, step4, (jnp.zeros((SEGS, ch), F32), jnp.ones((SEGS, ch), F32))
        )

        @pl.when(j == 0)
        def _():
            w_top(IN, 2)
            loads[3].wait()
            for i in (2, 3, 1):
                for copy in w_sources(OUT, i):
                    copy.start()

        s, q_ = lax.fori_loop(steps // 8, steps // 4, step4, half)
        ends[0, j] = s
        ends[1, j] = q_
        fsend[j] = jnp.broadcast_to(forward_chain(j, jnp.zeros((1, ch), F32)), (8, ch))
        pl.when(t == 2)(f_copy(j).start)

        @pl.when(j == 0)
        def _():
            w_mid(IN, 1)
            loads[4].wait()
            loads[5].wait()
            for i in (2, 3, 1):
                for copy in w_sources(FF, i):
                    copy.start()

        @pl.when(j == 1)
        def _():
            w_top(OUT, 1, 2, 3)

        @pl.when(j == 2)
        def _():
            w_mid(OUT, 1, 2, 3)

        return 0

    def forward_chain(j, start):
        run = start
        for seg in range(SEGS):
            st[j, pl.ds(seg, 1), :] = run
            run = ends[0, j, pl.ds(seg, 1), :] + ends[1, j, pl.ds(seg, 1), :] * run
        return run

    def f_copy(j):
        there = flip(j, 0)
        return remote(fsend.at[j], frecv.at[there], f_s.at[0], f_r.at[there], tensor=partner)

    lax.fori_loop(0, blocks, forward_block, 0)
    w_top(FF, 3)

    def forward_fix(i, _):
        b = flip(i, 0)

        @pl.when(t == 3)
        def _():
            wait_for(frecv.at[b], f_r.at[b])

        forward_chain(b, frecv[b, pl.ds(0, 1), :] * has_prev)

        def step8(i, s):
            for q in range(8):
                at = pl.multiple_of((i * 8 + q) * SEGS, SEGS)
                u = upd[b, pl.ds(at, SEGS), :]
                s = (1.0 - u) * s + u * dst[b, pl.ds(at, SEGS), :]
                st[b, pl.ds(at + SEGS, SEGS), :] = s
            return s

        lax.fori_loop(0, steps // 8, step8, st[b, pl.ds(0, SEGS), :])

        @pl.when(i == 1)
        def _():
            w_end(OUT, 1, 2, 3)

        return 0

    lax.fori_loop(0, blocks, forward_fix, 0)
    w_mid(FF, 2)
    for j in range(1, blocks):
        w_wait(OUT, j, 0)
    shards = [zflip(j) for j in range(blocks)]

    def second_rows(r, _):
        at = pl.multiple_of(r * 512, 512)
        m = xp[pl.ds(at, 512), :].astype(F32)
        for j in range(blocks):
            m = m + dot(
                st[j, pl.ds(at + SEGS, 512), :].astype(BF16), w_all[shards[j], pl.ds(o_out, ch), :]
            )
        mid[pl.ds(at, 512), :] = m
        sv = m * scale_of(m) * g2_ref[...]
        lhs[pl.ds(at, 512), :] = sv.astype(BF16)
        second_t[:, pl.ds(at, 512)] = sv.T.astype(BF16)
        bufa[pl.ds(at, 512), :] = m
        bufc[pl.ds(at, 512), :] = jnp.zeros((512, d), F32)
        return 0

    lax.fori_loop(0, rows // 512, second_rows, 0)

    w_mid(FF, 3)
    act, din = dproj.at[1], dproj.at[2]

    def ff_place(i):
        return lax.div(i + 3, 4) * (1 + lax.rem(i, 3))

    def ff_block(i, _):
        j, before, earlier = ff_place(i), ff_place(i - 1), ff_place(i - 2)
        s_ = zflip(j)

        @pl.when(i > 0)
        def _():
            w_wait(FF, j, 0)

        def ff_rows(r, _):
            at = pl.multiple_of(r * 512, 512)
            wu = w_all[s_, pl.ds(o_up, ff), :]
            wd = w_all[s_, pl.ds(o_down, ff), :]
            inner = dot(lhs[pl.ds(at, 512), :], wu)
            da = dot_t(dout[pl.ds(at, 512), :], wd)
            cdf = 0.5 + 0.5 * lax.erf(inner * np.float32(np.sqrt(0.5)))
            pdf = jnp.exp(inner * inner * -0.5) * np.float32(1.0 / np.sqrt(2.0 * np.pi))
            av = (inner * cdf).astype(BF16)
            dv = (da * (cdf + inner * pdf)).astype(BF16)
            act[pl.ds(at, 512), :] = av
            din[pl.ds(at, 512), :] = dv
            bufa[pl.ds(at, 512), :] += dot(av, wd)
            bufc[pl.ds(at, 512), :] += dot_t(dv, wu)

            @pl.when((r == 0) & (i == 0))
            def _():
                w_end(FF, 2)

            @pl.when((r == 1) & (i == 0))
            def _():
                w_top(FF, 1)

            @pl.when((r == 0) & (i == 1))
            def _():
                w_end(FF, 3)

            @pl.when((r == 0) & (i == 1))
            def _():
                w_mid(FF, 1)

            @pl.when((r == 0) & (i == 2))
            def _():
                w_end(FF, 1)

            @pl.when((r == 1) & (i > 0))
            def _():
                r_first(FF, before)

            return 0

        lax.fori_loop(0, rows // 512, ff_rows, 0)

        def ff_grads(r, _):
            at = pl.multiple_of(r * 512, 512)
            grad[s_, pl.ds(o_up + at, 512), :] = dot(second_t[pl.ds(at, 512), :], din[...]).astype(BF16)
            grad[s_, pl.ds(o_down + at, 512), :] = dot(dout_t[pl.ds(at, 512), :], act[...]).astype(BF16)
            return 0

        lax.fori_loop(0, d // 512, ff_grads, 0)
        @pl.when(i > 1)
        def _():
            r_middle(FF, earlier)

        r_start(FF, j, 0)
        return 0

    lax.fori_loop(0, blocks, ff_block, 0)

    def second_back(r, gain):
        at = pl.multiple_of(r * CHUNK, CHUNK)
        put_perm(at, bufa[pl.ds(at, CHUNK), :])
        m = mid[pl.ds(at, CHUNK), :]
        s = scale_of(m)
        dn = bufc[pl.ds(at, CHUNK), :]
        gain = gain + jnp.sum(dn * m * s, axis=0, keepdims=True)
        gd = dn * g2_ref[...]
        dm = dout[pl.ds(at, CHUNK), :].astype(F32) + s * gd - m * (s * s * s * jnp.mean(gd * m, axis=-1, keepdims=True))
        mid[pl.ds(at, CHUNK), :] = dm
        lhs[pl.ds(at, CHUNK), :] = dm.astype(BF16)
        second_t[:, pl.ds(at, CHUNK)] = dm.T.astype(BF16)
        bufc[pl.ds(at, CHUNK), :] = jnp.zeros((CHUNK, d), F32)
        return gain

    gain2 = lax.fori_loop(0, nchunk, second_back, jnp.zeros((1, d), F32))
    ssum[0] = jnp.zeros((16, d), F32)
    ssum[0, pl.ds(1, 1), :] = gain2
    gather(res)
    r_first(FF, 1)

    def backward_block(i, _):
        j = blocks - 1 - i
        s_ = zflip(j)

        def project(r, _):
            at = pl.multiple_of(r * 512, 512)
            dst[j, pl.ds(at, 512), :] = dot_t(lhs[pl.ds(at, 512), :], w_all[s_, pl.ds(o_out, ch), :])
            return 0

        lax.fori_loop(0, rows // 512, project, 0)
        state = st[j, pl.ds(SEGS, rows), :].astype(BF16)
        for half in range(2):
            rr = d // 2
            grad[s_, pl.ds(o_out, ch), half * ch : (half + 1) * ch] = dot(
                second_t[half * rr : (half + 1) * rr, :], state
            ).astype(BF16)
        r_start(OUT, j, 0)

        @pl.when(i == 0)
        def _():
            r_last(FF, 2)
            r_middle(FF, 3)

        @pl.when(i == 1)
        def _():
            r_last(FF, 0)

        @pl.when(i == 2)
        def _():
            r_middle(FF, 1)

        @pl.when(i == 3)
        def _():
            r_last(FF, 3)
            r_middle(OUT, 3)

        def one(step, w, q_):
            at = pl.multiple_of(step * SEGS, SEGS)
            a = 1.0 - upd[j, pl.ds(at, SEGS), :]
            c = dst[j, pl.ds(at, SEGS), :] + w
            return c, a * c, q_ * a

        w, q_ = jnp.zeros((SEGS, ch), F32), jnp.ones((SEGS, ch), F32)
        for step in range(steps - 1, steps - 6, -1):
            _, w, q_ = one(step, w, q_)

        def step8(n, carry):
            w, q_ = carry
            for q in range(8):
                _, w, q_ = one(steps - 6 - (n * 8 + q), w, q_)
            return w, q_

        w, q_ = lax.fori_loop(0, (steps - 8) // 8, step8, (w, q_))
        for step in range(2, -1, -1):
            bends[2 * step, j] = q_
            c, w, q_ = one(step, w, q_)
            bends[2 * step + 1, j] = c
        bends[6, j] = w
        bends[7, j] = q_
        bsend[j, pl.ds(0, 1), :] = backward_chain(j, jnp.zeros((1, ch), F32))
        for step in range(3):
            bsend[j, pl.ds(step + 1, 1), :] = upd[j, pl.ds(step * SEGS, 1), :] * (
                bends[2 * step + 1, j, pl.ds(0, 1), :]
                + bends[2 * step, j, pl.ds(0, 1), :] * ends[0, j, pl.ds(0, 1), :]
            )
        pl.when(t == 3)(b_copy(j).start)

        @pl.when(i > 0)
        def _():
            r_first(OUT, j + 1)

        return 0

    def backward_chain(j, start):
        run = start
        for seg in range(SEGS - 1, -1, -1):
            ends[0, j, pl.ds(seg, 1), :] = run
            run = bends[6, j, pl.ds(seg, 1), :] + bends[7, j, pl.ds(seg, 1), :] * run
        return run

    def b_copy(j):
        there = flip(j, 0)
        return remote(bsend.at[j], brecv.at[there], b_s.at[0], b_r.at[there], tensor=partner)

    lax.fori_loop(0, blocks, backward_block, 0)


    def backward_fix(i, _):
        j = blocks - 1 - i
        s_ = zflip(j)

        @pl.when(t == 2)
        def _():
            wait_for(brecv.at[j], b_r.at[j])

        backward_chain(j, brecv[j, pl.ds(0, 1), :] * has_next)
        w = ends[0, j]
        after = []
        for step in range(3):
            df = upd[j, pl.ds(step * SEGS, SEGS), :] * (bends[2 * step + 1, j] + bends[2 * step, j] * w)
            edge = brecv[j, pl.ds(step + 1, 1), :] * has_next
            after.append(jnp.where(seg_id == SEGS - 1, edge, pltpu.roll(df, SEGS - 1, 0)))
        k_ = [jnp.broadcast_to(cb[j, pl.ds(n, 1), :], (SEGS, ch)) for n in range(4)]
        zero = jnp.zeros((SEGS, ch), F32)

        def pair(n, carry):
            w, d1, d2, d3, c0, c1, c2, k0, k1, k2, k3, gb = carry
            top = steps - 2 - 2 * n
            made = []
            for q in range(2):
                at = pl.multiple_of((top + 1 - q) * SEGS, SEGS)
                u = upd[j, pl.ds(at, SEGS), :]
                c = dst[j, pl.ds(at, SEGS), :] + w
                d0 = c * u
                a = 1.0 - u
                w = a * c
                c3 = cand[j, pl.ds(at, SEGS), :]
                f = k_[0] * c0 + k_[1] * c1 + k_[2] * c2 + k_[3] * c3
                dg = d0 * a * (f - st[j, pl.ds(at, SEGS), :])
                dc = k_[0] * d0 + k_[1] * d1 + k_[2] * d2 + k_[3] * d3
                k0, k1, k2, k3 = k0 + d0 * c0, k1 + d0 * c1, k2 + d0 * c2, k3 + d0 * c3
                gb = gb + dg
                c0, c1, c2 = c1, c2, c3
                d1, d2, d3 = d0, d1, d2
                made.append((dg, dc))
            at = pl.multiple_of(top * SEGS, 2 * SEGS)
            dproj[j, pl.ds(at, 2 * SEGS), :ch] = jnp.concatenate([made[1][0], made[0][0]], axis=0).astype(BF16)
            dproj[j, pl.ds(at, 2 * SEGS), ch:] = jnp.concatenate([made[1][1], made[0][1]], axis=0).astype(BF16)
            return w, d1, d2, d3, c0, c1, c2, k0, k1, k2, k3, gb

        window = [cand[j, pl.ds((steps + 2 - n) * SEGS, SEGS), :] for n in range(3)]
        half = lax.fori_loop(0, steps // 4, pair, (w, *after, *window, zero, zero, zero, zero, zero))

        @pl.when(i == 0)
        def _():
            r_last(FF, 1)
            r_first(OUT, 0)
            r_middle(OUT, 2)

        @pl.when(i == 1)
        def _():
            r_last(OUT, 2)
            r_middle(OUT, 0)

        @pl.when(i == 2)
        def _():
            r_last(OUT, 0)
            a_first(FF)

        @pl.when(i == 3)
        def _():
            r_middle(IN, 3)
            a_first(OUT)

        out = lax.fori_loop(steps // 4, steps // 2, pair, half)
        for n in range(5):
            at = 2 + 2 * n + bit_of(s_, 1)
            ssum[0, pl.ds(at, 1), pl.ds(pl.multiple_of(bit_of(s_, 0) * ch, LANES), ch)] = jnp.sum(
                out[7 + n], axis=0, keepdims=True
            )

        @pl.when(i > 1)
        def _():
            r_first(IN, j + 1)

        def first_grad(r, _):
            at = pl.multiple_of(r * 512, 512)
            grad[s_, pl.ds(o_in + at, 512), :] = dot(first_t[pl.ds(at, 512), :], dproj[j]).astype(BF16)
            return 0

        lax.fori_loop(0, d // 512, first_grad, 0)
        r_start(IN, j, 0)


        @pl.when(i == 0)
        def _():
            r_last(OUT, 3)
            r_middle(OUT, 1)

        @pl.when(i == 1)
        def _():
            r_first(IN, 3)
            r_last(OUT, 1)

        @pl.when(i == 3)
        def _():
            r_middle(IN, 2)

        return 0

    lax.fori_loop(0, blocks, backward_fix, 0)

    def first_back(r):
        at = r * 512
        v = dot_t(dproj[0, pl.ds(at, 512), :], w_all[shards[0], pl.ds(o_in, d), :])
        for j in range(1, blocks):
            v = v + dot_t(dproj[j, pl.ds(at, 512), :], w_all[shards[j], pl.ds(o_in, d), :])
        bufc[pl.ds(at, 512), :] = v

    first_back(0)
    r_last(IN, 3)
    r_first(IN, 0)
    for r in range(1, rows // 512):
        first_back(r)
    r_middle(IN, 1)
    r_last(IN, 2)

    def first_norm_back(r, gain):
        at = pl.multiple_of(r * CHUNK, CHUNK)
        m = xp[pl.ds(at, CHUNK), :].astype(F32)
        s = scale_of(m)
        dn = bufc[pl.ds(at, CHUNK), :]
        gain = gain + jnp.sum(dn * m * s, axis=0, keepdims=True)
        gd = dn * g1_ref[...]
        dv = s * gd - m * (s * s * s * jnp.mean(gd * m, axis=-1, keepdims=True))
        put_perm(at, mid[pl.ds(at, CHUNK), :] + dv)
        return gain

    ssum[0, pl.ds(0, 1), :] = lax.fori_loop(0, nchunk, first_norm_back, jnp.zeros((1, d), F32))
    s_start(0)
    r_middle(IN, 0)
    r_last(IN, 1)
    s_next(0)
    a_mid(FF)
    a_mid(OUT)
    gather(mid)
    r_last(IN, 0)
    a_first(IN)
    a_end(FF)
    for g in range(1, len(groups) - 1):
        s_next(g)
    a_mid(IN)
    a_end(OUT)
    a_end(IN)
    s_next(len(groups) - 1)
    gains_ref[...] = ssum[len(groups), pl.ds(0, 8), :]
    for n in range(5):
        at = 2 + 2 * n + bit_of(t, 1)
        chan_ref[pl.ds(n, 1), :] = ssum[
            len(groups), pl.ds(at, 1), pl.ds(pl.multiple_of(bit_of(t, 0) * ch, LANES), ch)
        ]
    a_wait(FF, 0)
    a_wait(OUT, 0)
    a_wait(IN, 0)

    pl.when(t == 2)(hcopy.wait_send)
    wait_for(cb.at[pl.ds(0, blocks - 1)], c_s.at[0])
    pl.when(t == 2)(lambda: wait_for(fsend, f_s.at[0]))
    pl.when(t == 3)(lambda: wait_for(bsend, b_s.at[0]))
    for kind in (IN, OUT, FF):
        for k in range(halves[kind]):
            n = span(kind, k + 1)
            wait_for(w_all.at[0, pl.ds(0, (blocks - 1) * n), :], w_s.at[kind, k])
            wait_for(grad.at[pl.ds(0, 2), pl.ds(0, blocks // 2 * n), :], r_s.at[kind, k])
            wait_for(fin.at[pl.ds(0, n), :], a_s.at[kind, k])
        n = span(kind, nb)
        wait_for(w_all.at[0, pl.ds(0, (blocks - 1) * n), :], w_s.at[kind, nb])
        wait_for(w_all.at[0, pl.ds(0, (blocks - 1) * n), :], r_s.at[kind, nb])
    for g in range(len(groups)):
        wait_for(sgot.at[g, pl.ds(0, (1 << len(groups[g])) - 1)], s_s.at[g])


def finish_kernel(
    dims, gains, chan, res, gx, fin, res_out, gx_out, gin_o, gout_o, gup_o, gdown_o, gnorm, gmlp, taps, gbias,
    gin, gout, gup, gdown, sem,
):
    rows, d, ch, ff = dims
    outs = []

    def put(src, dst):
        copy = pltpu.make_async_copy(src, dst, sem.at[len(outs)])
        copy.start()
        outs.append(copy)

    put(gx, gx_out)
    put(res, res_out)
    gup[...] = fin[pl.ds(d + ch, d), :].astype(F32)
    put(gup, gup_o)
    gin[:, 0, :] = fin[pl.ds(0, d), :ch].astype(F32)
    gin[:, 1, :] = fin[pl.ds(0, d), ch:].astype(F32)
    put(gin, gin_o)
    gdown[...] = fin[pl.ds(d + ch + ff, d), :].astype(F32).T
    put(gdown, gdown_o)
    gout[:, : d // 2] = fin[pl.ds(d, ch), :ch].astype(F32).T
    gout[:, d // 2 :] = fin[pl.ds(d, ch), ch:].astype(F32).T
    put(gout, gout_o)
    gnorm[...] = gains[pl.ds(0, 1), :]
    gmlp[...] = gains[pl.ds(1, 1), :]
    taps[...] = chan[pl.ds(0, 4), :]
    gbias[...] = chan[pl.ds(4, 1), :]
    for copy in outs:
        copy.wait()


def per_device(
    inputs,
    norm_gain,
    in_weight,
    conv_kernel,
    gate_bias,
    out_weight,
    mlp_gain,
    up_weight,
    down_weight,
    short_lengths,
    long_lengths,
    cotangent,
):
    rows, d = inputs.shape
    ch = in_weight.shape[2]
    ff = up_weight.shape[1]
    blocks = lax.axis_size("tensor")
    dp = lax.axis_size("dp")
    nb = log2(dp)
    assert dp == 1 << nb and blocks == 4 and rows == LSHORT and 2 * rows == LLONG
    assert 2 * ch == d and short_lengths.shape == (2,) and long_lengths.shape == (1,)
    sizes = (d, ch, 2 * ff)
    total = sum(sizes)
    halves = tuple(min(nb, log2(r // TILE)) for r in sizes)

    def span_all(k):
        return sum(r >> min(k, h) for r, h in zip(sizes, halves))

    ngroups = len(bit_groups(nb))
    vm = pl.BlockSpec(memory_space=pltpu.VMEM)
    sm = pl.BlockSpec(memory_space=pltpu.SMEM)
    hb = pl.BlockSpec(memory_space=pl.ANY)
    dma = pltpu.SemaphoreType.DMA
    res, gx, fin, gains, chan = pl.pallas_call(
        functools.partial(block_kernel, (rows, d, blocks, ch, ff, nb)),
        out_shape=(
            pltpu.VMEM((rows, d), BF16),
            pltpu.VMEM((rows, d), F32),
            pltpu.VMEM((total, d), BF16),
            pltpu.VMEM((8, d), F32),
            pltpu.VMEM((8, ch), F32),
        ),
        in_specs=[sm, sm, hb, hb, vm, vm, vm, vm, hb, hb, hb, hb],
        out_specs=(vm,) * 5,
        scratch_shapes=[
            pltpu.VMEM((blocks, total, d), BF16),
            pltpu.VMEM((blocks, total, d), BF16),
            pltpu.VMEM((d, 2, ch), BF16),
            pltpu.VMEM((rows, d), BF16),
            pltpu.VMEM((blocks, rows + 3 * SEGS, ch), F32),
            pltpu.VMEM((blocks, rows, ch), F32),
            pltpu.VMEM((blocks, rows + SEGS, ch), F32),
            pltpu.VMEM((blocks, rows, ch), F32),
            pltpu.VMEM((16, d), BF16),
            pltpu.VMEM((d, rows), BF16),
            pltpu.VMEM((d, rows), BF16),
            pltpu.VMEM((rows, d), BF16),
            pltpu.VMEM((d, rows), BF16),
            pltpu.VMEM((rows, d), F32),
            pltpu.VMEM((rows, d), F32),
            pltpu.VMEM((blocks, rows, d), BF16),
            pltpu.VMEM((d // LANES, rows, LANES), F32),
            pltpu.VMEM((16, d), BF16),
            pltpu.VMEM((blocks, 8, ch), F32),
            pltpu.VMEM((2, blocks, SEGS, ch), F32),
            pltpu.VMEM((8, blocks, SEGS, ch), F32),
            pltpu.VMEM((blocks, 8, ch), F32),
            pltpu.VMEM((blocks, 8, ch), F32),
            pltpu.VMEM((blocks, 8, ch), F32),
            pltpu.VMEM((blocks, 8, ch), F32),
            pltpu.VMEM((blocks, span_all(nb), d), BF16),
            pltpu.VMEM((ngroups + 1, 16, d), F32),
            pltpu.VMEM((ngroups, 3, 16, d), F32),
            dma((6,)),
            dma((1,)),
            dma((blocks,)),
            dma((1,)),
            dma((blocks,)),
            dma((1,)),
            dma((blocks,)),
            dma((1,)),
            dma((1,)),
            dma((3, nb + 1)),
            dma((3, blocks, nb + 1)),
            dma((3, nb + 1)),
            dma((3, blocks, nb + 1)),
            dma((3, blocks, nb)),
            dma((3, nb)),
            dma((3, nb)),
            dma((ngroups,)),
            dma((ngroups, 3)),
        ]
        + [pltpu.VMEM((blocks, span_all(k + 1), d), BF16) for k in range(nb)],
        compiler_params=pltpu.CompilerParams(
            collective_id=0, has_side_effects=True, vmem_limit_bytes=59 << 20
        ),
        name="block",
    )(
        short_lengths,
        long_lengths,
        inputs,
        cotangent,
        norm_gain[None],
        mlp_gain[None],
        conv_kernel,
        gate_bias[None],
        in_weight,
        out_weight,
        up_weight,
        down_weight,
    )
    result, grad_inputs, gin, gout, gup, gdown, gnorm, gmlp, taps, gbias = pl.pallas_call(
        functools.partial(finish_kernel, (rows, d, ch, ff)),
        out_shape=(
            jax.ShapeDtypeStruct((rows, d), BF16),
            jax.ShapeDtypeStruct((rows, d), F32),
            jax.ShapeDtypeStruct((d, 2, ch), F32),
            jax.ShapeDtypeStruct((ch, d), F32),
            jax.ShapeDtypeStruct((d, ff), F32),
            jax.ShapeDtypeStruct((ff, d), F32),
            jax.ShapeDtypeStruct((1, d), F32),
            jax.ShapeDtypeStruct((1, d), F32),
            jax.ShapeDtypeStruct((4, ch), F32),
            jax.ShapeDtypeStruct((1, ch), F32),
        ),
        in_specs=[vm] * 5,
        out_specs=(hb,) * 6 + (vm,) * 4,
        scratch_shapes=[
            pltpu.VMEM((d, 2, ch), F32),
            pltpu.VMEM((ch, d), F32),
            pltpu.VMEM((d, ff), F32),
            pltpu.VMEM((ff, d), F32),
            dma((6,)),
        ],
        compiler_params=pltpu.CompilerParams(vmem_limit_bytes=32 << 20),
        name="finish",
    )(gains, chan, res, gx, fin)
    return (result, grad_inputs, gnorm[0], gin, taps, gbias[0], gout, gmlp[0], gup, gdown)


def solution(mesh):
    placed = (
        P(("dp", "tensor"), None),
        P(),
        P(None, None, "tensor"),
        P(None, "tensor"),
        P("tensor"),
        P("tensor", None),
        P(),
        P(None, "tensor"),
        P("tensor", None),
        P("dp"),
        P("dp"),
        P(("dp", "tensor"), None),
    )
    return jax.shard_map(
        per_device,
        mesh=mesh,
        in_specs=placed,
        out_specs=(
            P(("dp", "tensor"), None),
            P(("dp", "tensor"), None),
            P(),
            P(None, None, "tensor"),
            P(None, "tensor"),
            P("tensor"),
            P("tensor", None),
            P(),
            P(None, "tensor"),
            P("tensor", None),
        ),
        check_vma=False,
    )
```

```python
import functools

import jax
import jax.numpy as jnp
import numpy as np
from jax import lax
from jax.experimental import pallas as pl
from jax.experimental.pallas import tpu as pltpu
from jax.sharding import PartitionSpec as P

LSHORT = 1024
LLONG = 2048
SEGS = 8
EPS = 1e-05
CHUNK = 256
WIDE = 1024
TILE = 16
LANES = 128
F32 = jnp.float32
BF16 = jnp.bfloat16
MESH = pl.DeviceIdType.MESH
IN, OUT, FF = 0, 1, 2


def dot(a, b):
    return jnp.dot(a, b, preferred_element_type=F32)


def dot_t(a, b):
    return lax.dot_general(a, b, (((1,), (1,)), ((), ())), preferred_element_type=F32)


def scale_of(v):
    return lax.rsqrt(jnp.mean(v * v, axis=-1, keepdims=True) + EPS)


def sigmoid(v):
    return 1.0 / (1.0 + jnp.exp(-v))


def bit_of(v, bit):
    return lax.rem(lax.div(v, 1 << bit), 2)


def flip(v, bit):
    return v + (1 << bit) * (1 - 2 * bit_of(v, bit))


def log2(n):
    return int(n).bit_length() - 1


def bit_groups(nb):
    groups = [(0,)] + [tuple(range(b, min(b + 2, nb))) for b in range(1, nb, 2)]
    return groups + [(nb, nb + 1)]


def block_kernel(
    dims,
    short_ref,
    long_ref,
    x_hbm,
    cot_hbm,
    g1_hbm,
    g2_hbm,
    conv_hbm,
    bias_hbm,
    win_hbm,
    wout_hbm,
    wup_hbm,
    wdown_hbm,
    res,
    mid,
    fin,
    gains_ref,
    chan_ref,
    g1_ref,
    g2_ref,
    w_all,
    grad,
    win,
    xp,
    cand,
    upd,
    st,
    dst,
    edge_rows,
    first_t,
    second_t,
    dout,
    dout_t,
    bufa,
    bufc,
    dproj,
    perm,
    halo,
    cb,
    ends,
    bends,
    fsend,
    frecv,
    bsend,
    brecv,
    zbuf,
    ssum,
    sgot,
    lsem,
    c_s,
    c_r,
    f_s,
    f_r,
    b_s,
    b_r,
    h_s,
    h_r,
    w_s,
    w_r,
    r_s,
    r_r,
    x_s,
    a_s,
    a_r,
    s_s,
    s_r,
    *stage_bufs,
):
    rows, d, blocks, ch, ff, nb = dims
    steps = rows // SEGS
    t = lax.axis_index("tensor")
    p = lax.axis_index("dp")
    partner = flip(t, 0)
    nchunk = rows // CHUNK
    offs = (0, d, d + ch)
    sizes = (d, ch, 2 * ff)
    o_in, o_out, o_up, o_down = 0, d, d + ch, d + ch + ff
    halves = tuple(min(nb, log2(r // TILE)) for r in sizes)
    half_d = d // 2
    lanes = (pl.ds(0, half_d), pl.ds(half_d, half_d))
    orders = ((0,) + tuple(range(nb - 1, 0, -1)), tuple(range(nb)))
    lhs = dproj.at[3]

    def zflip(j):
        b0, b1 = lax.rem(j, 2), lax.div(j, 2)
        return t + b0 * (1 - 2 * bit_of(t, 0)) + b1 * (2 - 4 * bit_of(t, 1))

    def low_of(kind, c, k):
        low = 0
        for i in range(min(k, halves[kind])):
            low = low + bit_of(p, orders[c][i]) * (sizes[kind] >> (i + 1))
        return low

    def span(kind, k):
        return sizes[kind] >> min(k, halves[kind])

    def at_rows(kind, start, n):
        return pl.ds(pl.multiple_of(offs[kind] + start, TILE), n)

    def stage_rows(kind, k):
        base = sum(span(i, k + 1) for i in range(kind))
        return pl.ds(base, span(kind, k + 1))

    def remote(src, dst_, ss, rs, **dev):
        return pltpu.make_async_remote_copy(
            src_ref=src, dst_ref=dst_, send_sem=ss, recv_sem=rs, device_id=dev, device_id_type=MESH
        )

    def wait_for(ref, sem):
        pltpu.make_async_copy(ref, ref, sem).wait()

    def w_step(kind, j, k):
        made = []
        for c in range(1 if k == 0 else 2):
            at = at_rows(kind, low_of(kind, c, k + 1), span(kind, k + 1))
            ref = w_all.at[zflip(j), at, slice(None) if k == 0 else lanes[c]]
            made.append(remote(ref, ref, w_s.at[kind, k], w_r.at[kind, j, k], dp=flip(p, orders[c][k])))
        return made

    def w_sources(kind, j):
        made = []
        for c in range(2):
            ref = w_all.at[t, at_rows(kind, low_of(kind, c, nb), span(kind, nb)), lanes[c]]
            made.append(remote(ref, ref, w_s.at[kind, nb], w_r.at[kind, j, nb], tensor=zflip(j)))
        return made

    def w_wait(kind, j, k):
        k_ = nb if k == halves[kind] else k
        wait_for(w_all.at[0, pl.ds(0, span(kind, k + 1))], w_r.at[kind, j, k_])

    def w_forward(kind, j, k):
        w_wait(kind, j, k + 1)
        for copy in w_step(kind, j, k):
            copy.start()

    def w_top(kind, *js):
        for j in js:
            w_forward(kind, j, halves[kind] - 1)

    def w_mid(kind, *js):
        for k in range(halves[kind] - 2, 0, -1):
            for j in js:
                w_forward(kind, j, k)

    def w_end(kind, *js):
        for j in js:
            w_forward(kind, j, 0)

    def r_step(kind, j, k):
        s = zflip(j)
        base = sum(span(i, k + 1) for i in range(kind))
        made = []
        for c in range(1 if k == 0 else 2):
            low = low_of(kind, c, k)
            if k < halves[kind]:
                low = low + (1 - bit_of(p, orders[c][k])) * span(kind, k + 1)
            which = slice(None) if k == 0 else lanes[c]
            made.append(
                remote(
                    grad.at[s, at_rows(kind, low, span(kind, k + 1)), which],
                    stage_bufs[k].at[j, pl.ds(base, span(kind, k + 1)), which],
                    r_s.at[kind, k] if k < halves[kind] else x_s.at[kind, j, k],
                    r_r.at[kind, j, k],
                    dp=flip(p, orders[c][k]),
                )
            )
        return made

    def r_start(kind, j, k):
        for copy in r_step(kind, j, k):
            copy.start()

    def r_finish(kind, j, k):
        s = zflip(j)
        buf = stage_bufs[k]
        base = sum(span(i, k + 1) for i in range(kind))
        n = span(kind, k + 1)
        here = stage_bufs[k].at[j, pl.ds(base, n), :]
        if k >= halves[kind]:
            wait_for(here, x_s.at[kind, j, k])
        wait_for(here, r_r.at[kind, j, k])
        piece = min(n, 128)
        for c in range(2):
            low = low_of(kind, c, k + 1)

            def add(i, _):
                at = at_rows(kind, low + i * piece, piece)
                here = pl.ds(pl.multiple_of(base + i * piece, TILE), piece)
                grad[s, at, lanes[c]] += buf[j, here, lanes[c]]
                return 0

            lax.fori_loop(0, n // piece, add, 0)

    def r_z(kind, j):
        s = zflip(j)
        base = sum(span(i, nb) for i in range(kind))
        made = []
        for c in range(2):
            at = at_rows(kind, low_of(kind, c, nb), span(kind, nb))
            made.append(
                remote(
                    grad.at[s, at, lanes[c]],
                    zbuf.at[j, pl.ds(base, span(kind, nb)), lanes[c]],
                    r_s.at[kind, nb],
                    r_r.at[kind, j, nb],
                    tensor=s,
                )
            )
        return made

    def r_out(kind, j):
        for copy in r_z(kind, j):
            copy.start()

    def r_total(kind):
        base = sum(span(i, nb) for i in range(kind))
        n = span(kind, nb)
        for j in range(1, blocks):
            wait_for(zbuf.at[j, pl.ds(base, n), :], r_r.at[kind, j, nb])
        for c in range(2):
            at = at_rows(kind, low_of(kind, c, nb), n)
            total = grad[t, at, lanes[c]].astype(F32)
            for j in range(1, blocks):
                total = total + zbuf[j, pl.ds(base, n), lanes[c]].astype(F32)
            fin[at, lanes[c]] = total.astype(BF16)

    def a_step(kind, k):
        made = []
        for c in range(1 if k == 0 else 2):
            at = at_rows(kind, low_of(kind, c, k + 1), span(kind, k + 1))
            ref = fin.at[at, slice(None) if k == 0 else lanes[c]]
            made.append(remote(ref, ref, a_s.at[kind, k], a_r.at[kind, k], dp=flip(p, orders[c][k])))
        return made

    def a_start(kind, k):
        for copy in a_step(kind, k):
            copy.start()

    def a_wait(kind, k):
        wait_for(fin.at[pl.ds(0, span(kind, k + 1)), :], a_r.at[kind, k])

    def r_middle(kind, j):
        for k in range(1, nb - 1):
            r_finish(kind, j, k)
            r_start(kind, j, k + 1)

    def r_first(kind, j):
        r_finish(kind, j, 0)
        r_start(kind, j, 1)

    def r_last(kind, j):
        r_finish(kind, j, nb - 1)
        if isinstance(j, int):
            if j > 0:
                r_out(kind, j)
        else:
            pl.when(j > 0)(lambda: r_out(kind, j))

    def a_first(kind):
        r_total(kind)
        a_start(kind, halves[kind] - 1)

    def a_mid(kind):
        for k in range(halves[kind] - 2, 0, -1):
            a_wait(kind, k + 1)
            a_start(kind, k)

    def a_end(kind):
        a_wait(kind, 1)
        a_start(kind, 0)

    groups = bit_groups(nb)

    def s_start(g):
        bits = groups[g]
        for r in range(1, 1 << len(bits)):
            dp_, tensor_ = p, t
            for i, b in enumerate(bits):
                if r >> i & 1:
                    dp_, tensor_ = (flip(dp_, b), tensor_) if b < nb else (dp_, flip(tensor_, b - nb))
            dev = {"dp": dp_} if bits[0] < nb else {"tensor": tensor_}
            remote(ssum.at[g], sgot.at[g, r - 1], s_s.at[g], s_r.at[g, r - 1], **dev).start()

    def s_next(g):
        n = (1 << len(groups[g])) - 1
        for r in range(n):
            wait_for(sgot.at[g, r], s_r.at[g, r])
        v = ssum[g] + sgot[g, 0]
        if n == 3:
            v = v + (sgot[g, 1] + sgot[g, 2])
        ssum[g + 1] = v
        if g + 1 < len(groups):
            s_start(g + 1)

    def local(src, dst_, i):
        return pltpu.make_async_copy(src, dst_, lsem.at[i])

    loads = [
        local(win_hbm, win, 0),
        local(x_hbm, dproj.at[0], 1),
        local(cot_hbm, dproj.at[1], 2),
        local(wout_hbm, w_all.at[t, pl.ds(o_out, ch), :], 3),
        local(wup_hbm, w_all.at[t, pl.ds(o_up, ff), :], 4),
        local(wdown_hbm, w_all.at[t, pl.ds(o_down, ff), :], 5),
        local(conv_hbm, cb.at[0, pl.ds(0, 4), :], 6),
        local(bias_hbm, cb.at[0, pl.ds(4, 1), :], 7),
        local(g1_hbm, g1_ref, 8),
        local(g2_hbm, g2_ref, 9),
    ]
    for i in (0, 1, 6, 7, 8, 9, 2, 3, 4, 5):
        loads[i].start()
    frecv[...] = jnp.zeros_like(frecv)
    brecv[...] = jnp.zeros_like(brecv)
    halo[...] = jnp.zeros_like(halo)
    barrier = pltpu.get_barrier_semaphore()
    for b in range(nb):
        pl.semaphore_signal(barrier, inc=1, device_id={"dp": flip(p, b)}, device_id_type=MESH)
    for j in range(1, blocks):
        pl.semaphore_signal(barrier, inc=1, device_id={"tensor": zflip(j)}, device_id_type=MESH)
    loads[0].wait()

    piece = span(IN, nb)

    def part(c, start):
        w_all[t, at_rows(IN, start, piece), lanes[c]] = win[pl.ds(start, piece), c, :]

    for c in range(2):
        part(c, low_of(IN, c, nb))
    pl.semaphore_wait(barrier, nb + blocks - 1)

    def c_copy(j):
        return remote(cb.at[0], cb.at[j], c_s.at[0], c_r.at[j], tensor=zflip(j))

    hcopy = remote(x_hbm.at[pl.ds(rows - 16, 16), :], halo, h_s.at[0], h_r.at[0], tensor=partner)
    pl.when(t == 2)(hcopy.start)
    for j in range(1, blocks):
        for copy in w_sources(IN, j):
            copy.start()
    for i in range(6, 10):
        loads[i].wait()
    for j in range(1, blocks):
        c_copy(j).start()

    def other_part(i, _):
        for c in range(2):
            part(c, lax.rem(low_of(IN, c, nb) + (i + 1) * piece, d))
        return 0

    lax.fori_loop(0, d // piece - 1, other_part, 0)
    loads[1].wait()

    nlane = d // LANES

    def spread(ref):
        for seg in range(SEGS):
            v = ref[pl.ds(seg * steps, steps), :].astype(F32)
            for i in range(nlane):
                perm[i, pl.ds(seg, steps, stride=SEGS), :] = v[:, i * LANES : (i + 1) * LANES]

    def gather(ref):
        for seg in range(SEGS):
            for i in range(nlane):
                v = perm[i, pl.ds(seg, steps, stride=SEGS), :]
                ref[pl.ds(seg * steps, steps), i * LANES : (i + 1) * LANES] = v.astype(ref.dtype)

    def perm_rows(at):
        return jnp.concatenate([perm[i, pl.ds(at, CHUNK), :] for i in range(nlane)], axis=1)

    def put_perm(at, v):
        for i in range(nlane):
            perm[i, pl.ds(at, CHUNK), :] = v[:, i * LANES : (i + 1) * LANES]

    spread(dproj.at[0])
    limit = jnp.where(
        t == 0,
        short_ref[0],
        jnp.where(t == 1, short_ref[1], jnp.where(t == 2, long_ref[0], long_ref[0] - rows)),
    )

    def norm_rows(r, _):
        at = pl.multiple_of(r * CHUNK, CHUNK)
        xv = perm_rows(at)
        xp[pl.ds(at, CHUNK), :] = xv.astype(BF16)
        fv = xv * scale_of(xv) * g1_ref[...]
        lhs[pl.ds(at, CHUNK), :] = fv.astype(BF16)
        first_t[:, pl.ds(at, CHUNK)] = fv.T.astype(BF16)
        return 0

    lax.fori_loop(0, nchunk, norm_rows, 0)
    loads[2].wait()
    spread(dproj.at[1])

    def dout_rows(r, _):
        at = pl.multiple_of(r * CHUNK, CHUNK)
        place = at + lax.broadcasted_iota(jnp.int32, (CHUNK, d), 0)
        pos = lax.rem(place, SEGS) * steps + place // SEGS
        dv = jnp.where(pos < limit, perm_rows(at), 0.0)
        dout[pl.ds(at, CHUNK), :] = dv.astype(BF16)
        dout_t[:, pl.ds(at, CHUNK)] = dv.T.astype(BF16)
        return 0

    lax.fori_loop(0, nchunk, dout_rows, 0)
    w_top(IN, 1)
    seg_id = lax.broadcasted_iota(jnp.int32, (SEGS, ch), 0)
    has_prev = jnp.where(t == 3, 1.0, 0.0).astype(F32)
    has_next = jnp.where(t == 2, 1.0, 0.0).astype(F32)

    def forward_block(j, _):
        s_ = zflip(j)

        @pl.when(j == 1)
        def _():
            w_top(IN, 3)
            w_mid(IN, 2)
            w_end(IN, 1)
            w_mid(IN, 3)

        @pl.when(j > 0)
        def _():
            c_copy(j).wait_recv()
            w_wait(IN, j, 0)

        def project(r, _):
            at = pl.multiple_of(r * WIDE, WIDE)
            v = dot(lhs[pl.ds(at, WIDE), :], w_all[s_, pl.ds(o_in, d), :])
            bufa[pl.ds(at, WIDE), :ch] = v[:, :ch]
            cand[j, pl.ds(at + 3 * SEGS, WIDE), :] = v[:, ch:]

            return 0

        lax.fori_loop(0, rows // WIDE, project, 0)

        @pl.when(j == 0)
        def _():
            pl.when(t == 3)(hcopy.wait_recv)
            hv = halo[...].astype(F32)
            edge_rows[...] = (hv * scale_of(hv) * g1_ref[...]).astype(BF16)

        @pl.when(j == 1)
        def _():
            w_end(IN, 2)

        @pl.when(j == 2)
        def _():
            w_end(IN, 3)

        @pl.when(j == 3)
        def _():
            w_top(FF, 2)

        ph = dot(edge_rows[...], w_all[s_, pl.ds(o_in, d), ch:])
        for back in range(3):
            last = cand[j, pl.ds((steps + back) * SEGS, SEGS), :]
            rolled = pltpu.roll(last, 1, 0)
            edge = ph[13 + back : 14 + back, :] * has_prev
            cand[j, pl.ds(back * SEGS, SEGS), :] = jnp.where(seg_id == 0, edge, rolled)
        k_ = [jnp.broadcast_to(cb[j, pl.ds(i, 1), :], (SEGS, ch)) for i in range(4)]
        bias = jnp.broadcast_to(cb[j, pl.ds(4, 1), :], (SEGS, ch))

        def step8(i, carry):
            s, q_ = carry
            for q in range(8):
                at = pl.multiple_of((i * 8 + q) * SEGS, SEGS)
                u = sigmoid(bufa[pl.ds(at, SEGS), :ch] + bias)
                f = k_[0] * cand[j, pl.ds(at + 3 * SEGS, SEGS), :]
                for lag in range(1, 4):
                    f = f + k_[lag] * cand[j, pl.ds(at + (3 - lag) * SEGS, SEGS), :]
                upd[j, pl.ds(at, SEGS), :] = u
                dst[j, pl.ds(at, SEGS), :] = f
                a = 1.0 - u
                s = a * s + u * f
                q_ = a * q_
            return s, q_

        half = lax.fori_loop(
            0, steps // 16, step8, (jnp.zeros((SEGS, ch), F32), jnp.ones((SEGS, ch), F32))
        )

        @pl.when(j == 0)
        def _():
            w_top(IN, 2)
            loads[3].wait()
            for i in (2, 3, 1):
                for copy in w_sources(OUT, i):
                    copy.start()

        s, q_ = lax.fori_loop(steps // 16, steps // 8, step8, half)
        ends[0, j] = s
        ends[1, j] = q_
        fsend[j] = jnp.broadcast_to(forward_chain(j, jnp.zeros((1, ch), F32)), (8, ch))
        pl.when(t == 2)(f_copy(j).start)

        @pl.when(j == 0)
        def _():
            w_mid(IN, 1)
            loads[4].wait()
            loads[5].wait()
            for i in (2, 3, 1):
                for copy in w_sources(FF, i):
                    copy.start()

        @pl.when(j == 1)
        def _():
            w_top(OUT, 1, 2, 3)

        @pl.when(j == 2)
        def _():
            w_mid(OUT, 1, 2, 3)

        return 0

    def forward_chain(j, start):
        run = start
        for seg in range(SEGS):
            st[j, pl.ds(seg, 1), :] = run
            run = ends[0, j, pl.ds(seg, 1), :] + ends[1, j, pl.ds(seg, 1), :] * run
        return run

    def f_copy(j):
        there = flip(j, 0)
        return remote(fsend.at[j], frecv.at[there], f_s.at[0], f_r.at[there], tensor=partner)

    lax.fori_loop(0, blocks, forward_block, 0)
    w_top(FF, 3)

    def forward_fix(i, _):
        b = flip(i, 0)

        @pl.when(t == 3)
        def _():
            wait_for(frecv.at[b], f_r.at[b])

        forward_chain(b, frecv[b, pl.ds(0, 1), :] * has_prev)

        def step8(i, s):
            for q in range(8):
                at = pl.multiple_of((i * 8 + q) * SEGS, SEGS)
                u = upd[b, pl.ds(at, SEGS), :]
                s = (1.0 - u) * s + u * dst[b, pl.ds(at, SEGS), :]
                st[b, pl.ds(at + SEGS, SEGS), :] = s
            return s

        lax.fori_loop(0, steps // 8, step8, st[b, pl.ds(0, SEGS), :])

        @pl.when(i == 1)
        def _():
            w_end(OUT, 1, 2, 3)

        return 0

    lax.fori_loop(0, blocks, forward_fix, 0)
    w_mid(FF, 2)
    for j in range(1, blocks):
        w_wait(OUT, j, 0)
    shards = [zflip(j) for j in range(blocks)]

    def second_rows(r, _):
        at = pl.multiple_of(r * 512, 512)
        m = xp[pl.ds(at, 512), :].astype(F32)
        for j in range(blocks):
            m = m + dot(
                st[j, pl.ds(at + SEGS, 512), :].astype(BF16), w_all[shards[j], pl.ds(o_out, ch), :]
            )
        mid[pl.ds(at, 512), :] = m
        sv = m * scale_of(m) * g2_ref[...]
        lhs[pl.ds(at, 512), :] = sv.astype(BF16)
        second_t[:, pl.ds(at, 512)] = sv.T.astype(BF16)
        bufa[pl.ds(at, 512), :] = m
        bufc[pl.ds(at, 512), :] = jnp.zeros((512, d), F32)
        return 0

    lax.fori_loop(0, rows // 512, second_rows, 0)

    w_mid(FF, 3)
    act, din = dproj.at[1], dproj.at[2]

    def ff_place(i):
        return lax.div(i + 3, 4) * (1 + lax.rem(i, 3))

    def ff_block(i, _):
        j, before, earlier = ff_place(i), ff_place(i - 1), ff_place(i - 2)
        s_ = zflip(j)

        @pl.when(i > 0)
        def _():
            w_wait(FF, j, 0)

        def ff_rows(r, _):
            at = pl.multiple_of(r * 512, 512)
            wu = w_all[s_, pl.ds(o_up, ff), :]
            wd = w_all[s_, pl.ds(o_down, ff), :]
            inner = dot(lhs[pl.ds(at, 512), :], wu)
            da = dot_t(dout[pl.ds(at, 512), :], wd)
            cdf = 0.5 + 0.5 * lax.erf(inner * np.float32(np.sqrt(0.5)))
            pdf = jnp.exp(inner * inner * -0.5) * np.float32(1.0 / np.sqrt(2.0 * np.pi))
            av = (inner * cdf).astype(BF16)
            dv = (da * (cdf + inner * pdf)).astype(BF16)
            act[pl.ds(at, 512), :] = av
            din[pl.ds(at, 512), :] = dv
            bufa[pl.ds(at, 512), :] += dot(av, wd)
            bufc[pl.ds(at, 512), :] += dot_t(dv, wu)

            @pl.when((r == 0) & (i == 0))
            def _():
                w_end(FF, 2)

            @pl.when((r == 1) & (i == 0))
            def _():
                w_top(FF, 1)

            @pl.when((r == 0) & (i == 1))
            def _():
                w_end(FF, 3)

            @pl.when((r == 0) & (i == 1))
            def _():
                w_mid(FF, 1)

            @pl.when((r == 0) & (i == 2))
            def _():
                w_end(FF, 1)

            @pl.when((r == 1) & (i > 0))
            def _():
                r_first(FF, before)

            return 0

        lax.fori_loop(0, rows // 512, ff_rows, 0)

        def ff_grads(r, _):
            at = pl.multiple_of(r * 512, 512)
            grad[s_, pl.ds(o_up + at, 512), :] = dot(second_t[pl.ds(at, 512), :], din[...]).astype(BF16)
            grad[s_, pl.ds(o_down + at, 512), :] = dot(dout_t[pl.ds(at, 512), :], act[...]).astype(BF16)
            return 0

        lax.fori_loop(0, d // 512, ff_grads, 0)
        @pl.when(i > 1)
        def _():
            r_middle(FF, earlier)

        r_start(FF, j, 0)
        return 0

    lax.fori_loop(0, blocks, ff_block, 0)

    def second_back(r, gain):
        at = pl.multiple_of(r * CHUNK, CHUNK)
        m = mid[pl.ds(at, CHUNK), :]
        s = scale_of(m)
        dn = bufc[pl.ds(at, CHUNK), :]
        gain = gain + jnp.sum(dn * m * s, axis=0, keepdims=True)
        gd = dn * g2_ref[...]
        dm = dout[pl.ds(at, CHUNK), :].astype(F32) + s * gd - m * (s * s * s * jnp.mean(gd * m, axis=-1, keepdims=True))
        mid[pl.ds(at, CHUNK), :] = dm
        lhs[pl.ds(at, CHUNK), :] = dm.astype(BF16)
        second_t[:, pl.ds(at, CHUNK)] = dm.T.astype(BF16)
        bufc[pl.ds(at, CHUNK), :] = jnp.zeros((CHUNK, d), F32)
        return gain

    gain2 = lax.fori_loop(0, nchunk, second_back, jnp.zeros((1, d), F32))
    ssum[0] = jnp.zeros((16, d), F32)
    ssum[0, pl.ds(1, 1), :] = gain2
    r_first(FF, 1)

    def backward_block(i, _):
        j = blocks - 1 - i
        s_ = zflip(j)

        def project(r, _):
            at = pl.multiple_of(r * 512, 512)
            dst[j, pl.ds(at, 512), :] = dot_t(lhs[pl.ds(at, 512), :], w_all[s_, pl.ds(o_out, ch), :])
            return 0

        lax.fori_loop(0, rows // 512, project, 0)
        state = st[j, pl.ds(SEGS, rows), :].astype(BF16)
        for half in range(2):
            rr = d // 2
            grad[s_, pl.ds(o_out, ch), half * ch : (half + 1) * ch] = dot(
                second_t[half * rr : (half + 1) * rr, :], state
            ).astype(BF16)
        r_start(OUT, j, 0)

        @pl.when(i == 0)
        def _():
            r_last(FF, 2)
            r_middle(FF, 3)

        @pl.when(i == 1)
        def _():
            r_last(FF, 0)

        @pl.when(i == 2)
        def _():
            r_middle(FF, 1)

        @pl.when(i == 3)
        def _():
            r_last(FF, 3)
            r_middle(OUT, 3)

        def one(step, w, q_):
            at = pl.multiple_of(step * SEGS, SEGS)
            a = 1.0 - upd[j, pl.ds(at, SEGS), :]
            c = dst[j, pl.ds(at, SEGS), :] + w
            return c, a * c, q_ * a

        w, q_ = jnp.zeros((SEGS, ch), F32), jnp.ones((SEGS, ch), F32)
        for step in range(steps - 1, steps - 6, -1):
            _, w, q_ = one(step, w, q_)

        def step8(n, carry):
            w, q_ = carry
            for q in range(8):
                _, w, q_ = one(steps - 6 - (n * 8 + q), w, q_)
            return w, q_

        w, q_ = lax.fori_loop(0, (steps - 8) // 8, step8, (w, q_))
        for step in range(2, -1, -1):
            bends[2 * step, j] = q_
            c, w, q_ = one(step, w, q_)
            bends[2 * step + 1, j] = c
        bends[6, j] = w
        bends[7, j] = q_
        bsend[j, pl.ds(0, 1), :] = backward_chain(j, jnp.zeros((1, ch), F32))
        for step in range(3):
            bsend[j, pl.ds(step + 1, 1), :] = upd[j, pl.ds(step * SEGS, 1), :] * (
                bends[2 * step + 1, j, pl.ds(0, 1), :]
                + bends[2 * step, j, pl.ds(0, 1), :] * ends[0, j, pl.ds(0, 1), :]
            )
        pl.when(t == 3)(b_copy(j).start)

        @pl.when(i > 0)
        def _():
            r_first(OUT, j + 1)

        return 0

    def backward_chain(j, start):
        run = start
        for seg in range(SEGS - 1, -1, -1):
            ends[0, j, pl.ds(seg, 1), :] = run
            run = bends[6, j, pl.ds(seg, 1), :] + bends[7, j, pl.ds(seg, 1), :] * run
        return run

    def b_copy(j):
        there = flip(j, 0)
        return remote(bsend.at[j], brecv.at[there], b_s.at[0], b_r.at[there], tensor=partner)

    lax.fori_loop(0, blocks, backward_block, 0)


    def backward_fix(i, _):
        j = blocks - 1 - i
        s_ = zflip(j)

        @pl.when(t == 2)
        def _():
            wait_for(brecv.at[j], b_r.at[j])

        backward_chain(j, brecv[j, pl.ds(0, 1), :] * has_next)
        w = ends[0, j]
        after = []
        for step in range(3):
            df = upd[j, pl.ds(step * SEGS, SEGS), :] * (bends[2 * step + 1, j] + bends[2 * step, j] * w)
            edge = brecv[j, pl.ds(step + 1, 1), :] * has_next
            after.append(jnp.where(seg_id == SEGS - 1, edge, pltpu.roll(df, SEGS - 1, 0)))
        k_ = [jnp.broadcast_to(cb[j, pl.ds(n, 1), :], (SEGS, ch)) for n in range(4)]
        zero = jnp.zeros((SEGS, ch), F32)

        def pair(n, carry):
            w, d1, d2, d3, c0, c1, c2, k0, k1, k2, k3, gb = carry
            top = steps - 2 - 2 * n
            made = []
            for q in range(2):
                at = pl.multiple_of((top + 1 - q) * SEGS, SEGS)
                u = upd[j, pl.ds(at, SEGS), :]
                c = dst[j, pl.ds(at, SEGS), :] + w
                d0 = c * u
                a = 1.0 - u
                w = a * c
                c3 = cand[j, pl.ds(at, SEGS), :]
                f = k_[0] * c0 + k_[1] * c1 + k_[2] * c2 + k_[3] * c3
                dg = d0 * a * (f - st[j, pl.ds(at, SEGS), :])
                dc = k_[0] * d0 + k_[1] * d1 + k_[2] * d2 + k_[3] * d3
                k0, k1, k2, k3 = k0 + d0 * c0, k1 + d0 * c1, k2 + d0 * c2, k3 + d0 * c3
                gb = gb + dg
                c0, c1, c2 = c1, c2, c3
                d1, d2, d3 = d0, d1, d2
                made.append((dg, dc))
            at = pl.multiple_of(top * SEGS, 2 * SEGS)
            dproj[j, pl.ds(at, 2 * SEGS), :ch] = jnp.concatenate([made[1][0], made[0][0]], axis=0).astype(BF16)
            dproj[j, pl.ds(at, 2 * SEGS), ch:] = jnp.concatenate([made[1][1], made[0][1]], axis=0).astype(BF16)
            return w, d1, d2, d3, c0, c1, c2, k0, k1, k2, k3, gb

        window = [cand[j, pl.ds((steps + 2 - n) * SEGS, SEGS), :] for n in range(3)]
        def quad(n, carry):
            return pair(2 * n + 1, pair(2 * n, carry))

        half = lax.fori_loop(0, steps // 8, quad, (w, *after, *window, zero, zero, zero, zero, zero))

        @pl.when(i == 0)
        def _():
            r_last(FF, 1)
            r_first(OUT, 0)
            r_middle(OUT, 2)

        @pl.when(i == 1)
        def _():
            r_last(OUT, 2)
            r_middle(OUT, 0)

        @pl.when(i == 2)
        def _():
            r_last(OUT, 0)

        @pl.when(i == 3)
        def _():
            r_middle(IN, 3)
            a_first(OUT)

        out = lax.fori_loop(steps // 8, steps // 4, quad, half)
        for n in range(5):
            at = 2 + 2 * n + bit_of(s_, 1)
            ssum[0, pl.ds(at, 1), pl.ds(pl.multiple_of(bit_of(s_, 0) * ch, LANES), ch)] = jnp.sum(
                out[7 + n], axis=0, keepdims=True
            )

        @pl.when(i > 1)
        def _():
            r_first(IN, j + 1)

        def first_grad(r, _):
            at = pl.multiple_of(r * 512, 512)
            grad[s_, pl.ds(o_in + at, 512), :] = dot(first_t[pl.ds(at, 512), :], dproj[j]).astype(BF16)
            return 0

        lax.fori_loop(0, d // 512, first_grad, 0)
        r_start(IN, j, 0)


        @pl.when(i == 0)
        def _():
            r_last(OUT, 3)
            r_middle(OUT, 1)

        @pl.when(i == 1)
        def _():
            r_first(IN, 3)
            r_last(OUT, 1)

        @pl.when(i == 2)
        def _():
            a_first(FF)

        @pl.when(i == 3)
        def _():
            r_middle(IN, 2)

        return 0

    lax.fori_loop(0, blocks, backward_fix, 0)

    def first_back(r):
        at = r * 512
        v = dot_t(dproj[0, pl.ds(at, 512), :], w_all[shards[0], pl.ds(o_in, d), :])
        for j in range(1, blocks):
            v = v + dot_t(dproj[j, pl.ds(at, 512), :], w_all[shards[j], pl.ds(o_in, d), :])
        bufc[pl.ds(at, 512), :] = v

    first_back(0)
    r_last(IN, 3)
    r_first(IN, 0)
    for r in range(1, rows // 512):
        first_back(r)
    r_middle(IN, 1)
    a_mid(FF)
    r_last(IN, 2)

    def first_norm_back(r, gain):
        at = pl.multiple_of(r * CHUNK, CHUNK)
        m = xp[pl.ds(at, CHUNK), :].astype(F32)
        s = scale_of(m)
        dn = bufc[pl.ds(at, CHUNK), :]
        gain = gain + jnp.sum(dn * m * s, axis=0, keepdims=True)
        gd = dn * g1_ref[...]
        dv = s * gd - m * (s * s * s * jnp.mean(gd * m, axis=-1, keepdims=True))
        put_perm(at, mid[pl.ds(at, CHUNK), :] + dv)
        return gain

    ssum[0, pl.ds(0, 1), :] = lax.fori_loop(0, nchunk, first_norm_back, jnp.zeros((1, d), F32))
    s_start(0)
    r_middle(IN, 0)
    r_last(IN, 1)
    s_next(0)
    gather(mid)
    r_last(IN, 0)
    a_first(IN)
    a_mid(OUT)
    a_end(FF)
    for r in range(nchunk):
        put_perm(r * CHUNK, bufa[pl.ds(r * CHUNK, CHUNK), :])
    gather(res)
    for g in range(1, len(groups) - 1):
        s_next(g)
    a_mid(IN)
    a_end(OUT)
    a_end(IN)
    s_next(len(groups) - 1)
    gains_ref[...] = ssum[len(groups), pl.ds(0, 8), :]
    for n in range(5):
        at = 2 + 2 * n + bit_of(t, 1)
        chan_ref[pl.ds(n, 1), :] = ssum[
            len(groups), pl.ds(at, 1), pl.ds(pl.multiple_of(bit_of(t, 0) * ch, LANES), ch)
        ]
    a_wait(FF, 0)
    a_wait(OUT, 0)
    a_wait(IN, 0)

    pl.when(t == 2)(hcopy.wait_send)
    wait_for(cb.at[pl.ds(0, blocks - 1)], c_s.at[0])
    pl.when(t == 2)(lambda: wait_for(fsend, f_s.at[0]))
    pl.when(t == 3)(lambda: wait_for(bsend, b_s.at[0]))
    for kind in (IN, OUT, FF):
        for k in range(halves[kind]):
            n = span(kind, k + 1)
            wait_for(w_all.at[0, pl.ds(0, (blocks - 1) * n), :], w_s.at[kind, k])
            wait_for(grad.at[pl.ds(0, 2), pl.ds(0, blocks // 2 * n), :], r_s.at[kind, k])
            wait_for(fin.at[pl.ds(0, n), :], a_s.at[kind, k])
        n = span(kind, nb)
        wait_for(w_all.at[0, pl.ds(0, (blocks - 1) * n), :], w_s.at[kind, nb])
        wait_for(w_all.at[0, pl.ds(0, (blocks - 1) * n), :], r_s.at[kind, nb])
    for g in range(len(groups)):
        wait_for(sgot.at[g, pl.ds(0, (1 << len(groups[g])) - 1)], s_s.at[g])


def finish_kernel(
    dims, gains, chan, res, gx, fin, res_out, gx_out, gin_o, gout_o, gup_o, gdown_o, gnorm, gmlp, taps, gbias,
    gin, gout, gup, gdown, sem,
):
    rows, d, ch, ff = dims
    outs = []

    def put(src, dst):
        copy = pltpu.make_async_copy(src, dst, sem.at[len(outs)])
        copy.start()
        outs.append(copy)

    put(gx, gx_out)
    put(res, res_out)
    gup[...] = fin[pl.ds(d + ch, d), :].astype(F32)
    put(gup, gup_o)
    gin[:, 0, :] = fin[pl.ds(0, d), :ch].astype(F32)
    gin[:, 1, :] = fin[pl.ds(0, d), ch:].astype(F32)
    put(gin, gin_o)
    gdown[...] = fin[pl.ds(d + ch + ff, d), :].astype(F32).T
    put(gdown, gdown_o)
    gout[:, : d // 2] = fin[pl.ds(d, ch), :ch].astype(F32).T
    gout[:, d // 2 :] = fin[pl.ds(d, ch), ch:].astype(F32).T
    put(gout, gout_o)
    gnorm[...] = gains[pl.ds(0, 1), :]
    gmlp[...] = gains[pl.ds(1, 1), :]
    taps[...] = chan[pl.ds(0, 4), :]
    gbias[...] = chan[pl.ds(4, 1), :]
    for copy in outs:
        copy.wait()


def per_device(
    inputs,
    norm_gain,
    in_weight,
    conv_kernel,
    gate_bias,
    out_weight,
    mlp_gain,
    up_weight,
    down_weight,
    short_lengths,
    long_lengths,
    cotangent,
):
    rows, d = inputs.shape
    ch = in_weight.shape[2]
    ff = up_weight.shape[1]
    blocks = lax.axis_size("tensor")
    dp = lax.axis_size("dp")
    nb = log2(dp)
    assert dp == 1 << nb and blocks == 4 and rows == LSHORT and 2 * rows == LLONG
    assert 2 * ch == d and short_lengths.shape == (2,) and long_lengths.shape == (1,)
    sizes = (d, ch, 2 * ff)
    total = sum(sizes)
    halves = tuple(min(nb, log2(r // TILE)) for r in sizes)

    def span_all(k):
        return sum(r >> min(k, h) for r, h in zip(sizes, halves))

    ngroups = len(bit_groups(nb))
    vm = pl.BlockSpec(memory_space=pltpu.VMEM)
    sm = pl.BlockSpec(memory_space=pltpu.SMEM)
    hb = pl.BlockSpec(memory_space=pl.ANY)
    dma = pltpu.SemaphoreType.DMA
    res, gx, fin, gains, chan = pl.pallas_call(
        functools.partial(block_kernel, (rows, d, blocks, ch, ff, nb)),
        out_shape=(
            pltpu.VMEM((rows, d), BF16),
            pltpu.VMEM((rows, d), F32),
            pltpu.VMEM((total, d), BF16),
            pltpu.VMEM((8, d), F32),
            pltpu.VMEM((8, ch), F32),
        ),
        in_specs=[sm, sm] + [hb] * 10,
        out_specs=(vm,) * 5,
        scratch_shapes=[
            pltpu.VMEM((1, d), F32),
            pltpu.VMEM((1, d), F32),
            pltpu.VMEM((blocks, total, d), BF16),
            pltpu.VMEM((blocks, total, d), BF16),
            pltpu.VMEM((d, 2, ch), BF16),
            pltpu.VMEM((rows, d), BF16),
            pltpu.VMEM((blocks, rows + 3 * SEGS, ch), F32),
            pltpu.VMEM((blocks, rows, ch), F32),
            pltpu.VMEM((blocks, rows + SEGS, ch), F32),
            pltpu.VMEM((blocks, rows, ch), F32),
            pltpu.VMEM((16, d), BF16),
            pltpu.VMEM((d, rows), BF16),
            pltpu.VMEM((d, rows), BF16),
            pltpu.VMEM((rows, d), BF16),
            pltpu.VMEM((d, rows), BF16),
            pltpu.VMEM((rows, d), F32),
            pltpu.VMEM((rows, d), F32),
            pltpu.VMEM((blocks, rows, d), BF16),
            pltpu.VMEM((d // LANES, rows, LANES), F32),
            pltpu.VMEM((16, d), BF16),
            pltpu.VMEM((blocks, 8, ch), F32),
            pltpu.VMEM((2, blocks, SEGS, ch), F32),
            pltpu.VMEM((8, blocks, SEGS, ch), F32),
            pltpu.VMEM((blocks, 8, ch), F32),
            pltpu.VMEM((blocks, 8, ch), F32),
            pltpu.VMEM((blocks, 8, ch), F32),
            pltpu.VMEM((blocks, 8, ch), F32),
            pltpu.VMEM((blocks, span_all(nb), d), BF16),
            pltpu.VMEM((ngroups + 1, 16, d), F32),
            pltpu.VMEM((ngroups, 3, 16, d), F32),
            dma((10,)),
            dma((1,)),
            dma((blocks,)),
            dma((1,)),
            dma((blocks,)),
            dma((1,)),
            dma((blocks,)),
            dma((1,)),
            dma((1,)),
            dma((3, nb + 1)),
            dma((3, blocks, nb + 1)),
            dma((3, nb + 1)),
            dma((3, blocks, nb + 1)),
            dma((3, blocks, nb)),
            dma((3, nb)),
            dma((3, nb)),
            dma((ngroups,)),
            dma((ngroups, 3)),
        ]
        + [pltpu.VMEM((blocks, span_all(k + 1), d), BF16) for k in range(nb)],
        compiler_params=pltpu.CompilerParams(
            collective_id=0, has_side_effects=True, vmem_limit_bytes=59 << 20
        ),
        name="block",
    )(
        short_lengths,
        long_lengths,
        inputs,
        cotangent,
        norm_gain[None],
        mlp_gain[None],
        conv_kernel,
        gate_bias[None],
        in_weight,
        out_weight,
        up_weight,
        down_weight,
    )
    result, grad_inputs, gin, gout, gup, gdown, gnorm, gmlp, taps, gbias = pl.pallas_call(
        functools.partial(finish_kernel, (rows, d, ch, ff)),
        out_shape=(
            jax.ShapeDtypeStruct((rows, d), BF16),
            jax.ShapeDtypeStruct((rows, d), F32),
            jax.ShapeDtypeStruct((d, 2, ch), F32),
            jax.ShapeDtypeStruct((ch, d), F32),
            jax.ShapeDtypeStruct((d, ff), F32),
            jax.ShapeDtypeStruct((ff, d), F32),
            jax.ShapeDtypeStruct((1, d), F32),
            jax.ShapeDtypeStruct((1, d), F32),
            jax.ShapeDtypeStruct((4, ch), F32),
            jax.ShapeDtypeStruct((1, ch), F32),
        ),
        in_specs=[vm] * 5,
        out_specs=(hb,) * 6 + (vm,) * 4,
        scratch_shapes=[
            pltpu.VMEM((d, 2, ch), F32),
            pltpu.VMEM((ch, d), F32),
            pltpu.VMEM((d, ff), F32),
            pltpu.VMEM((ff, d), F32),
            dma((6,)),
        ],
        compiler_params=pltpu.CompilerParams(vmem_limit_bytes=32 << 20),
        name="finish",
    )(gains, chan, res, gx, fin)
    return (result, grad_inputs, gnorm[0], gin, taps, gbias[0], gout, gmlp[0], gup, gdown)


def solution(mesh):
    placed = (
        P(("dp", "tensor"), None),
        P(),
        P(None, None, "tensor"),
        P(None, "tensor"),
        P("tensor"),
        P("tensor", None),
        P(),
        P(None, "tensor"),
        P("tensor", None),
        P("dp"),
        P("dp"),
        P(("dp", "tensor"), None),
    )
    return jax.shard_map(
        per_device,
        mesh=mesh,
        in_specs=placed,
        out_specs=(
            P(("dp", "tensor"), None),
            P(("dp", "tensor"), None),
            P(),
            P(None, None, "tensor"),
            P(None, "tensor"),
            P("tensor"),
            P("tensor", None),
            P(),
            P(None, "tensor"),
            P("tensor", None),
        ),
        check_vma=False,
    )
```

```python
import functools

import jax
import jax.numpy as jnp
import numpy as np
from jax import lax
from jax.experimental import pallas as pl
from jax.experimental.pallas import tpu as pltpu
from jax.sharding import PartitionSpec as P

LSHORT = 1024
LLONG = 2048
SEGS = 8
EPS = 1e-05
CHUNK = 256
WIDE = 1024
TILE = 16
LANES = 128
F32 = jnp.float32
BF16 = jnp.bfloat16
MESH = pl.DeviceIdType.MESH
IN, OUT, FF = 0, 1, 2


def dot(a, b):
    return jnp.dot(a, b, preferred_element_type=F32)


def dot_t(a, b):
    return lax.dot_general(a, b, (((1,), (1,)), ((), ())), preferred_element_type=F32)


def scale_of(v):
    return lax.rsqrt(jnp.mean(v * v, axis=-1, keepdims=True) + EPS)


def sigmoid(v):
    return 1.0 / (1.0 + jnp.exp(-v))


def bit_of(v, bit):
    return lax.rem(lax.div(v, 1 << bit), 2)


def flip(v, bit):
    return v + (1 << bit) * (1 - 2 * bit_of(v, bit))


def log2(n):
    return int(n).bit_length() - 1


def bit_groups(nb):
    groups = [(0,)] + [tuple(range(b, min(b + 2, nb))) for b in range(1, nb, 2)]
    return groups + [(nb, nb + 1)]


def block_kernel(
    dims,
    short_ref,
    long_ref,
    x_hbm,
    cot_hbm,
    g1_hbm,
    g2_hbm,
    conv_hbm,
    bias_hbm,
    win_hbm,
    wout_hbm,
    wup_hbm,
    wdown_hbm,
    res,
    mid,
    fin,
    gains_ref,
    chan_ref,
    g1_ref,
    g2_ref,
    w_all,
    grad,
    win,
    xp,
    cand,
    upd,
    st,
    dst,
    edge_rows,
    first_t,
    second_t,
    dout,
    dout_t,
    bufa,
    bufc,
    dproj,
    perm,
    halo,
    cb,
    ends,
    bends,
    fsend,
    frecv,
    bsend,
    brecv,
    zbuf,
    ssum,
    sgot,
    lsem,
    c_s,
    c_r,
    f_s,
    f_r,
    b_s,
    b_r,
    h_s,
    h_r,
    w_s,
    w_r,
    r_s,
    r_r,
    x_s,
    a_s,
    a_r,
    s_s,
    s_r,
    *stage_bufs,
):
    rows, d, blocks, ch, ff, nb = dims
    steps = rows // SEGS
    t = lax.axis_index("tensor")
    p = lax.axis_index("dp")
    partner = flip(t, 0)
    nchunk = rows // CHUNK
    offs = (0, d, d + ch)
    sizes = (d, ch, 2 * ff)
    o_in, o_out, o_up, o_down = 0, d, d + ch, d + ch + ff
    halves = tuple(min(nb, log2(r // TILE)) for r in sizes)
    half_d = d // 2
    lanes = (pl.ds(0, half_d), pl.ds(half_d, half_d))
    orders = ((0,) + tuple(range(nb - 1, 0, -1)), tuple(range(nb)))
    lhs = dproj.at[3]

    def zflip(j):
        b0, b1 = lax.rem(j, 2), lax.div(j, 2)
        return t + b0 * (1 - 2 * bit_of(t, 0)) + b1 * (2 - 4 * bit_of(t, 1))

    def low_of(kind, c, k):
        low = 0
        for i in range(min(k, halves[kind])):
            low = low + bit_of(p, orders[c][i]) * (sizes[kind] >> (i + 1))
        return low

    def span(kind, k):
        return sizes[kind] >> min(k, halves[kind])

    def at_rows(kind, start, n):
        return pl.ds(pl.multiple_of(offs[kind] + start, TILE), n)

    def stage_rows(kind, k):
        base = sum(span(i, k + 1) for i in range(kind))
        return pl.ds(base, span(kind, k + 1))

    def remote(src, dst_, ss, rs, **dev):
        return pltpu.make_async_remote_copy(
            src_ref=src, dst_ref=dst_, send_sem=ss, recv_sem=rs, device_id=dev, device_id_type=MESH
        )

    def wait_for(ref, sem):
        pltpu.make_async_copy(ref, ref, sem).wait()

    def w_step(kind, j, k):
        made = []
        for c in range(1 if k == 0 else 2):
            at = at_rows(kind, low_of(kind, c, k + 1), span(kind, k + 1))
            ref = w_all.at[zflip(j), at, slice(None) if k == 0 else lanes[c]]
            made.append(remote(ref, ref, w_s.at[kind, k], w_r.at[kind, j, k], dp=flip(p, orders[c][k])))
        return made

    def w_sources(kind, j):
        made = []
        for c in range(2):
            ref = w_all.at[t, at_rows(kind, low_of(kind, c, nb), span(kind, nb)), lanes[c]]
            made.append(remote(ref, ref, w_s.at[kind, nb], w_r.at[kind, j, nb], tensor=zflip(j)))
        return made

    def w_wait(kind, j, k):
        k_ = nb if k == halves[kind] else k
        wait_for(w_all.at[0, pl.ds(0, span(kind, k + 1))], w_r.at[kind, j, k_])

    def w_forward(kind, j, k):
        w_wait(kind, j, k + 1)
        for copy in w_step(kind, j, k):
            copy.start()

    def w_top(kind, *js):
        for j in js:
            w_forward(kind, j, halves[kind] - 1)

    def w_mid(kind, *js):
        for k in range(halves[kind] - 2, 0, -1):
            for j in js:
                w_forward(kind, j, k)

    def w_end(kind, *js):
        for j in js:
            w_forward(kind, j, 0)

    def r_step(kind, j, k):
        s = zflip(j)
        base = sum(span(i, k + 1) for i in range(kind))
        made = []
        for c in range(1 if k == 0 else 2):
            low = low_of(kind, c, k)
            if k < halves[kind]:
                low = low + (1 - bit_of(p, orders[c][k])) * span(kind, k + 1)
            which = slice(None) if k == 0 else lanes[c]
            made.append(
                remote(
                    grad.at[s, at_rows(kind, low, span(kind, k + 1)), which],
                    stage_bufs[k].at[j, pl.ds(base, span(kind, k + 1)), which],
                    r_s.at[kind, k] if k < halves[kind] else x_s.at[kind, j, k],
                    r_r.at[kind, j, k],
                    dp=flip(p, orders[c][k]),
                )
            )
        return made

    def r_start(kind, j, k):
        for copy in r_step(kind, j, k):
            copy.start()

    def r_finish(kind, j, k):
        s = zflip(j)
        buf = stage_bufs[k]
        base = sum(span(i, k + 1) for i in range(kind))
        n = span(kind, k + 1)
        here = stage_bufs[k].at[j, pl.ds(base, n), :]
        if k >= halves[kind]:
            wait_for(here, x_s.at[kind, j, k])
        wait_for(here, r_r.at[kind, j, k])
        piece = min(n, 128)
        for c in range(2):
            low = low_of(kind, c, k + 1)

            def add(i, _):
                at = at_rows(kind, low + i * piece, piece)
                here = pl.ds(pl.multiple_of(base + i * piece, TILE), piece)
                grad[s, at, lanes[c]] += buf[j, here, lanes[c]]
                return 0

            lax.fori_loop(0, n // piece, add, 0)

    def r_z(kind, j):
        s = zflip(j)
        base = sum(span(i, nb) for i in range(kind))
        made = []
        for c in range(2):
            at = at_rows(kind, low_of(kind, c, nb), span(kind, nb))
            made.append(
                remote(
                    grad.at[s, at, lanes[c]],
                    zbuf.at[j, pl.ds(base, span(kind, nb)), lanes[c]],
                    r_s.at[kind, nb],
                    r_r.at[kind, j, nb],
                    tensor=s,
                )
            )
        return made

    def r_out(kind, j):
        for copy in r_z(kind, j):
            copy.start()

    def r_total(kind):
        base = sum(span(i, nb) for i in range(kind))
        n = span(kind, nb)
        for j in range(1, blocks):
            wait_for(zbuf.at[j, pl.ds(base, n), :], r_r.at[kind, j, nb])
        for c in range(2):
            at = at_rows(kind, low_of(kind, c, nb), n)
            total = grad[t, at, lanes[c]].astype(F32)
            for j in range(1, blocks):
                total = total + zbuf[j, pl.ds(base, n), lanes[c]].astype(F32)
            fin[at, lanes[c]] = total.astype(BF16)

    def a_step(kind, k):
        made = []
        for c in range(1 if k == 0 else 2):
            at = at_rows(kind, low_of(kind, c, k + 1), span(kind, k + 1))
            ref = fin.at[at, slice(None) if k == 0 else lanes[c]]
            made.append(remote(ref, ref, a_s.at[kind, k], a_r.at[kind, k], dp=flip(p, orders[c][k])))
        return made

    def a_start(kind, k):
        for copy in a_step(kind, k):
            copy.start()

    def a_wait(kind, k):
        wait_for(fin.at[pl.ds(0, span(kind, k + 1)), :], a_r.at[kind, k])

    def r_middle(kind, j):
        for k in range(1, nb - 1):
            r_finish(kind, j, k)
            r_start(kind, j, k + 1)

    def r_first(kind, j):
        r_finish(kind, j, 0)
        r_start(kind, j, 1)

    def r_last(kind, j):
        r_finish(kind, j, nb - 1)
        if isinstance(j, int):
            if j > 0:
                r_out(kind, j)
        else:
            pl.when(j > 0)(lambda: r_out(kind, j))

    def a_first(kind):
        r_total(kind)
        a_start(kind, halves[kind] - 1)

    def a_mid(kind):
        for k in range(halves[kind] - 2, 0, -1):
            a_wait(kind, k + 1)
            a_start(kind, k)

    def a_end(kind):
        a_wait(kind, 1)
        a_start(kind, 0)

    def a_part(kind, rest):
        n = span(kind, 2)
        for c in range(2):
            low = low_of(kind, c, 2)
            if rest:
                low = low + (1 - 2 * bit_of(p, orders[c][1])) * n
            ref = fin.at[at_rows(kind, low, n), lanes[c]]
            remote(ref, ref, a_s.at[kind, 0], a_r.at[kind, 0], dp=flip(p, orders[c][0])).start()

    groups = bit_groups(nb)

    def s_start(g):
        bits = groups[g]
        for r in range(1, 1 << len(bits)):
            dp_, tensor_ = p, t
            for i, b in enumerate(bits):
                if r >> i & 1:
                    dp_, tensor_ = (flip(dp_, b), tensor_) if b < nb else (dp_, flip(tensor_, b - nb))
            dev = {"dp": dp_} if bits[0] < nb else {"tensor": tensor_}
            remote(ssum.at[g], sgot.at[g, r - 1], s_s.at[g], s_r.at[g, r - 1], **dev).start()

    def s_next(g):
        n = (1 << len(groups[g])) - 1
        for r in range(n):
            wait_for(sgot.at[g, r], s_r.at[g, r])
        v = ssum[g] + sgot[g, 0]
        if n == 3:
            v = v + (sgot[g, 1] + sgot[g, 2])
        ssum[g + 1] = v
        if g + 1 < len(groups):
            s_start(g + 1)

    def local(src, dst_, i):
        return pltpu.make_async_copy(src, dst_, lsem.at[i])

    loads = [
        local(win_hbm, win, 0),
        local(x_hbm, dproj.at[0], 1),
        local(cot_hbm, dproj.at[1], 2),
        local(wout_hbm, w_all.at[t, pl.ds(o_out, ch), :], 3),
        local(wup_hbm, w_all.at[t, pl.ds(o_up, ff), :], 4),
        local(wdown_hbm, w_all.at[t, pl.ds(o_down, ff), :], 5),
        local(conv_hbm, cb.at[0, pl.ds(0, 4), :], 6),
        local(bias_hbm, cb.at[0, pl.ds(4, 1), :], 7),
        local(g1_hbm, g1_ref, 8),
        local(g2_hbm, g2_ref, 9),
    ]
    for i in (0, 1, 6, 7, 8, 9, 2, 3, 4, 5):
        loads[i].start()
    frecv[...] = jnp.zeros_like(frecv)
    brecv[...] = jnp.zeros_like(brecv)
    halo[...] = jnp.zeros_like(halo)
    barrier = pltpu.get_barrier_semaphore()
    for b in range(nb):
        pl.semaphore_signal(barrier, inc=1, device_id={"dp": flip(p, b)}, device_id_type=MESH)
    for j in range(1, blocks):
        pl.semaphore_signal(barrier, inc=1, device_id={"tensor": zflip(j)}, device_id_type=MESH)
    loads[0].wait()

    piece = span(IN, nb)

    def part(c, start):
        w_all[t, at_rows(IN, start, piece), lanes[c]] = win[pl.ds(start, piece), c, :]

    for c in range(2):
        part(c, low_of(IN, c, nb))
    pl.semaphore_wait(barrier, nb + blocks - 1)

    def c_copy(j):
        return remote(cb.at[0], cb.at[j], c_s.at[0], c_r.at[j], tensor=zflip(j))

    hcopy = remote(x_hbm.at[pl.ds(rows - 16, 16), :], halo, h_s.at[0], h_r.at[0], tensor=partner)
    pl.when(t == 2)(hcopy.start)
    def w_send(kind, j):
        for copy in w_sources(kind, j):
            copy.start()

    for j in range(1, blocks):
        w_send(IN, j)
    for i in range(6, 10):
        loads[i].wait()
    for j in range(1, blocks):
        c_copy(j).start()

    def other_part(i, _):
        for c in range(2):
            part(c, lax.rem(low_of(IN, c, nb) + (i + 1) * piece, d))
        return 0

    lax.fori_loop(0, d // piece - 1, other_part, 0)
    loads[1].wait()

    nlane = d // LANES

    def spread(ref):
        for seg in range(SEGS):
            v = ref[pl.ds(seg * steps, steps), :].astype(F32)
            for i in range(nlane):
                perm[i, pl.ds(seg, steps, stride=SEGS), :] = v[:, i * LANES : (i + 1) * LANES]

    def gather(ref):
        for seg in range(SEGS):
            for i in range(nlane):
                v = perm[i, pl.ds(seg, steps, stride=SEGS), :]
                ref[pl.ds(seg * steps, steps), i * LANES : (i + 1) * LANES] = v.astype(ref.dtype)

    def perm_rows(at):
        return jnp.concatenate([perm[i, pl.ds(at, CHUNK), :] for i in range(nlane)], axis=1)

    def put_perm(at, v):
        for i in range(nlane):
            perm[i, pl.ds(at, CHUNK), :] = v[:, i * LANES : (i + 1) * LANES]

    spread(dproj.at[0])
    limit = jnp.where(
        t == 0,
        short_ref[0],
        jnp.where(t == 1, short_ref[1], jnp.where(t == 2, long_ref[0], long_ref[0] - rows)),
    )

    def norm_rows(r, _):
        at = pl.multiple_of(r * CHUNK, CHUNK)
        xv = perm_rows(at)
        xp[pl.ds(at, CHUNK), :] = xv.astype(BF16)
        fv = xv * scale_of(xv) * g1_ref[...]
        lhs[pl.ds(at, CHUNK), :] = fv.astype(BF16)
        first_t[:, pl.ds(at, CHUNK)] = fv.T.astype(BF16)
        return 0

    lax.fori_loop(0, nchunk, norm_rows, 0)
    loads[2].wait()
    spread(dproj.at[1])

    def dout_rows(r, _):
        at = pl.multiple_of(r * CHUNK, CHUNK)
        place = at + lax.broadcasted_iota(jnp.int32, (CHUNK, d), 0)
        pos = lax.rem(place, SEGS) * steps + place // SEGS
        dv = jnp.where(pos < limit, perm_rows(at), 0.0)
        dout[pl.ds(at, CHUNK), :] = dv.astype(BF16)
        dout_t[:, pl.ds(at, CHUNK)] = dv.T.astype(BF16)
        return 0

    lax.fori_loop(0, nchunk, dout_rows, 0)
    w_top(IN, 1)
    seg_id = lax.broadcasted_iota(jnp.int32, (SEGS, ch), 0)
    has_prev = jnp.where(t == 3, 1.0, 0.0).astype(F32)
    has_next = jnp.where(t == 2, 1.0, 0.0).astype(F32)

    def forward_block(j, _):
        s_ = zflip(j)

        @pl.when(j == 1)
        def _():
            w_top(IN, 3)
            loads[4].wait()
            loads[5].wait()
            w_send(FF, 2)
            w_mid(IN, 2)
            w_end(IN, 1)
            w_mid(IN, 3)

        @pl.when(j > 0)
        def _():
            c_copy(j).wait_recv()
            w_wait(IN, j, 0)

        def project(r, _):
            at = pl.multiple_of(r * WIDE, WIDE)
            v = dot(lhs[pl.ds(at, WIDE), :], w_all[s_, pl.ds(o_in, d), :])
            bufa[pl.ds(at, WIDE), :ch] = v[:, :ch]
            cand[j, pl.ds(at + 3 * SEGS, WIDE), :] = v[:, ch:]

            return 0

        lax.fori_loop(0, rows // WIDE, project, 0)

        @pl.when(j == 0)
        def _():
            pl.when(t == 3)(hcopy.wait_recv)
            hv = halo[...].astype(F32)
            edge_rows[...] = (hv * scale_of(hv) * g1_ref[...]).astype(BF16)

        @pl.when(j == 1)
        def _():
            w_end(IN, 2)
            w_send(FF, 3)

        @pl.when(j == 2)
        def _():
            w_end(IN, 3)

        @pl.when(j == 3)
        def _():
            w_top(FF, 2)

        ph = dot(edge_rows[...], w_all[s_, pl.ds(o_in, d), ch:])
        for back in range(3):
            last = cand[j, pl.ds((steps + back) * SEGS, SEGS), :]
            rolled = pltpu.roll(last, 1, 0)
            edge = ph[13 + back : 14 + back, :] * has_prev
            cand[j, pl.ds(back * SEGS, SEGS), :] = jnp.where(seg_id == 0, edge, rolled)
        k_ = [jnp.broadcast_to(cb[j, pl.ds(i, 1), :], (SEGS, ch)) for i in range(4)]
        bias = jnp.broadcast_to(cb[j, pl.ds(4, 1), :], (SEGS, ch))

        def step8(i, carry):
            s, q_ = carry
            for q in range(8):
                at = pl.multiple_of((i * 8 + q) * SEGS, SEGS)
                u = sigmoid(bufa[pl.ds(at, SEGS), :ch] + bias)
                f = k_[0] * cand[j, pl.ds(at + 3 * SEGS, SEGS), :]
                for lag in range(1, 4):
                    f = f + k_[lag] * cand[j, pl.ds(at + (3 - lag) * SEGS, SEGS), :]
                upd[j, pl.ds(at, SEGS), :] = u
                dst[j, pl.ds(at, SEGS), :] = f
                a = 1.0 - u
                s = a * s + u * f
                q_ = a * q_
            return s, q_

        half = lax.fori_loop(
            0, steps // 16, step8, (jnp.zeros((SEGS, ch), F32), jnp.ones((SEGS, ch), F32))
        )

        @pl.when(j == 0)
        def _():
            w_top(IN, 2)
            loads[3].wait()
            for i in (2, 3, 1):
                w_send(OUT, i)

        s, q_ = lax.fori_loop(steps // 16, steps // 8, step8, half)
        ends[0, j] = s
        ends[1, j] = q_
        fsend[j] = jnp.broadcast_to(forward_chain(j, jnp.zeros((1, ch), F32)), (8, ch))
        pl.when(t == 2)(f_copy(j).start)

        @pl.when(j == 0)
        def _():
            w_mid(IN, 1)

        @pl.when(j == 1)
        def _():
            w_top(OUT, 1, 2, 3)
            w_send(FF, 1)

        @pl.when(j == 2)
        def _():
            w_mid(OUT, 1, 2, 3)

        return 0

    def forward_chain(j, start):
        run = start
        for seg in range(SEGS):
            st[j, pl.ds(seg, 1), :] = run
            run = ends[0, j, pl.ds(seg, 1), :] + ends[1, j, pl.ds(seg, 1), :] * run
        return run

    def f_copy(j):
        there = flip(j, 0)
        return remote(fsend.at[j], frecv.at[there], f_s.at[0], f_r.at[there], tensor=partner)

    lax.fori_loop(0, blocks, forward_block, 0)
    w_top(FF, 3)

    def forward_fix(i, _):
        b = flip(i, 0)

        @pl.when(t == 3)
        def _():
            wait_for(frecv.at[b], f_r.at[b])

        forward_chain(b, frecv[b, pl.ds(0, 1), :] * has_prev)

        def step8(i, s):
            for q in range(8):
                at = pl.multiple_of((i * 8 + q) * SEGS, SEGS)
                u = upd[b, pl.ds(at, SEGS), :]
                s = (1.0 - u) * s + u * dst[b, pl.ds(at, SEGS), :]
                st[b, pl.ds(at + SEGS, SEGS), :] = s
            return s

        lax.fori_loop(0, steps // 8, step8, st[b, pl.ds(0, SEGS), :])

        @pl.when(i == 1)
        def _():
            w_end(OUT, 1, 2, 3)

        return 0

    lax.fori_loop(0, blocks, forward_fix, 0)
    w_mid(FF, 2)
    for j in range(1, blocks):
        w_wait(OUT, j, 0)
    shards = [zflip(j) for j in range(blocks)]

    def second_rows(r, _):
        at = pl.multiple_of(r * 512, 512)
        m = xp[pl.ds(at, 512), :].astype(F32)
        for j in range(blocks):
            m = m + dot(
                st[j, pl.ds(at + SEGS, 512), :].astype(BF16), w_all[shards[j], pl.ds(o_out, ch), :]
            )
        mid[pl.ds(at, 512), :] = m
        sv = m * scale_of(m) * g2_ref[...]
        lhs[pl.ds(at, 512), :] = sv.astype(BF16)
        second_t[:, pl.ds(at, 512)] = sv.T.astype(BF16)
        bufa[pl.ds(at, 512), :] = m
        bufc[pl.ds(at, 512), :] = jnp.zeros((512, d), F32)
        return 0

    lax.fori_loop(0, rows // 512, second_rows, 0)

    w_mid(FF, 3)
    act, din = dproj.at[1], dproj.at[2]

    def ff_place(i):
        return lax.div(i + 3, 4) * (1 + lax.rem(i, 3))

    def ff_block(i, _):
        j, before, earlier = ff_place(i), ff_place(i - 1), ff_place(i - 2)
        s_ = zflip(j)

        @pl.when(i > 0)
        def _():
            w_wait(FF, j, 0)

        def ff_rows(r, _):
            at = pl.multiple_of(r * 512, 512)
            wu = w_all[s_, pl.ds(o_up, ff), :]
            wd = w_all[s_, pl.ds(o_down, ff), :]
            inner = dot(lhs[pl.ds(at, 512), :], wu)
            da = dot_t(dout[pl.ds(at, 512), :], wd)
            cdf = 0.5 + 0.5 * lax.erf(inner * np.float32(np.sqrt(0.5)))
            pdf = jnp.exp(inner * inner * -0.5) * np.float32(1.0 / np.sqrt(2.0 * np.pi))
            av = (inner * cdf).astype(BF16)
            dv = (da * (cdf + inner * pdf)).astype(BF16)
            act[pl.ds(at, 512), :] = av
            din[pl.ds(at, 512), :] = dv
            bufa[pl.ds(at, 512), :] += dot(av, wd)
            bufc[pl.ds(at, 512), :] += dot_t(dv, wu)

            @pl.when((r == 0) & (i == 0))
            def _():
                w_end(FF, 2)

            @pl.when((r == 1) & (i == 0))
            def _():
                w_top(FF, 1)

            @pl.when((r == 0) & (i == 1))
            def _():
                w_end(FF, 3)

            @pl.when((r == 0) & (i == 1))
            def _():
                w_mid(FF, 1)

            @pl.when((r == 0) & (i == 2))
            def _():
                w_end(FF, 1)

            @pl.when((r == 1) & (i > 0))
            def _():
                r_first(FF, before)

            return 0

        lax.fori_loop(0, rows // 512, ff_rows, 0)

        def ff_grads(r, _):
            at = pl.multiple_of(r * 512, 512)
            grad[s_, pl.ds(o_up + at, 512), :] = dot(second_t[pl.ds(at, 512), :], din[...]).astype(BF16)
            grad[s_, pl.ds(o_down + at, 512), :] = dot(dout_t[pl.ds(at, 512), :], act[...]).astype(BF16)
            return 0

        lax.fori_loop(0, d // 512, ff_grads, 0)
        @pl.when(i > 1)
        def _():
            r_middle(FF, earlier)

        r_start(FF, j, 0)
        return 0

    lax.fori_loop(0, blocks, ff_block, 0)

    def second_back(r, gain):
        at = pl.multiple_of(r * CHUNK, CHUNK)
        m = mid[pl.ds(at, CHUNK), :]
        s = scale_of(m)
        dn = bufc[pl.ds(at, CHUNK), :]
        gain = gain + jnp.sum(dn * m * s, axis=0, keepdims=True)
        gd = dn * g2_ref[...]
        dm = dout[pl.ds(at, CHUNK), :].astype(F32) + s * gd - m * (s * s * s * jnp.mean(gd * m, axis=-1, keepdims=True))
        mid[pl.ds(at, CHUNK), :] = dm
        lhs[pl.ds(at, CHUNK), :] = dm.astype(BF16)
        second_t[:, pl.ds(at, CHUNK)] = dm.T.astype(BF16)
        bufc[pl.ds(at, CHUNK), :] = jnp.zeros((CHUNK, d), F32)
        return gain

    gain2 = lax.fori_loop(0, nchunk, second_back, jnp.zeros((1, d), F32))
    ssum[0] = jnp.zeros((16, d), F32)
    ssum[0, pl.ds(1, 1), :] = gain2
    r_first(FF, 1)

    def backward_block(i, _):
        j = blocks - 1 - i
        s_ = zflip(j)

        def project(r, _):
            at = pl.multiple_of(r * 512, 512)
            dst[j, pl.ds(at, 512), :] = dot_t(lhs[pl.ds(at, 512), :], w_all[s_, pl.ds(o_out, ch), :])
            return 0

        lax.fori_loop(0, rows // 512, project, 0)
        state = st[j, pl.ds(SEGS, rows), :].astype(BF16)
        for half in range(2):
            rr = d // 2
            grad[s_, pl.ds(o_out, ch), half * ch : (half + 1) * ch] = dot(
                second_t[half * rr : (half + 1) * rr, :], state
            ).astype(BF16)
        r_start(OUT, j, 0)

        @pl.when(i == 0)
        def _():
            r_last(FF, 2)
            r_middle(FF, 3)

        @pl.when(i == 1)
        def _():
            r_last(FF, 0)

        @pl.when(i == 2)
        def _():
            r_middle(FF, 1)

        @pl.when(i == 3)
        def _():
            r_last(FF, 3)
            r_middle(OUT, 3)

        def one(step, w, q_):
            at = pl.multiple_of(step * SEGS, SEGS)
            a = 1.0 - upd[j, pl.ds(at, SEGS), :]
            c = dst[j, pl.ds(at, SEGS), :] + w
            return c, a * c, q_ * a

        w, q_ = jnp.zeros((SEGS, ch), F32), jnp.ones((SEGS, ch), F32)
        for step in range(steps - 1, steps - 6, -1):
            _, w, q_ = one(step, w, q_)

        def step8(n, carry):
            w, q_ = carry
            for q in range(8):
                _, w, q_ = one(steps - 6 - (n * 8 + q), w, q_)
            return w, q_

        w, q_ = lax.fori_loop(0, (steps - 8) // 8, step8, (w, q_))
        for step in range(2, -1, -1):
            bends[2 * step, j] = q_
            c, w, q_ = one(step, w, q_)
            bends[2 * step + 1, j] = c
        bends[6, j] = w
        bends[7, j] = q_
        bsend[j, pl.ds(0, 1), :] = backward_chain(j, jnp.zeros((1, ch), F32))
        for step in range(3):
            bsend[j, pl.ds(step + 1, 1), :] = upd[j, pl.ds(step * SEGS, 1), :] * (
                bends[2 * step + 1, j, pl.ds(0, 1), :]
                + bends[2 * step, j, pl.ds(0, 1), :] * ends[0, j, pl.ds(0, 1), :]
            )
        pl.when(t == 3)(b_copy(j).start)

        @pl.when(i > 0)
        def _():
            r_first(OUT, j + 1)

        return 0

    def backward_chain(j, start):
        run = start
        for seg in range(SEGS - 1, -1, -1):
            ends[0, j, pl.ds(seg, 1), :] = run
            run = bends[6, j, pl.ds(seg, 1), :] + bends[7, j, pl.ds(seg, 1), :] * run
        return run

    def b_copy(j):
        there = flip(j, 0)
        return remote(bsend.at[j], brecv.at[there], b_s.at[0], b_r.at[there], tensor=partner)

    lax.fori_loop(0, blocks, backward_block, 0)


    def backward_fix(i, _):
        j = blocks - 1 - i
        s_ = zflip(j)

        @pl.when(t == 2)
        def _():
            wait_for(brecv.at[j], b_r.at[j])

        backward_chain(j, brecv[j, pl.ds(0, 1), :] * has_next)
        w = ends[0, j]
        after = []
        for step in range(3):
            df = upd[j, pl.ds(step * SEGS, SEGS), :] * (bends[2 * step + 1, j] + bends[2 * step, j] * w)
            edge = brecv[j, pl.ds(step + 1, 1), :] * has_next
            after.append(jnp.where(seg_id == SEGS - 1, edge, pltpu.roll(df, SEGS - 1, 0)))
        k_ = [jnp.broadcast_to(cb[j, pl.ds(n, 1), :], (SEGS, ch)) for n in range(4)]
        zero = jnp.zeros((SEGS, ch), F32)

        def pair(n, carry):
            w, d1, d2, d3, c0, c1, c2, k0, k1, k2, k3, gb = carry
            top = steps - 2 - 2 * n
            made = []
            for q in range(2):
                at = pl.multiple_of((top + 1 - q) * SEGS, SEGS)
                u = upd[j, pl.ds(at, SEGS), :]
                c = dst[j, pl.ds(at, SEGS), :] + w
                d0 = c * u
                a = 1.0 - u
                w = a * c
                c3 = cand[j, pl.ds(at, SEGS), :]
                f = k_[0] * c0 + k_[1] * c1 + k_[2] * c2 + k_[3] * c3
                dg = d0 * a * (f - st[j, pl.ds(at, SEGS), :])
                dc = k_[0] * d0 + k_[1] * d1 + k_[2] * d2 + k_[3] * d3
                k0, k1, k2, k3 = k0 + d0 * c0, k1 + d0 * c1, k2 + d0 * c2, k3 + d0 * c3
                gb = gb + dg
                c0, c1, c2 = c1, c2, c3
                d1, d2, d3 = d0, d1, d2
                made.append((dg, dc))
            at = pl.multiple_of(top * SEGS, 2 * SEGS)
            dproj[j, pl.ds(at, 2 * SEGS), :ch] = jnp.concatenate([made[1][0], made[0][0]], axis=0).astype(BF16)
            dproj[j, pl.ds(at, 2 * SEGS), ch:] = jnp.concatenate([made[1][1], made[0][1]], axis=0).astype(BF16)
            return w, d1, d2, d3, c0, c1, c2, k0, k1, k2, k3, gb

        window = [cand[j, pl.ds((steps + 2 - n) * SEGS, SEGS), :] for n in range(3)]
        def quad(n, carry):
            return pair(2 * n + 1, pair(2 * n, carry))

        half = lax.fori_loop(0, steps // 8, quad, (w, *after, *window, zero, zero, zero, zero, zero))

        @pl.when(i == 0)
        def _():
            r_last(FF, 1)
            r_first(OUT, 0)
            r_middle(OUT, 2)

        @pl.when(i == 1)
        def _():
            r_last(OUT, 2)
            r_middle(OUT, 0)

        @pl.when(i == 2)
        def _():
            r_last(OUT, 0)

        @pl.when(i == 3)
        def _():
            r_middle(IN, 3)
            a_first(OUT)

        out = lax.fori_loop(steps // 8, steps // 4, quad, half)
        for n in range(5):
            at = 2 + 2 * n + bit_of(s_, 1)
            ssum[0, pl.ds(at, 1), pl.ds(pl.multiple_of(bit_of(s_, 0) * ch, LANES), ch)] = jnp.sum(
                out[7 + n], axis=0, keepdims=True
            )

        @pl.when(i > 1)
        def _():
            r_first(IN, j + 1)

        def first_grad(r, _):
            at = pl.multiple_of(r * 512, 512)
            grad[s_, pl.ds(o_in + at, 512), :] = dot(first_t[pl.ds(at, 512), :], dproj[j]).astype(BF16)
            return 0

        lax.fori_loop(0, d // 512, first_grad, 0)
        r_start(IN, j, 0)


        @pl.when(i == 0)
        def _():
            r_last(OUT, 3)
            r_middle(OUT, 1)

        @pl.when(i == 1)
        def _():
            r_first(IN, 3)
            r_last(OUT, 1)

        @pl.when(i == 2)
        def _():
            a_first(FF)

        @pl.when(i == 3)
        def _():
            r_middle(IN, 2)

        return 0

    lax.fori_loop(0, blocks, backward_fix, 0)

    def first_back(r):
        at = r * 512
        v = dot_t(dproj[0, pl.ds(at, 512), :], w_all[shards[0], pl.ds(o_in, d), :])
        for j in range(1, blocks):
            v = v + dot_t(dproj[j, pl.ds(at, 512), :], w_all[shards[j], pl.ds(o_in, d), :])
        bufc[pl.ds(at, 512), :] = v

    first_back(0)
    r_last(IN, 3)
    r_first(IN, 0)
    for r in range(1, rows // 512):
        first_back(r)
    r_middle(IN, 1)
    a_mid(FF)
    r_last(IN, 2)

    def first_norm_back(r, gain):
        at = pl.multiple_of(r * CHUNK, CHUNK)
        m = xp[pl.ds(at, CHUNK), :].astype(F32)
        s = scale_of(m)
        dn = bufc[pl.ds(at, CHUNK), :]
        gain = gain + jnp.sum(dn * m * s, axis=0, keepdims=True)
        gd = dn * g1_ref[...]
        dv = s * gd - m * (s * s * s * jnp.mean(gd * m, axis=-1, keepdims=True))
        put_perm(at, mid[pl.ds(at, CHUNK), :] + dv)
        return gain

    ssum[0, pl.ds(0, 1), :] = lax.fori_loop(0, nchunk, first_norm_back, jnp.zeros((1, d), F32))
    s_start(0)
    r_middle(IN, 0)
    r_last(IN, 1)
    s_next(0)
    gather(mid)
    r_last(IN, 0)
    a_first(IN)
    a_mid(OUT)
    a_end(FF)
    for r in range(nchunk):
        put_perm(r * CHUNK, bufa[pl.ds(r * CHUNK, CHUNK), :])
    gather(res)
    for g in range(1, len(groups) - 1):
        s_next(g)
    a_mid(IN)
    a_part(IN, False)
    a_end(OUT)
    a_wait(IN, 1)
    a_part(IN, True)
    s_next(len(groups) - 1)
    gains_ref[...] = ssum[len(groups), pl.ds(0, 8), :]
    for n in range(5):
        at = 2 + 2 * n + bit_of(t, 1)
        chan_ref[pl.ds(n, 1), :] = ssum[
            len(groups), pl.ds(at, 1), pl.ds(pl.multiple_of(bit_of(t, 0) * ch, LANES), ch)
        ]
    a_wait(FF, 0)
    a_wait(OUT, 0)
    a_wait(IN, 0)

    pl.when(t == 2)(hcopy.wait_send)
    wait_for(cb.at[pl.ds(0, blocks - 1)], c_s.at[0])
    pl.when(t == 2)(lambda: wait_for(fsend, f_s.at[0]))
    pl.when(t == 3)(lambda: wait_for(bsend, b_s.at[0]))
    for kind in (IN, OUT, FF):
        for k in range(halves[kind]):
            n = span(kind, k + 1)
            wait_for(w_all.at[0, pl.ds(0, (blocks - 1) * n), :], w_s.at[kind, k])
            wait_for(grad.at[pl.ds(0, 2), pl.ds(0, blocks // 2 * n), :], r_s.at[kind, k])
            wait_for(fin.at[pl.ds(0, n), :], a_s.at[kind, k])
        n = span(kind, nb)
        wait_for(w_all.at[0, pl.ds(0, (blocks - 1) * n), :], w_s.at[kind, nb])
        wait_for(w_all.at[0, pl.ds(0, (blocks - 1) * n), :], r_s.at[kind, nb])
    for g in range(len(groups)):
        wait_for(sgot.at[g, pl.ds(0, (1 << len(groups[g])) - 1)], s_s.at[g])


def finish_kernel(
    dims, gains, chan, res, gx, fin, res_out, gx_out, gin_o, gout_o, gup_o, gdown_o, gnorm, gmlp, taps, gbias,
    gin, gout, gup, gdown, sem,
):
    rows, d, ch, ff = dims
    outs = []

    def put(src, dst):
        copy = pltpu.make_async_copy(src, dst, sem.at[len(outs)])
        copy.start()
        outs.append(copy)

    put(gx, gx_out)
    put(res, res_out)
    gup[...] = fin[pl.ds(d + ch, d), :].astype(F32)
    put(gup, gup_o)
    gin[:, 0, :] = fin[pl.ds(0, d), :ch].astype(F32)
    gin[:, 1, :] = fin[pl.ds(0, d), ch:].astype(F32)
    put(gin, gin_o)
    gdown[...] = fin[pl.ds(d + ch + ff, d), :].astype(F32).T
    put(gdown, gdown_o)
    gout[:, : d // 2] = fin[pl.ds(d, ch), :ch].astype(F32).T
    gout[:, d // 2 :] = fin[pl.ds(d, ch), ch:].astype(F32).T
    put(gout, gout_o)
    gnorm[...] = gains[pl.ds(0, 1), :]
    gmlp[...] = gains[pl.ds(1, 1), :]
    taps[...] = chan[pl.ds(0, 4), :]
    gbias[...] = chan[pl.ds(4, 1), :]
    for copy in outs:
        copy.wait()


def per_device(
    inputs,
    norm_gain,
    in_weight,
    conv_kernel,
    gate_bias,
    out_weight,
    mlp_gain,
    up_weight,
    down_weight,
    short_lengths,
    long_lengths,
    cotangent,
):
    rows, d = inputs.shape
    ch = in_weight.shape[2]
    ff = up_weight.shape[1]
    blocks = lax.axis_size("tensor")
    dp = lax.axis_size("dp")
    nb = log2(dp)
    assert dp == 1 << nb and blocks == 4 and rows == LSHORT and 2 * rows == LLONG
    assert 2 * ch == d and short_lengths.shape == (2,) and long_lengths.shape == (1,)
    sizes = (d, ch, 2 * ff)
    total = sum(sizes)
    halves = tuple(min(nb, log2(r // TILE)) for r in sizes)

    def span_all(k):
        return sum(r >> min(k, h) for r, h in zip(sizes, halves))

    ngroups = len(bit_groups(nb))
    vm = pl.BlockSpec(memory_space=pltpu.VMEM)
    sm = pl.BlockSpec(memory_space=pltpu.SMEM)
    hb = pl.BlockSpec(memory_space=pl.ANY)
    dma = pltpu.SemaphoreType.DMA
    res, gx, fin, gains, chan = pl.pallas_call(
        functools.partial(block_kernel, (rows, d, blocks, ch, ff, nb)),
        out_shape=(
            pltpu.VMEM((rows, d), BF16),
            pltpu.VMEM((rows, d), F32),
            pltpu.VMEM((total, d), BF16),
            pltpu.VMEM((8, d), F32),
            pltpu.VMEM((8, ch), F32),
        ),
        in_specs=[sm, sm] + [hb] * 10,
        out_specs=(vm,) * 5,
        scratch_shapes=[
            pltpu.VMEM((1, d), F32),
            pltpu.VMEM((1, d), F32),
            pltpu.VMEM((blocks, total, d), BF16),
            pltpu.VMEM((blocks, total, d), BF16),
            pltpu.VMEM((d, 2, ch), BF16),
            pltpu.VMEM((rows, d), BF16),
            pltpu.VMEM((blocks, rows + 3 * SEGS, ch), F32),
            pltpu.VMEM((blocks, rows, ch), F32),
            pltpu.VMEM((blocks, rows + SEGS, ch), F32),
            pltpu.VMEM((blocks, rows, ch), F32),
            pltpu.VMEM((16, d), BF16),
            pltpu.VMEM((d, rows), BF16),
            pltpu.VMEM((d, rows), BF16),
            pltpu.VMEM((rows, d), BF16),
            pltpu.VMEM((d, rows), BF16),
            pltpu.VMEM((rows, d), F32),
            pltpu.VMEM((rows, d), F32),
            pltpu.VMEM((blocks, rows, d), BF16),
            pltpu.VMEM((d // LANES, rows, LANES), F32),
            pltpu.VMEM((16, d), BF16),
            pltpu.VMEM((blocks, 8, ch), F32),
            pltpu.VMEM((2, blocks, SEGS, ch), F32),
            pltpu.VMEM((8, blocks, SEGS, ch), F32),
            pltpu.VMEM((blocks, 8, ch), F32),
            pltpu.VMEM((blocks, 8, ch), F32),
            pltpu.VMEM((blocks, 8, ch), F32),
            pltpu.VMEM((blocks, 8, ch), F32),
            pltpu.VMEM((blocks, span_all(nb), d), BF16),
            pltpu.VMEM((ngroups + 1, 16, d), F32),
            pltpu.VMEM((ngroups, 3, 16, d), F32),
            dma((10,)),
            dma((1,)),
            dma((blocks,)),
            dma((1,)),
            dma((blocks,)),
            dma((1,)),
            dma((blocks,)),
            dma((1,)),
            dma((1,)),
            dma((3, nb + 1)),
            dma((3, blocks, nb + 1)),
            dma((3, nb + 1)),
            dma((3, blocks, nb + 1)),
            dma((3, blocks, nb)),
            dma((3, nb)),
            dma((3, nb)),
            dma((ngroups,)),
            dma((ngroups, 3)),
        ]
        + [pltpu.VMEM((blocks, span_all(k + 1), d), BF16) for k in range(nb)],
        compiler_params=pltpu.CompilerParams(
            collective_id=0, has_side_effects=True, vmem_limit_bytes=59 << 20
        ),
        name="block",
    )(
        short_lengths,
        long_lengths,
        inputs,
        cotangent,
        norm_gain[None],
        mlp_gain[None],
        conv_kernel,
        gate_bias[None],
        in_weight,
        out_weight,
        up_weight,
        down_weight,
    )
    result, grad_inputs, gin, gout, gup, gdown, gnorm, gmlp, taps, gbias = pl.pallas_call(
        functools.partial(finish_kernel, (rows, d, ch, ff)),
        out_shape=(
            jax.ShapeDtypeStruct((rows, d), BF16),
            jax.ShapeDtypeStruct((rows, d), F32),
            jax.ShapeDtypeStruct((d, 2, ch), F32),
            jax.ShapeDtypeStruct((ch, d), F32),
            jax.ShapeDtypeStruct((d, ff), F32),
            jax.ShapeDtypeStruct((ff, d), F32),
            jax.ShapeDtypeStruct((1, d), F32),
            jax.ShapeDtypeStruct((1, d), F32),
            jax.ShapeDtypeStruct((4, ch), F32),
            jax.ShapeDtypeStruct((1, ch), F32),
        ),
        in_specs=[vm] * 5,
        out_specs=(hb,) * 6 + (vm,) * 4,
        scratch_shapes=[
            pltpu.VMEM((d, 2, ch), F32),
            pltpu.VMEM((ch, d), F32),
            pltpu.VMEM((d, ff), F32),
            pltpu.VMEM((ff, d), F32),
            dma((6,)),
        ],
        compiler_params=pltpu.CompilerParams(vmem_limit_bytes=32 << 20),
        name="finish",
    )(gains, chan, res, gx, fin)
    return (result, grad_inputs, gnorm[0], gin, taps, gbias[0], gout, gmlp[0], gup, gdown)


def solution(mesh):
    placed = (
        P(("dp", "tensor"), None),
        P(),
        P(None, None, "tensor"),
        P(None, "tensor"),
        P("tensor"),
        P("tensor", None),
        P(),
        P(None, "tensor"),
        P("tensor", None),
        P("dp"),
        P("dp"),
        P(("dp", "tensor"), None),
    )
    return jax.shard_map(
        per_device,
        mesh=mesh,
        in_specs=placed,
        out_specs=(
            P(("dp", "tensor"), None),
            P(("dp", "tensor"), None),
            P(),
            P(None, None, "tensor"),
            P(None, "tensor"),
            P("tensor"),
            P("tensor", None),
            P(),
            P(None, "tensor"),
            P("tensor", None),
        ),
        check_vma=False,
    )
```
